256 devices in a mesh: grp: 4 (over z_hi), gx: 16 (over z_lo, y, core), gy: 4 (over x).
Axes of the slice: x: 4, y: 4, z: 8 (z_hi: 4, z_lo: 2; z = z_hi * 2 + z_lo), core: 2. Of those that a mesh axis runs over, the one named last changes fastest.
Arguments:
- states: bfloat16 [12, 256, 64, 512], P(None, 'gx', 'gy', 'grp'), may hold values from 0 to 1
- membrane: float32 [256, 64, 512], P('gx', 'gy', 'grp'), may hold values from -3 to 3
- phi_heart: float32 [256, 64, 512], P('gx', 'gy', 'grp'), may hold values from -3 to 3
- ion_params: float32 [5, 12], replicated, may hold values from -1.5 to 20, as said below
- torso_phi: float32 [256, 128, 512], P('gx', 'gy', 'grp'), may hold values from -3 to 3
- tissue_scale: float32 [256, 128, 512], P('gx', 'gy', 'grp'), may hold values from 0.5 to 2
- labels: int32 [256, 128, 512], P('gx', 'gy', 'grp'), may hold values from 0 to 3
- cond_table: float32 [4], replicated, may hold values from 0.1 to 2
- send_node: int32 [4, 16, 4, 64, 512], P('grp', 'gx', 'gy'), may hold values from 0 to 8191
- send_count: int32 [4, 16, 4, 64], P('grp', 'gx', 'gy'), may hold values from 64 to 512, as said below
- recv_voxel: int32 [4, 16, 4, 64, 512], P('grp', 'gx', 'gy'), may hold values from 0 to 16383
- recv_count: int32 [4, 16, 4, 64], P('grp', 'gx', 'gy'), may hold values from 64 to 512, as said below
Outputs:
- new_membrane: float32 [256, 64, 512], P('gx', 'gy', 'grp')
- heart_phi: float32 [256, 64, 512], P('gx', 'gy', 'grp')
- torso_out: float32 [256, 128, 512], P('gx', 'gy', 'grp')
The draws below stay inside these ranges and needn't reach their ends.
Inputs may be any that keep to these rules, and one draw needn't show every extreme that they name: `ion_params`: rows are midpoints in -1 to 1, slopes in 0.1 to 0.5, relaxation rates in 0.5 to 20, conductances in 0.1 to 0.6 and reversal potentials in -1.5 to 1.5, one column per state. send_count[g, i, j, p] is the number of live slots, from the first on, of the patch that device (g, i, j) sends to peer p of its slab; every device sends exactly 512 to one peer. recv_count[g, i, j, s] equals send_count of peer s of slab g for peer i * 4 + j; every device receives exactly 512 from one peer.
All inputs are finite; a program needn't handle non-finite values.
Results may differ from the reference program's by a relative error of at most 0.0003.
Values sent between devices are 32-bit elements; how exact they have to be, the bound alone decides.
No kernel may reach another device: no remote copies, remote signals or barrier semaphores. Data moves between devices by JAX's collectives and lax.ppermute only.
A program may use at most 128 MiB of HBM per device.

```python
import math
import jax
import jax.numpy as jnp

STATES = 12
LABELS = 4
SWEEPS_H = 3
SWEEPS_T = 4
CAP = 512
HX = 16
HY = 16
HZ = 128
TX = 16
TY = 32
TZ = 128
PEERS = 64
HNODES = 32768
TVOX = 65536
NHX = 256
NHY = 64
NHZ = 512
NTX = 256
NTY = 128
NTZ = 512
N_GRP = 4
N_GX = 16
N_GY = 4


def one_perm(subkey):
    return jax.random.permutation(subkey, PEERS).astype(jnp.int32)


def pair_counts(key):
    base_key = jax.random.fold_in(key, 7)
    key_hi, key_base, key_perm = jax.random.split(base_key, 3)
    ceiling = jax.random.randint(key_hi, (N_GRP, 1, PEERS), CAP // 4, CAP + 1)
    counts = jax.random.randint(key_base, (N_GRP, PEERS, PEERS), ceiling // 2, ceiling + 1)
    chosen = jax.vmap(one_perm)(jax.random.split(key_perm, N_GRP))
    full_pair = jnp.arange(PEERS, dtype=jnp.int32)[None, None, :] == chosen[:, :, None]
    return jnp.where(full_pair, CAP, counts).astype(jnp.int32)


def draw_send_count(key, part):
    return pair_counts(key).reshape(N_GRP, N_GX, N_GY, PEERS)


def draw_recv_count(key, part):
    return pair_counts(key).transpose(0, 2, 1).reshape(N_GRP, N_GX, N_GY, PEERS)


def draw_ion_params(key, part):
    subkeys = jax.random.split(jax.random.fold_in(key, 11), 5)
    midpoint = jax.random.uniform(subkeys[0], (STATES,), jnp.float32, -1.0, 1.0)
    steepness = jax.random.uniform(subkeys[1], (STATES,), jnp.float32, 0.1, 0.5)
    relax_rate = jnp.exp(jax.random.uniform(subkeys[2], (STATES,), jnp.float32, jnp.log(0.5), jnp.log(20.0)))
    conductance = jax.random.uniform(subkeys[3], (STATES,), jnp.float32, 0.1, 0.6)
    reversal = jax.random.uniform(subkeys[4], (STATES,), jnp.float32, -1.5, 1.5)
    return jnp.stack([midpoint, steepness, relax_rate, conductance, reversal]).astype(jnp.float32)


def plant(result, own_key, smallest, high):
    longest = result.shape.index(max(result.shape))
    spots = []
    for shift in (0, 1):
        where = [jax.random.randint(jax.random.fold_in(own_key, axis), (), 0, length) for axis, length in enumerate(result.shape)]
        where[longest] = (where[longest] + shift) % result.shape[longest]
        spots.append(tuple(where))
    return result.at[spots[0]].set(smallest).at[spots[1]].set(high)


def levels(own_key, dims, pieces, smallest, top_value):
    factor_of = 1.0
    for position, shards_of in pieces:
        draws = jax.random.uniform(jax.random.fold_in(jax.random.fold_in(own_key, 6), position), (shards_of,), jnp.float32, smallest / len(pieces), top_value / len(pieces))
        factor_of = factor_of * jnp.repeat(jnp.exp(draws), dims[position] // shards_of).reshape((-1,) + (1,) * (len(dims) - 1 - position))
    return factor_of


def bell_draw(own_key, shape, scale, reach, pieces=(), kind=jnp.bfloat16):
    factor_of = levels(own_key, shape, pieces, -0.22, 0.18) if pieces else 1.0
    drawn = jax.random.normal(own_key, shape, jnp.float32) * scale * factor_of
    return jnp.minimum(jnp.maximum(drawn, -reach), reach).astype(kind)


def setup_inputs(seed: int = 0) -> dict:
    keys = jax.random.split(jax.random.key(seed), 13)
    return {
        "states": jnp.clip(1.0 * jax.random.uniform(keys[0], (STATES, NHX, NHY, NHZ), jnp.float32) ** levels(keys[0], (STATES, NHX, NHY, NHZ), ((1, 16), (2, 4), (3, 4)), -0.2, 0.2), 0.0, 1.0).astype(jnp.bfloat16),
        "membrane": bell_draw(keys[1], (NHX, NHY, NHZ), 0.5, 3.0, ((0, 16), (1, 4), (2, 4)), jnp.float32),
        "phi_heart": bell_draw(keys[2], (NHX, NHY, NHZ), 0.5, 3.0, ((0, 16), (1, 4), (2, 4)), jnp.float32),
        "ion_params": draw_ion_params(jax.random.fold_in(keys[12], 71), 0),
        "torso_phi": bell_draw(keys[4], (NTX, NTY, NTZ), 0.5, 3.0, ((0, 16), (1, 4), (2, 4)), jnp.float32),
        "tissue_scale": jnp.clip(jnp.exp(math.log(2.0) - 1.3862944 * jax.random.uniform(keys[5], (NTX, NTY, NTZ), jnp.float32) ** levels(keys[5], (NTX, NTY, NTZ), ((0, 16), (1, 4), (2, 4)), -0.2, 0.2)), 0.5, 2.0),
        "labels": plant(jax.random.randint(keys[6], (NTX, NTY, NTZ), 0, LABELS), jax.random.fold_in(keys[6], 1), 0, LABELS - 1).astype(jnp.int32),
        "cond_table": jnp.clip(jnp.exp(jax.random.uniform(keys[7], (LABELS,), jnp.float32, math.log(0.1), math.log(2.0))), 0.1, 2.0),
        "send_node": plant(jax.random.randint(keys[8], (N_GRP, N_GX, N_GY, PEERS, CAP), 0, HNODES // 4), jax.random.fold_in(keys[8], 1), 0, (HNODES // 4) - 1).astype(jnp.int32),
        "send_count": draw_send_count(jax.random.fold_in(keys[12], 71), 0),
        "recv_voxel": plant(jax.random.randint(keys[10], (N_GRP, N_GX, N_GY, PEERS, CAP), 0, TVOX // 4), jax.random.fold_in(keys[10], 1), 0, (TVOX // 4) - 1).astype(jnp.int32),
        "recv_count": draw_recv_count(jax.random.fold_in(keys[12], 71), 0),
    }


time_step = 0.1
intra_cond = 0.25
extra_cond = 0.5
penalty = 2.0
cheb_low = 0.1
cheb_high = 2.0


def cheb_coeffs(sweeps):
    centre = 0.5 * (cheb_high + cheb_low)
    half_width = 0.5 * (cheb_high - cheb_low)
    scaled = centre / half_width
    coeffs = [(0.0, 1.0 / centre)]
    rho_old = 1.0 / scaled
    for number in range(1, sweeps):
        rho_new = 1.0 / (2.0 * scaled - rho_old)
        coeffs.append((rho_new * rho_old, 2.0 * rho_new / half_width))
        rho_old = rho_new
    return coeffs


def face_mask(cell_count, margin, start_at, whole):
    positions = start_at + jnp.arange(cell_count + 2 * margin, dtype=jnp.int32) - margin
    return ((positions >= 0) & (positions + 1 <= whole - 1)).astype(jnp.float32)


def harmonic(lower_cell, upper_cell):
    return 2.0 * lower_cell * upper_cell / (lower_cell + upper_cell)


def faces_from(conduct, mask_x, mask_y, mask_z):
    face_x = jnp.concatenate([harmonic(conduct[:-1], conduct[1:]), jnp.zeros_like(conduct[:1])], 0) * mask_x[:, None, None]
    face_y = jnp.concatenate([harmonic(conduct[:, :-1], conduct[:, 1:]), jnp.zeros_like(conduct[:, :1])], 1) * mask_y[None, :, None]
    face_z = jnp.concatenate([harmonic(conduct[:, :, :-1], conduct[:, :, 1:]), jnp.zeros_like(conduct[:, :, :1])], 2) * mask_z[None, None, :]
    return face_x, face_y, face_z


def flux_sum(values, conductances):
    face_x, face_y, face_z = conductances
    along_x = face_x[:-1] * (values[1:] - values[:-1])
    along_y = face_y[:, :-1] * (values[:, 1:] - values[:, :-1])
    along_z = face_z[:, :, :-1] * (values[:, :, 1:] - values[:, :, :-1])
    summed = (along_x[:-1] - along_x[1:])[:, 1:-1, 1:-1]
    summed = summed + (along_y[:, :-1] - along_y[:, 1:])[1:-1, :, 1:-1]
    return summed + (along_z[:, :, :-1] - along_z[:, :, 1:])[1:-1, 1:-1, :]


def face_total(conductances):
    face_x, face_y, face_z = conductances
    summed = (face_x[:-2] + face_x[1:-1])[:, 1:-1, 1:-1]
    summed = summed + (face_y[:, :-2] + face_y[:, 1:-1])[1:-1, :, 1:-1]
    return summed + (face_z[:, :, :-2] + face_z[:, :, 1:-1])[1:-1, 1:-1, :]


def lookup(labels, cond_table):
    picked = jnp.zeros(labels.shape, jnp.float32)
    for number in range(LABELS):
        picked = picked + jnp.where(labels == number, cond_table[number], jnp.zeros((), jnp.float32))
    return picked


def ionic_current(states, membrane, ion_params):
    params_col = ion_params[:, :, None, None, None]
    gate_vals = states.astype(jnp.float32)
    voltage = membrane[None]
    steady = jax.nn.sigmoid((voltage - params_col[0]) / params_col[1])
    gate_vals = steady + (gate_vals - steady) * jnp.exp(-time_step * params_col[2])
    return jnp.sum(params_col[3] * gate_vals * (voltage - params_col[4]), axis=0)


def padded(values):
    return jnp.pad(values, 1, mode="wrap")


def global_faces(conduct_ext, grid_shape):
    mask_x = jnp.ones((grid_shape[0] + 2,), jnp.float32)
    mask_y = face_mask(grid_shape[1], 1, 0, grid_shape[1])
    mask_z = face_mask(grid_shape[2], 1, 0, grid_shape[2])
    return faces_from(conduct_ext, mask_x, mask_y, mask_z)


def to_blocks(values, size_x, size_y, size_z):
    blocks = values.reshape(N_GX, size_x, N_GY, size_y, N_GRP, size_z).transpose(4, 0, 2, 1, 3, 5)
    return blocks.reshape(N_GRP, N_GX * N_GY, size_x * size_y * size_z)


def from_blocks(blocks, size_x, size_y, size_z):
    values = blocks.reshape(N_GRP, N_GX, N_GY, size_x, size_y, size_z).transpose(1, 3, 2, 4, 0, 5)
    return values.reshape(N_GX * size_x, N_GY * size_y, N_GRP * size_z)


def reference(states, membrane, phi_heart, ion_params, torso_phi, tissue_scale, labels, cond_table, send_node, send_count, recv_voxel, recv_count):
    heart_shape = membrane.shape
    torso_shape = torso_phi.shape
    unit_faces = global_faces(jnp.ones((heart_shape[0] + 2, heart_shape[1] + 2, heart_shape[2] + 2), jnp.float32), heart_shape)
    heart_total = (intra_cond + extra_cond) * face_total(unit_faces)
    lap_membrane = flux_sum(padded(membrane), unit_faces)
    source = -intra_cond * lap_membrane
    iterate = phi_heart
    update = jnp.zeros_like(iterate)
    for carry_coef, resid_coef in cheb_coeffs(SWEEPS_H):
        residue = (source - (intra_cond + extra_cond) * flux_sum(padded(iterate), unit_faces)) / heart_total
        update = carry_coef * update + resid_coef * residue
        iterate = iterate + update
    phi_new = iterate
    current = ionic_current(states, membrane, ion_params)
    lap_phi = flux_sum(padded(phi_new), unit_faces)
    new_membrane = membrane + time_step * (-intra_cond * (lap_membrane + lap_phi) - current)

    peer_count = N_GX * N_GY
    slot_ids = jnp.arange(CAP, dtype=jnp.int32)
    slab_ids = jnp.arange(N_GRP, dtype=jnp.int32)[:, None, None, None]
    peer_ids = jnp.arange(peer_count, dtype=jnp.int32)[None, :, None, None]
    sender_live = slot_ids[None, None, None, :] < send_count.reshape(N_GRP, peer_count, peer_count)[..., None]
    heart_index = (slab_ids * peer_count + peer_ids) * HNODES + send_node.reshape(N_GRP, peer_count, peer_count, CAP).astype(jnp.int32)
    heart_flat = to_blocks(phi_new, HX, HY, HZ).reshape(-1)
    sent_vals = jnp.where(sender_live, heart_flat[heart_index], jnp.zeros((), jnp.float32))
    arrived = sent_vals.transpose(0, 2, 1, 3)
    receiver_live = slot_ids[None, None, None, :] < recv_count.reshape(N_GRP, peer_count, peer_count)[..., None]
    torso_index = (slab_ids * peer_count + peer_ids) * TVOX + recv_voxel.reshape(N_GRP, peer_count, peer_count, CAP).astype(jnp.int32)
    live_weight = receiver_live.astype(jnp.float32) * penalty
    right_side = jnp.zeros((N_GRP * peer_count * TVOX,), jnp.float32).at[torso_index.reshape(-1)].add((live_weight * arrived).reshape(-1))
    weight = jnp.zeros((N_GRP * peer_count * TVOX,), jnp.float32).at[torso_index.reshape(-1)].add(live_weight.reshape(-1))
    right_side = from_blocks(right_side.reshape(N_GRP, peer_count, TVOX), TX, TY, TZ)
    weight = from_blocks(weight.reshape(N_GRP, peer_count, TVOX), TX, TY, TZ)

    conduct = tissue_scale * lookup(labels, cond_table)
    conductances = global_faces(padded(conduct), torso_shape)
    diagonal = face_total(conductances) + weight
    iterate = torso_phi
    update = jnp.zeros_like(iterate)
    for carry_coef, resid_coef in cheb_coeffs(SWEEPS_T):
        residue = (right_side - (flux_sum(padded(iterate), conductances) + weight * iterate)) / diagonal
        update = carry_coef * update + resid_coef * residue
        iterate = iterate + update
    torso_out = iterate

    torso_flat = to_blocks(torso_out, TX, TY, TZ).reshape(-1)
    returned = jnp.where(receiver_live, penalty * (arrived - torso_flat[torso_index]), jnp.zeros((), jnp.float32))
    came_back = returned.transpose(0, 2, 1, 3)
    flux_in = jnp.zeros((N_GRP * peer_count * HNODES,), jnp.float32).at[heart_index.reshape(-1)].add(jnp.where(sender_live, came_back, jnp.zeros((), jnp.float32)).reshape(-1))
    flux_in = from_blocks(flux_in.reshape(N_GRP, peer_count, HNODES), HX, HY, HZ)
    heart_phi = phi_new - flux_in / heart_total
    return new_membrane, heart_phi, torso_out
```

```python
import functools

import jax
import jax.numpy as jnp
from jax import lax
from jax.experimental import pallas as pl
from jax.experimental.pallas import tpu as pltpu
from jax.sharding import PartitionSpec as P

LABELS = 4
SWEEPS_H = 3
SWEEPS_T = 4
W = 4
LANES = 128

time_step = 0.1
intra_cond = 0.25
extra_cond = 0.5
penalty = 2.0
cheb_low = 0.1
cheb_high = 2.0
VMEM_LIMIT = 40 << 20


def cheb_coeffs(sweeps):
    centre = 0.5 * (cheb_high + cheb_low)
    half_width = 0.5 * (cheb_high - cheb_low)
    scaled = centre / half_width
    coeffs = [(0.0, 1.0 / centre)]
    rho_old = 1.0 / scaled
    for number in range(1, sweeps):
        rho_new = 1.0 / (2.0 * scaled - rho_old)
        coeffs.append((rho_new * rho_old, 2.0 * rho_new / half_width))
        rho_old = rho_new
    return coeffs


def f32(*shape):
    return jax.ShapeDtypeStruct(shape, jnp.float32)


def call(body, outs, name, scratch=(), smem=(), n_in=0):
    specs = [
        pl.BlockSpec(memory_space=pltpu.SMEM) if i in smem else pl.BlockSpec(memory_space=pltpu.VMEM)
        for i in range(n_in)
    ]
    return pl.pallas_call(
        body,
        out_shape=outs,
        in_specs=specs,
        out_specs=jax.tree.map(lambda _: pl.BlockSpec(memory_space=pltpu.VMEM), outs),
        scratch_shapes=list(scratch),
        name=name,
        compiler_params=pltpu.CompilerParams(vmem_limit_bytes=VMEM_LIMIT),
    )


def lane_iota(rows):
    return lax.broadcasted_iota(jnp.int32, (rows, LANES), 1)


def z_faces(values, zlo, zhi):
    for number, value in enumerate(values):
        turned = value.T
        zlo[W * number : W * (number + 1), :] = turned[:W]
        zhi[W * number : W * (number + 1), :] = turned[LANES - W :]


def lane_pack(slices):
    rows = slices[0].shape[0]
    lane = lane_iota(rows)
    packed = jnp.zeros((rows, LANES), jnp.float32)
    for x, item in enumerate(slices):
        spot = (lane >= 2 * W * x) & (lane < 2 * W * (x + 1))
        packed = jnp.where(spot, pltpu.roll(item, (2 * W * x + W) % LANES, 1), packed)
    return packed


def lane_unpack(packed, x):
    lane = lane_iota(packed.shape[0])
    moved = pltpu.roll(packed, (2 * LANES - (2 * W * x + W)) % LANES, 1)
    return jnp.where((lane < W) | (lane >= LANES - W), moved, 0.0)


def y_body(f0, f1, rl, rr, h0, h1, ylo, yhi):
    X, Y, _ = f0.shape
    for number, h in enumerate((h0, h1)):
        part = slice(W * number, W * (number + 1))
        rows = jnp.concatenate([rl[part, :], rr[part, :]], 0).T
        wide = jnp.concatenate([rows, jnp.zeros((X * Y, LANES - 2 * W), jnp.float32)], 1)
        h[...] = pltpu.roll(wide, LANES - W, 1).reshape(X, Y, LANES)
    for out, part in ((ylo, slice(0, W)), (yhi, slice(Y - W, Y))):
        out[0:X] = jnp.concatenate([f0[:, part, :], f1[:, part, :]], 1)
        out[X] = lane_pack([jnp.concatenate([h0[x, part], h1[x, part]], 0) for x in range(X)])


def y_stage(f0, f1, rl, rr, name):
    X, Y, _ = f0.shape
    outs = (f32(X, Y, LANES), f32(X, Y, LANES), f32(X + 1, 2 * W, LANES), f32(X + 1, 2 * W, LANES))
    return call(y_body, outs, name, n_in=4)(f0, f1, rl, rr)


def x_body(both, f0, f1, h0, h1, ryl, ryr, ym0, ym1, yh0, yh1, *faces):
    X, Y, _ = f0.shape
    for number, (ym, yh) in enumerate(((ym0, yh0), (ym1, yh1))):
        part = slice(W * number, W * (number + 1))
        ym[...] = jnp.concatenate([ryr[0:X, part], ryl[0:X, part]], 1)
        packed = jnp.concatenate([ryr[X, part], ryl[X, part]], 0)
        for x in range(X):
            yh[x] = lane_unpack(packed, x)
    starts = (0, X - W) if both else (0,)
    for out, start in zip(faces, starts):
        for number, (f, h, ym, yh) in enumerate(((f0, h0, ym0, yh0), (f1, h1, ym1, yh1))):
            base = (W + 1) * number
            for x in range(W):
                out[base + x, 0:Y] = f[start + x]
                out[base + x, Y:] = ym[start + x]
            out[base + W, 0:Y] = lane_pack([h[start + x] for x in range(W)])
            out[base + W, Y:] = lane_pack([yh[start + x] for x in range(W)])


def x_stage(f0, f1, h0, h1, ryl, ryr, both, name):
    X, Y, _ = f0.shape
    side = f32(X, 2 * W, LANES)
    face = f32(2 * (W + 1), Y + 2 * W, LANES)
    outs = (side,) * 4 + (face,) * (2 if both else 1)
    return call(functools.partial(x_body, both), outs, name, n_in=6)(f0, f1, h0, h1, ryl, ryr)


def from_next(value, axis, wrap):
    count = lax.axis_size(axis)
    return lax.ppermute(value, axis, [((i + 1) % count, i) for i in range(count if wrap else count - 1)])


def from_last(value, axis, wrap):
    count = lax.axis_size(axis)
    return lax.ppermute(value, axis, [(i, (i + 1) % count) for i in range(count if wrap else count - 1)])


def assemble(M, H, number, f, h, ym, yh, rxl, rxr):
    X, Y, _ = f.shape
    base = (W + 1) * number
    M[0:X, 0:Y] = f[...]
    M[0:X, Y:] = ym[...]
    H[0:X, 0:Y] = h[...]
    H[0:X, Y:] = yh[...]
    top = M.shape[0] - 2 * W
    for start, source in ((top, rxr), (top + W, rxl)):
        if source is None:
            continue
        M[start : start + W] = source[base : base + W]
        for x in range(W):
            H[start + x] = lane_unpack(source[base + W], x)


def y_next(v):
    return pltpu.roll(v, v.shape[0] - 1, 0)


def y_last(v):
    return pltpu.roll(v, 1, 0)


def z_next(m, h):
    end = lane_iota(m.shape[0]) == LANES - 1
    rm, rh = pltpu.roll(m, LANES - 1, 1), pltpu.roll(h, LANES - 1, 1)
    return jnp.where(end, rh, rm), jnp.where(end, rm, rh)


def z_last(m, h):
    end = lane_iota(m.shape[0]) == 0
    rm, rh = pltpu.roll(m, 1, 1), pltpu.roll(h, 1, 1)
    return jnp.where(end, rh, rm), jnp.where(end, rm, rh)


def wrapped(x, count):
    return jnp.where(x >= count, x - count, jnp.where(x < 0, x + count, x))


def around(M, H, x, count):
    xn, xl = wrapped(x + 1, count), wrapped(x - 1, count)
    m, h = M[x], H[x]
    zn, zl = z_next(m, h), z_last(m, h)
    sm = M[xn] + M[xl] + y_next(m) + y_last(m) + zn[0] + zl[0]
    sh = H[xn] + H[xl] + y_next(h) + y_last(h) + zn[1] + zl[1]
    return m, h, sm, sh


def gather_rows(table, index, store):
    rows_n = table.shape[0]

    def tile(i, carry):
        top = pl.multiple_of(i * 8, 8)
        for j in range(index.shape[1] // LANES):
            spot = (pl.ds(top, 8), slice(j * LANES, (j + 1) * LANES))
            where = index[spot[0], spot[1]]
            cols, rows = where & (LANES - 1), where >> 7
            total = jnp.zeros((8, LANES), jnp.float32)
            for r in range(rows_n):
                line = jnp.broadcast_to(table[r : r + 1, :], (8, LANES))
                got = jnp.take_along_axis(line, cols, axis=1, mode="promise_in_bounds")
                total = jnp.where(rows == r, got, total)
            store(spot, where, total)
        return carry

    lax.fori_loop(0, index.shape[0] // 8, tile, 0)


def scatter_rows(values, index, rows_n, total, unroll):
    cap = index.shape[1]
    total[...] = jnp.zeros_like(total)

    def hot(count, key, weight):
        same = lax.broadcasted_iota(jnp.int32, (count, cap), 0) == key
        return jnp.where(same, weight, 0.0).astype(jnp.bfloat16)

    def one(s):
        where = index[pl.ds(s, 1), :]
        rows, cols = where >> 7, where & (LANES - 1)
        if values is None:
            left = hot(rows_n, rows, 1.0)
        else:
            value = values[pl.ds(s, 1), :]
            high = value.astype(jnp.bfloat16).astype(jnp.float32)
            left = jnp.concatenate([hot(rows_n, rows, high), hot(rows_n, rows, value - high)], 0)
        return lax.dot_general(
            left, hot(LANES, cols, 1.0), (((1,), (1,)), ((), ())), preferred_element_type=jnp.float32
        )

    def step(i, carry):
        part = one(i * unroll)
        for u in range(1, unroll):
            part = part + one(i * unroll + u)
        total[...] += part
        return carry

    lax.fori_loop(0, index.shape[0] // unroll, step, 0)


def heart_z_body(m, p, zlo, zhi):
    X, Y, _ = m.shape
    z_faces([m[...].reshape(X * Y, LANES), p[...].reshape(X * Y, LANES)], zlo, zhi)


def torso_z_body(table, phi, scale, labels, cond, zlo, zhi):
    X, Y, _ = phi.shape
    picked = jnp.zeros(labels.shape, jnp.float32)
    for number in range(LABELS):
        picked = jnp.where(labels[...] == number, table[number], picked)
    value = scale[...] * picked
    cond[...] = value
    z_faces([phi[...].reshape(X * Y, LANES), value.reshape(X * Y, LANES)], zlo, zhi)


def weight_body(index, weight, total):
    scatter_rows(None, index, total.shape[0], total, 8)
    weight[...] = (penalty * total[...]).reshape(weight.shape)


def heart_tiles(place, Y):
    j, g = place[0], place[1]
    row = lax.broadcasted_iota(jnp.int32, (Y + 2 * W, LANES), 0)
    lane = lane_iota(Y + 2 * W)
    yg = j * Y + jnp.where(row >= Y + W, row - Y - 2 * W, row)
    tiles = []
    for zl in (lane, jnp.where(lane >= LANES // 2, lane - LANES, lane + LANES)):
        zg = g * LANES + zl
        ny, nz = place[2], place[3]
        one = lambda cond: cond.astype(jnp.float32)
        inside = one((yg >= 0) & (yg < ny) & (zg >= 0) & (zg < nz))
        diag = 2.0 + one(yg + 1 < ny) + one(yg - 1 >= 0) + one(zg + 1 < nz) + one(zg - 1 >= 0)
        tiles.append((diag, inside / diag, inside))
    return tiles


def heart_body(
    place, m, p, hm, hp, ymm, ymp, yhm, yhp, rxl, rxr, index,
    phi_out, base_out, sent, mM, mH, uM, uH, wM, wH, vM, vH, fM, fH,
):
    X, Y, _ = m.shape
    count = X + 2 * W
    assemble(mM, mH, 0, m, hm, ymm, yhm, rxl, rxr)
    assemble(uM, uH, 1, p, hp, ymp, yhp, rxl, rxr)
    (dm, qm, im), (dh, qh, ih) = heart_tiles(place, Y)
    ratio = intra_cond / (intra_cond + extra_cond)

    def prepare(x, carry):
        a, b, sa, sb = around(mM, mH, x, count)
        fM[x] = -ratio * (a * im - sa * qm)
        fH[x] = -ratio * (b * ih - sb * qh)
        vM[x] = jnp.zeros_like(a)
        vH[x] = jnp.zeros_like(b)
        return carry

    lax.fori_loop(0, count, prepare, 0)
    old, new = (uM, uH), (wM, wH)
    for carry_coef, resid_coef in cheb_coeffs(SWEEPS_H):

        def sweep(x, carry, old=old, new=new, cc=carry_coef, rc=resid_coef):
            a, b, sa, sb = around(old[0], old[1], x, count)
            va = cc * vM[x] + rc * (fM[x] + sa * qm - a)
            vb = cc * vH[x] + rc * (fH[x] + sb * qh - b)
            vM[x], vH[x] = va, vb
            new[0][x], new[1][x] = a + va, b + vb
            return carry

        lax.fori_loop(0, count, sweep, 0)
        old, new = new, old
    phi_out[...] = old[0][0:X, 0:Y]

    def finish(x, carry):
        a, _, sa, _ = around(mM, mH, x, count)
        c, _, sc, _ = around(old[0], old[1], x, count)
        lap = dm * (a + c) - (sa + sc)
        base_out[x] = (a - time_step * intra_cond * lap)[0:Y]
        return carry

    lax.fori_loop(0, X, finish, 0)
    table = phi_out[0 : X // 4].reshape(X // 4 * Y, LANES)

    def store(spot, where, value):
        sent[spot[0], spot[1]] = value

    gather_rows(table, index, store)


def right_body(arrived, index, weight, right, zlo, zhi, total):
    rows = index_rows = weight.shape[0] * weight.shape[1]
    scatter_rows(arrived, index, rows, total, 8)
    value = penalty * (total[0:rows] + total[rows : 2 * rows])
    right[...] = value.reshape(right.shape)
    z_faces([value, weight[...].reshape(index_rows, LANES)], zlo, zhi)


def faces_body(
    p, c, hp, hc, ymp, ymc, yhp, yhc, rxl, rxr,
    uM, uH, fxM, fxH, fyM, fyH, fzM, fzH, dM, dH, cM, cH,
):
    X, Y, _ = p.shape
    count = X + 2 * W
    assemble(uM, uH, 0, p, hp, ymp, yhp, rxl, rxr)
    assemble(cM, cH, 1, c, hc, ymc, yhc, rxl, rxr)

    def harmonic(a, b):
        total = a + b
        return jnp.where(total > 0.0, 2.0 * a * b / jnp.where(total > 0.0, total, 1.0), 0.0)

    def prepare(x, carry):
        xn = wrapped(x + 1, count)
        a, b = cM[x], cH[x]
        za, zb = z_next(a, b)
        fxM[x], fxH[x] = harmonic(a, cM[xn]), harmonic(b, cH[xn])
        fyM[x], fyH[x] = harmonic(a, y_next(a)), harmonic(b, y_next(b))
        fzM[x], fzH[x] = harmonic(a, za), harmonic(b, zb)
        return carry

    lax.fori_loop(0, count, prepare, 0)

    def total(x, carry):
        xl = wrapped(x - 1, count)
        za, zb = z_last(fzM[x], fzH[x])
        dM[x] = fxM[x] + fxM[xl] + fyM[x] + y_last(fyM[x]) + fzM[x] + za
        dH[x] = fxH[x] + fxH[xl] + fyH[x] + y_last(fyH[x]) + fzH[x] + zb
        return carry

    lax.fori_loop(0, count, total, 0)


def torso_body(
    right, weight, hr, hw, ymr, ymw, yhr, yhw, rxr, arrived, index,
    uM, uH, fxM, fxH, fyM, fyH, fzM, fzH, dM, dH,
    torso_out, returned, aM, aH, bM, bH, vM, vH, rM, rH, iM, iH,
):
    count = uM.shape[0]
    X, Y = torso_out.shape[0], torso_out.shape[1]
    S = right.shape[0]
    for ref in (rM, rH, iM, iH):
        ref[S:X] = jnp.zeros((X - S,) + ref.shape[1:], jnp.float32)
        ref[X + W :] = jnp.zeros((W,) + ref.shape[1:], jnp.float32)
    assemble(rM, rH, 0, right, hr, ymr, yhr, None, rxr)
    assemble(iM, iH, 1, weight, hw, ymw, yhw, None, rxr)

    def invert(x, carry):
        for d, i in ((dM, iM), (dH, iH)):
            whole = d[x] + i[x]
            i[x] = jnp.where(whole > 0.0, 1.0 / jnp.where(whole > 0.0, whole, 1.0), 0.0)
        return carry

    lax.fori_loop(0, count, invert, 0)
    old, new = (uM, uH), (aM, aH)
    for number, (carry_coef, resid_coef) in enumerate(cheb_coeffs(SWEEPS_T)):

        def sweep(x, carry, old=old, new=new, cc=carry_coef, rc=resid_coef, number=number):
            xn, xl = wrapped(x + 1, count), wrapped(x - 1, count)
            m, h = old[0][x], old[1][x]
            fy, gy, fz, gz = fyM[x], fyH[x], fzM[x], fzH[x]
            zn = z_next(m, h)
            zl = z_last(fz * m, gz * h)
            sm = fxM[x] * old[0][xn] + fxM[xl] * old[0][xl] + fy * y_next(m) + y_last(fy * m)
            sh = fxH[x] * old[1][xn] + fxH[xl] * old[1][xl] + gy * y_next(h) + y_last(gy * h)
            sm = sm + fz * zn[0] + zl[0]
            sh = sh + gz * zn[1] + zl[1]
            va = rc * ((rM[x] + sm) * iM[x] - m)
            vb = rc * ((rH[x] + sh) * iH[x] - h)
            if number > 0:
                va, vb = cc * vM[x] + va, cc * vH[x] + vb
            vM[x], vH[x] = va, vb
            new[0][x], new[1][x] = m + va, h + vb
            return carry

        lax.fori_loop(0, count, sweep, 0)
        old, new = new, ((bM, bH) if number == 0 else old)
    torso_out[...] = old[0][0:X, 0:Y]
    table = torso_out[0:S].reshape(S * Y, LANES)

    def store(spot, where, value):
        returned[spot[0], spot[1]] = jnp.where(
            where >= 0, penalty * (arrived[spot[0], spot[1]] - value), 0.0
        )

    gather_rows(table, index, store)


def final_body(place, back, index, phi, out, total):
    X, Y, _ = phi.shape
    rows = X // 4 * Y
    scatter_rows(back, index, rows, total, 8)
    flux = (total[0:rows] + total[rows : 2 * rows]).reshape(X // 4, Y, LANES)
    (dm, _, _), _ = heart_tiles(place, Y)
    out[X // 4 :] = phi[X // 4 :]
    scale = (1.0 / ((intra_cond + extra_cond) * dm))[0:Y]
    for x in range(X // 4):
        out[x] = phi[x] - flux[x] * scale


def ionic_current(states, membrane, ion_params):
    params_col = ion_params[:, :, None, None, None]
    gate_vals = states.astype(jnp.float32)
    voltage = membrane[None]
    steady = jax.nn.sigmoid((voltage - params_col[0]) / params_col[1])
    gate_vals = steady + (gate_vals - steady) * jnp.exp(-time_step * params_col[2])
    return jnp.sum(params_col[3] * gate_vals * (voltage - params_col[4]), axis=0)


def per_device(
    states, membrane, phi_heart, ion_params, torso_phi, tissue_scale, labels, cond_table,
    send_node, send_count, recv_voxel, recv_count,
):
    X, Y, _ = membrane.shape
    TX, TY, _ = torso_phi.shape
    peers = lax.axis_size("gx") * lax.axis_size("gy")
    cap = send_node.shape[-1]
    place = jnp.stack([
        lax.axis_index("gy"), lax.axis_index("grp"),
        jnp.int32(Y * lax.axis_size("gy")), jnp.int32(LANES * lax.axis_size("grp")),
    ])
    slots = jnp.arange(cap, dtype=jnp.int32)[None, :]
    send_index = jnp.where(slots < send_count.reshape(peers, 1), send_node.reshape(peers, cap), -1)
    recv_index = jnp.where(slots < recv_count.reshape(peers, 1), recv_voxel.reshape(peers, cap), -1)

    def exchange(f0, f1, zlo, zhi, both, name):
        rr, rl = from_next(zlo, "grp", False), from_last(zhi, "grp", False)
        h0, h1, ylo, yhi = y_stage(f0, f1, rl, rr, name + "_y")
        ryr, ryl = from_next(ylo, "gy", False), from_last(yhi, "gy", False)
        ym0, ym1, yh0, yh1, *faces = x_stage(f0, f1, h0, h1, ryl, ryr, both, name + "_x")
        moved = [from_next(faces[0], "gx", True)]
        if both:
            moved.insert(0, from_last(faces[1], "gx", True))
        return (h0, h1, ym0, ym1, yh0, yh1, *moved)

    zlo, zhi = call(heart_z_body, (f32(2 * W, X * Y),) * 2, "heart_z", n_in=2)(membrane, phi_heart)
    heart_halo = exchange(membrane, phi_heart, zlo, zhi, True, "heart")
    cond, tzlo, tzhi = call(
        torso_z_body, (f32(TX, TY, LANES),) + (f32(2 * W, TX * TY),) * 2, "torso_z", smem=(0,), n_in=4
    )(cond_table, torso_phi, tissue_scale, labels)
    S = TX // 4
    weight = call(
        weight_body, f32(S, TY, LANES), "weight", scratch=[pltpu.VMEM((S * TY, LANES), jnp.float32)], n_in=1
    )(recv_index)
    ext = pltpu.VMEM((X + 2 * W, Y + 2 * W, LANES), jnp.float32)
    phi_new, base, sent = call(
        heart_body,
        (f32(X, Y, LANES), f32(X, Y, LANES), f32(peers, cap)),
        "heart", scratch=[ext] * 10, smem=(0,), n_in=12,
    )(place, membrane, phi_heart, *heart_halo, send_index)
    arrived = lax.all_to_all(sent, ("gx", "gy"), split_axis=0, concat_axis=0, tiled=True)

    torso_halo = exchange(torso_phi, cond, tzlo, tzhi, True, "torso")
    text = (TX + 2 * W, TY + 2 * W, LANES)
    faces = call(
        faces_body, (f32(*text),) * 10, "faces", scratch=[pltpu.VMEM(text, jnp.float32)] * 2, n_in=10
    )(torso_phi, cond, *torso_halo)
    current = ionic_current(states, membrane, ion_params)
    new_membrane = base - time_step * current

    right, rzlo, rzhi = call(
        right_body,
        (f32(S, TY, LANES), f32(2 * W, S * TY), f32(2 * W, S * TY)),
        "right", scratch=[pltpu.VMEM((2 * S * TY, LANES), jnp.float32)], n_in=3,
    )(arrived, recv_index, weight)
    right_halo = exchange(right, weight, rzlo, rzhi, False, "right")
    torso_out, returned = call(
        torso_body,
        (f32(TX, TY, LANES), f32(peers, cap)),
        "torso", scratch=[pltpu.VMEM(text, jnp.float32)] * 10, n_in=21,
    )(right, weight, *right_halo, arrived, recv_index, *faces)
    back = lax.all_to_all(returned, ("gx", "gy"), split_axis=0, concat_axis=0, tiled=True)
    heart_phi = call(
        final_body, f32(X, Y, LANES), "final",
        scratch=[pltpu.VMEM((2 * X // 4 * Y, LANES), jnp.float32)], smem=(0,), n_in=4,
    )(place, back, send_index, phi_new)
    return (new_membrane, heart_phi, torso_out)


def solution(mesh):
    placed = (
        P(None, "gx", "gy", "grp"),
        P("gx", "gy", "grp"),
        P("gx", "gy", "grp"),
        P(),
        P("gx", "gy", "grp"),
        P("gx", "gy", "grp"),
        P("gx", "gy", "grp"),
        P(),
        P("grp", "gx", "gy", None, None),
        P("grp", "gx", "gy", None),
        P("grp", "gx", "gy", None, None),
        P("grp", "gx", "gy", None),
    )
    return jax.shard_map(
        per_device,
        mesh=mesh,
        in_specs=placed,
        out_specs=(P("gx", "gy", "grp"), P("gx", "gy", "grp"), P("gx", "gy", "grp")),
        check_vma=False,
    )
```

```python
import functools

import jax
import jax.numpy as jnp
from jax import lax
from jax.experimental import pallas as pl
from jax.experimental.pallas import tpu as pltpu
from jax.sharding import PartitionSpec as P

LABELS = 4
SWEEPS_H = 3
SWEEPS_T = 4
W = 4
LANES = 128

time_step = 0.1
intra_cond = 0.25
extra_cond = 0.5
penalty = 2.0
cheb_low = 0.1
cheb_high = 2.0
VMEM_LIMIT = 40 << 20


def cheb_coeffs(sweeps):
    centre = 0.5 * (cheb_high + cheb_low)
    half_width = 0.5 * (cheb_high - cheb_low)
    scaled = centre / half_width
    coeffs = [(0.0, 1.0 / centre)]
    rho_old = 1.0 / scaled
    for number in range(1, sweeps):
        rho_new = 1.0 / (2.0 * scaled - rho_old)
        coeffs.append((rho_new * rho_old, 2.0 * rho_new / half_width))
        rho_old = rho_new
    return coeffs


def f32(*shape):
    return jax.ShapeDtypeStruct(shape, jnp.float32)


def call(body, outs, name, scratch=(), smem=(), n_in=0):
    specs = [
        pl.BlockSpec(memory_space=pltpu.SMEM) if i in smem else pl.BlockSpec(memory_space=pltpu.VMEM)
        for i in range(n_in)
    ]
    return pl.pallas_call(
        body,
        out_shape=outs,
        in_specs=specs,
        out_specs=jax.tree.map(lambda _: pl.BlockSpec(memory_space=pltpu.VMEM), outs),
        scratch_shapes=list(scratch),
        name=name,
        compiler_params=pltpu.CompilerParams(vmem_limit_bytes=VMEM_LIMIT),
    )


def loop(count, body, unroll):
    def step(i, carry):
        for u in range(unroll):
            body(i * unroll + u)
        return carry

    lax.fori_loop(0, count // unroll, step, 0)


def lane_iota(rows):
    return lax.broadcasted_iota(jnp.int32, (rows, LANES), 1)


def z_faces(values, zlo, zhi):
    for number, value in enumerate(values):
        turned = value.T
        zlo[W * number : W * (number + 1), :] = turned[:W]
        zhi[W * number : W * (number + 1), :] = turned[LANES - W :]


def lane_pack(slices):
    rows = slices[0].shape[0]
    lane = lane_iota(rows)
    packed = jnp.zeros((rows, LANES), jnp.float32)
    for x, item in enumerate(slices):
        spot = (lane >= 2 * W * x) & (lane < 2 * W * (x + 1))
        packed = jnp.where(spot, pltpu.roll(item, (2 * W * x + W) % LANES, 1), packed)
    return packed


def lane_unpack(packed, x):
    lane = lane_iota(packed.shape[0])
    moved = pltpu.roll(packed, (2 * LANES - (2 * W * x + W)) % LANES, 1)
    return jnp.where((lane < W) | (lane >= LANES - W), moved, 0.0)


def edges(place):
    j, g, ny, nz, rows = place[0], place[1], place[2], place[3], place[4]
    return (j > 0, (j + 1) * rows < ny), (g > 0, (g + 1) * LANES < nz)


def y_part(f0, f1, rl, rr, h0, h1, ylo, yhi, near):
    X, Y, _ = f0.shape
    for number, h in enumerate((h0, h1)):
        part = slice(W * number, W * (number + 1))
        left = jnp.where(near[0], rl[part, :], 0.0)
        right = jnp.where(near[1], rr[part, :], 0.0)
        rows = jnp.concatenate([left, right], 0).T
        wide = jnp.concatenate([rows, jnp.zeros((X * Y, LANES - 2 * W), jnp.float32)], 1)
        h[...] = pltpu.roll(wide, LANES - W, 1).reshape(X, Y, LANES)
    for out, part in ((ylo, slice(0, W)), (yhi, slice(Y - W, Y))):
        out[0:X] = jnp.concatenate([f0[:, part, :], f1[:, part, :]], 1)
        out[X] = lane_pack([jnp.concatenate([h0[x, part], h1[x, part]], 0) for x in range(X)])


def x_part(f0, f1, h0, h1, ryl, ryr, ym0, ym1, yh0, yh1, faces, near):
    X, Y, _ = f0.shape
    for number, (ym, yh) in enumerate(((ym0, yh0), (ym1, yh1))):
        part = slice(W * number, W * (number + 1))
        right = jnp.where(near[1], ryr[:, part], 0.0)
        left = jnp.where(near[0], ryl[:, part], 0.0)
        both = jnp.concatenate([right, left], 1)
        ym[...] = both[0:X]
        for x in range(X):
            yh[x] = lane_unpack(both[X], x)
    for out, start in zip(faces, (0, X - W)):
        for number, (f, h, ym, yh) in enumerate(((f0, h0, ym0, yh0), (f1, h1, ym1, yh1))):
            base = (W + 1) * number
            for x in range(W):
                out[base + x, 0:Y] = f[start + x]
                out[base + x, Y:] = ym[start + x]
            out[base + W, 0:Y] = lane_pack([h[start + x] for x in range(W)])
            out[base + W, Y:] = lane_pack([yh[start + x] for x in range(W)])


def y_body(groups, place, *refs):
    fields, rest = refs[: 2 * groups], refs[2 * groups :]
    rl, rr, halos, ylo, yhi = rest[0], rest[1], rest[2:-2], rest[-2], rest[-1]
    near = edges(place)[1]
    col = row = 0
    for k in range(groups):
        f0, f1 = fields[2 * k : 2 * k + 2]
        X, Y, _ = f0.shape
        cols, rows = pl.ds(col, X * Y), pl.ds(row, X + 1)
        y_part(
            f0, f1, rl.at[:, cols], rr.at[:, cols], halos[2 * k], halos[2 * k + 1],
            ylo.at[rows], yhi.at[rows], near,
        )
        col, row = col + X * Y, row + X + 1


def x_body(groups, place, *refs):
    fields, halos, rest = refs[: 2 * groups], refs[2 * groups : 4 * groups], refs[4 * groups :]
    ryl, ryr, sides, faces = rest[0], rest[1], rest[2 : 2 + 4 * groups], rest[2 + 4 * groups :]
    near = edges(place)[0]
    row = top = 0
    for k in range(groups):
        X, Y, _ = fields[2 * k].shape
        rows, tops = pl.ds(row, X + 1), pl.ds(top, Y + 2 * W)
        x_part(
            *fields[2 * k : 2 * k + 2], *halos[2 * k : 2 * k + 2], ryl.at[rows], ryr.at[rows],
            *sides[4 * k : 4 * k + 4], [face.at[:, tops] for face in faces], near,
        )
        row, top = row + X + 1, top + Y + 2 * W


def from_next(value, axis):
    count = lax.axis_size(axis)
    return lax.ppermute(value, axis, [((i + 1) % count, i) for i in range(count)])


def from_last(value, axis):
    count = lax.axis_size(axis)
    return lax.ppermute(value, axis, [(i, (i + 1) % count) for i in range(count)])


def exchange(place, groups, zlo, zhi, both, name):
    count = len(groups)
    fields = [f for group in groups for f in group]
    shapes = [group[0].shape for group in groups]
    rr, rl = from_next(zlo, "grp"), from_last(zhi, "grp")
    tall = f32(sum(s[0] + 1 for s in shapes), 2 * W, LANES)
    *halos, ylo, yhi = call(
        functools.partial(y_body, count),
        tuple(f32(*f.shape) for f in fields) + (tall, tall),
        name + "_y", smem=(0,), n_in=3 + len(fields),
    )(place, *fields, rl, rr)
    ryr, ryl = from_next(ylo, "gy"), from_last(yhi, "gy")
    sides = tuple(f32(s[0], 2 * W, LANES) for s in shapes for _ in range(4))
    face = f32(2 * (W + 1), sum(s[1] + 2 * W for s in shapes), LANES)
    outs = call(
        functools.partial(x_body, count), sides + (face,) * (2 if both else 1),
        name + "_x", smem=(0,), n_in=3 + 2 * len(fields),
    )(place, *fields, *halos, ryl, ryr)
    moved = [from_next(outs[len(sides)], "gx")]
    if both:
        moved.insert(0, from_last(outs[len(sides) + 1], "gx"))
    return [(*halos[2 * k : 2 * k + 2], *outs[4 * k : 4 * k + 4]) for k in range(count)], moved


def assemble(M, H, number, f, h, ym, yh, rxl, rxr):
    X, Y, _ = f.shape
    base = (W + 1) * number
    M[0:X, 0:Y] = f[...]
    M[0:X, Y:] = ym[...]
    H[0:X, 0:Y] = h[...]
    H[0:X, Y:] = yh[...]
    top = M.shape[0] - 2 * W
    for start, source in ((top, rxr), (top + W, rxl)):
        if source is None:
            continue
        M[start : start + W] = source[base : base + W]
        for x in range(W):
            H[start + x] = lane_unpack(source[base + W], x)


def y_next(v):
    return pltpu.roll(v, v.shape[0] - 1, 0)


def y_last(v):
    return pltpu.roll(v, 1, 0)


def z_next(m, h):
    end = lane_iota(m.shape[0]) == LANES - 1
    rm, rh = pltpu.roll(m, LANES - 1, 1), pltpu.roll(h, LANES - 1, 1)
    return jnp.where(end, rh, rm), jnp.where(end, rm, rh)


def z_last(m, h):
    end = lane_iota(m.shape[0]) == 0
    rm, rh = pltpu.roll(m, 1, 1), pltpu.roll(h, 1, 1)
    return jnp.where(end, rh, rm), jnp.where(end, rm, rh)


def wrapped(x, count):
    return jnp.where(x >= count, x - count, jnp.where(x < 0, x + count, x))


def around(M, H, x, count):
    xn, xl = wrapped(x + 1, count), wrapped(x - 1, count)
    m, h = M[x], H[x]
    zn, zl = z_next(m, h), z_last(m, h)
    sm = M[xn] + M[xl] + y_next(m) + y_last(m) + zn[0] + zl[0]
    sh = H[xn] + H[xl] + y_next(h) + y_last(h) + zn[1] + zl[1]
    return m, h, sm, sh


def gather_rows(table, index, store):
    rows_n = table.shape[0]

    def tile(i, carry):
        top = pl.multiple_of(i * 8, 8)
        for j in range(index.shape[1] // LANES):
            spot = (pl.ds(top, 8), slice(j * LANES, (j + 1) * LANES))
            where = index[spot[0], spot[1]]
            cols, rows = where & (LANES - 1), where >> 7
            total = jnp.zeros((8, LANES), jnp.float32)
            for r in range(rows_n):
                line = jnp.broadcast_to(table[r : r + 1, :], (8, LANES))
                got = jnp.take_along_axis(line, cols, axis=1, mode="promise_in_bounds")
                total = jnp.where(rows == r, got, total)
            store(spot, where, total)
        return carry

    lax.fori_loop(0, index.shape[0] // 8, tile, 0)


def scatter_rows(values, index, rows_n, total, unroll):
    cap = index.shape[1]
    total[...] = jnp.zeros_like(total)

    def hot(count, key, weight):
        same = lax.broadcasted_iota(jnp.int32, (count, cap), 0) == key
        return jnp.where(same, weight, 0.0).astype(jnp.bfloat16)

    def one(s):
        where = index[pl.ds(s, 1), :]
        rows, cols = where >> 7, where & (LANES - 1)
        if values is None:
            left = hot(rows_n, rows, 1.0)
        else:
            value = values[pl.ds(s, 1), :]
            high = value.astype(jnp.bfloat16).astype(jnp.float32)
            left = jnp.concatenate([hot(rows_n, rows, high), hot(rows_n, rows, value - high)], 0)
        return lax.dot_general(
            left, hot(LANES, cols, 1.0), (((1,), (1,)), ((), ())), preferred_element_type=jnp.float32
        )

    def step(i, carry):
        part = one(i * unroll)
        for u in range(1, unroll):
            part = part + one(i * unroll + u)
        total[...] += part
        return carry

    lax.fori_loop(0, index.shape[0] // unroll, step, 0)


def start_body(table, m, p, phi, scale, labels, cond, zlo, zhi):
    X, Y, _ = m.shape
    TX, TY, _ = phi.shape
    cols, more = pl.ds(0, X * Y), pl.ds(X * Y, TX * TY)
    z_faces(
        [m[...].reshape(X * Y, LANES), p[...].reshape(X * Y, LANES)], zlo.at[:, cols], zhi.at[:, cols]
    )
    picked = jnp.zeros(labels.shape, jnp.float32)
    for number in range(LABELS):
        picked = jnp.where(labels[...] == number, table[number], picked)
    value = scale[...] * picked
    cond[...] = value
    z_faces(
        [phi[...].reshape(TX * TY, LANES), value.reshape(TX * TY, LANES)], zlo.at[:, more], zhi.at[:, more]
    )


def weight_body(index, weight, total):
    scatter_rows(None, index, total.shape[0], total, 8)
    weight[...] = (penalty * total[...]).reshape(weight.shape)


def heart_tiles(place, Y):
    j, g = place[0], place[1]
    row = lax.broadcasted_iota(jnp.int32, (Y + 2 * W, LANES), 0)
    lane = lane_iota(Y + 2 * W)
    yg = j * Y + jnp.where(row >= Y + W, row - Y - 2 * W, row)
    tiles = []
    for zl in (lane, jnp.where(lane >= LANES // 2, lane - LANES, lane + LANES)):
        zg = g * LANES + zl
        ny, nz = place[2], place[3]
        one = lambda cond: cond.astype(jnp.float32)
        inside = one((yg >= 0) & (yg < ny) & (zg >= 0) & (zg < nz))
        diag = 2.0 + one(yg + 1 < ny) + one(yg - 1 >= 0) + one(zg + 1 < nz) + one(zg - 1 >= 0)
        tiles.append((diag, inside / diag, inside))
    return tiles


def heart_body(
    place, m, p, hm, hp, ymm, ymp, yhm, yhp, rxl, rxr, index,
    phi_out, base_out, sent, mM, mH, uM, uH, wM, wH, vM, vH, fM, fH,
):
    X, Y, _ = m.shape
    count = X + 2 * W
    near = pl.ds(0, Y + 2 * W)
    assemble(mM, mH, 0, m, hm, ymm, yhm, rxl.at[:, near], rxr.at[:, near])
    assemble(uM, uH, 1, p, hp, ymp, yhp, rxl.at[:, near], rxr.at[:, near])
    (dm, qm, im), (dh, qh, ih) = heart_tiles(place, Y)
    ratio = intra_cond / (intra_cond + extra_cond)

    def prepare(x):
        a, b, sa, sb = around(mM, mH, x, count)
        fM[x] = -ratio * (a * im - sa * qm)
        fH[x] = -ratio * (b * ih - sb * qh)

    loop(count, prepare, 4)
    old, new = (uM, uH), (wM, wH)
    for number, (carry_coef, resid_coef) in enumerate(cheb_coeffs(SWEEPS_H)):

        def sweep(x, old=old, new=new, cc=carry_coef, rc=resid_coef, number=number):
            a, b, sa, sb = around(old[0], old[1], x, count)
            va = rc * (fM[x] + sa * qm - a)
            vb = rc * (fH[x] + sb * qh - b)
            if number > 0:
                va, vb = cc * vM[x] + va, cc * vH[x] + vb
            vM[x], vH[x] = va, vb
            new[0][x], new[1][x] = a + va, b + vb

        loop(count, sweep, 4)
        old, new = new, old
    phi_out[...] = old[0][0:X, 0:Y]

    def finish(x):
        a, _, sa, _ = around(mM, mH, x, count)
        c, _, sc, _ = around(old[0], old[1], x, count)
        lap = dm * (a + c) - (sa + sc)
        base_out[x] = (a - time_step * intra_cond * lap)[0:Y]

    loop(X, finish, 4)
    table = phi_out[0 : X // 4].reshape(X // 4 * Y, LANES)

    def store(spot, where, value):
        sent[spot[0], spot[1]] = value

    gather_rows(table, index, store)


def right_body(arrived, index, weight, right, zlo, zhi, total):
    rows = index_rows = weight.shape[0] * weight.shape[1]
    scatter_rows(arrived, index, rows, total, 8)
    value = penalty * (total[0:rows] + total[rows : 2 * rows])
    right[...] = value.reshape(right.shape)
    z_faces([value, weight[...].reshape(index_rows, LANES)], zlo, zhi)


def faces_body(
    p, c, hp, hc, ymp, ymc, yhp, yhc, rxl, rxr,
    uM, uH, fxM, fxH, fyM, fyH, fzM, fzH, dM, dH, cM, cH,
):
    X, Y, _ = p.shape
    count = X + 2 * W
    far = pl.ds(rxl.shape[1] - Y - 2 * W, Y + 2 * W)
    assemble(uM, uH, 0, p, hp, ymp, yhp, rxl.at[:, far], rxr.at[:, far])
    assemble(cM, cH, 1, c, hc, ymc, yhc, rxl.at[:, far], rxr.at[:, far])

    def harmonic(a, b):
        total = a + b
        return jnp.where(total > 0.0, 2.0 * a * b / jnp.where(total > 0.0, total, 1.0), 0.0)

    def prepare(x):
        xn = wrapped(x + 1, count)
        a, b = cM[x], cH[x]
        za, zb = z_next(a, b)
        fxM[x], fxH[x] = harmonic(a, cM[xn]), harmonic(b, cH[xn])
        fyM[x], fyH[x] = harmonic(a, y_next(a)), harmonic(b, y_next(b))
        fzM[x], fzH[x] = harmonic(a, za), harmonic(b, zb)

    loop(count, prepare, 2)

    def total(x):
        xl = wrapped(x - 1, count)
        za, zb = z_last(fzM[x], fzH[x])
        dM[x] = fxM[x] + fxM[xl] + fyM[x] + y_last(fyM[x]) + fzM[x] + za
        dH[x] = fxH[x] + fxH[xl] + fyH[x] + y_last(fyH[x]) + fzH[x] + zb

    loop(count, total, 2)


def torso_body(
    right, weight, hr, hw, ymr, ymw, yhr, yhw, rxr, arrived, index,
    uM, uH, fxM, fxH, fyM, fyH, fzM, fzH, dM, dH,
    torso_out, returned, aM, aH, bM, bH, vM, vH, rM, rH, iM, iH,
):
    count = uM.shape[0]
    X, Y = torso_out.shape[0], torso_out.shape[1]
    S = right.shape[0]
    for ref in (rM, rH, iM, iH):
        ref[S:X] = jnp.zeros((X - S,) + ref.shape[1:], jnp.float32)
        ref[X + W :] = jnp.zeros((W,) + ref.shape[1:], jnp.float32)
    assemble(rM, rH, 0, right, hr, ymr, yhr, None, rxr)
    assemble(iM, iH, 1, weight, hw, ymw, yhw, None, rxr)

    def invert(x):
        for d, i in ((dM, iM), (dH, iH)):
            whole = d[x] + i[x]
            i[x] = jnp.where(whole > 0.0, 1.0 / jnp.where(whole > 0.0, whole, 1.0), 0.0)

    loop(count, invert, 4)
    old, new = (uM, uH), (aM, aH)
    for number, (carry_coef, resid_coef) in enumerate(cheb_coeffs(SWEEPS_T)):

        def sweep(x, old=old, new=new, cc=carry_coef, rc=resid_coef, number=number):
            xn, xl = wrapped(x + 1, count), wrapped(x - 1, count)
            m, h = old[0][x], old[1][x]
            fy, gy, fz, gz = fyM[x], fyH[x], fzM[x], fzH[x]
            zn = z_next(m, h)
            zl = z_last(fz * m, gz * h)
            sm = fxM[x] * old[0][xn] + fxM[xl] * old[0][xl] + fy * y_next(m) + y_last(fy * m)
            sh = fxH[x] * old[1][xn] + fxH[xl] * old[1][xl] + gy * y_next(h) + y_last(gy * h)
            sm = sm + fz * zn[0] + zl[0]
            sh = sh + gz * zn[1] + zl[1]
            va = rc * ((rM[x] + sm) * iM[x] - m)
            vb = rc * ((rH[x] + sh) * iH[x] - h)
            if number > 0:
                va, vb = cc * vM[x] + va, cc * vH[x] + vb
            vM[x], vH[x] = va, vb
            new[0][x], new[1][x] = m + va, h + vb

        loop(count, sweep, 2)
        old, new = new, ((bM, bH) if number == 0 else old)
    torso_out[...] = old[0][0:X, 0:Y]
    table = torso_out[0:S].reshape(S * Y, LANES)

    def store(spot, where, value):
        returned[spot[0], spot[1]] = jnp.where(
            where >= 0, penalty * (arrived[spot[0], spot[1]] - value), 0.0
        )

    gather_rows(table, index, store)


def final_body(place, back, index, phi, out, total):
    X, Y, _ = phi.shape
    rows = X // 4 * Y
    scatter_rows(back, index, rows, total, 8)
    flux = (total[0:rows] + total[rows : 2 * rows]).reshape(X // 4, Y, LANES)
    (dm, _, _), _ = heart_tiles(place, Y)
    out[X // 4 :] = phi[X // 4 :]
    scale = (1.0 / ((intra_cond + extra_cond) * dm))[0:Y]
    for x in range(X // 4):
        out[x] = phi[x] - flux[x] * scale


def ionic_current(states, membrane, ion_params):
    params_col = ion_params[:, :, None, None, None]
    gate_vals = states.astype(jnp.float32)
    voltage = membrane[None]
    steady = jax.nn.sigmoid((voltage - params_col[0]) / params_col[1])
    gate_vals = steady + (gate_vals - steady) * jnp.exp(-time_step * params_col[2])
    return jnp.sum(params_col[3] * gate_vals * (voltage - params_col[4]), axis=0)


def per_device(
    states, membrane, phi_heart, ion_params, torso_phi, tissue_scale, labels, cond_table,
    send_node, send_count, recv_voxel, recv_count,
):
    X, Y, _ = membrane.shape
    TX, TY, _ = torso_phi.shape
    peers = lax.axis_size("gx") * lax.axis_size("gy")
    cap = send_node.shape[-1]
    place = jnp.stack([
        lax.axis_index("gy"), lax.axis_index("grp"),
        jnp.int32(Y * lax.axis_size("gy")), jnp.int32(LANES * lax.axis_size("grp")), jnp.int32(Y),
    ])
    slots = jnp.arange(cap, dtype=jnp.int32)[None, :]
    send_index = jnp.where(slots < send_count.reshape(peers, 1), send_node.reshape(peers, cap), -1)
    recv_index = jnp.where(slots < recv_count.reshape(peers, 1), recv_voxel.reshape(peers, cap), -1)

    wide = f32(2 * W, X * Y + TX * TY)
    cond, zlo, zhi = call(
        start_body, (f32(TX, TY, LANES), wide, wide), "start", smem=(0,), n_in=6
    )(cond_table, membrane, phi_heart, torso_phi, tissue_scale, labels)
    (heart_halo, torso_halo), moved = exchange(
        place, ((membrane, phi_heart), (torso_phi, cond)), zlo, zhi, True, "static"
    )
    S = TX // 4
    weight = call(
        weight_body, f32(S, TY, LANES), "weight", scratch=[pltpu.VMEM((S * TY, LANES), jnp.float32)], n_in=1
    )(recv_index)
    ext = pltpu.VMEM((X + 2 * W, Y + 2 * W, LANES), jnp.float32)
    phi_new, base, sent = call(
        heart_body,
        (f32(X, Y, LANES), f32(X, Y, LANES), f32(peers, cap)),
        "heart", scratch=[ext] * 10, smem=(0,), n_in=12,
    )(place, membrane, phi_heart, *heart_halo, *moved, send_index)
    arrived = lax.all_to_all(sent, ("gx", "gy"), split_axis=0, concat_axis=0, tiled=True)

    text = (TX + 2 * W, TY + 2 * W, LANES)
    faces = call(
        faces_body, (f32(*text),) * 10, "faces", scratch=[pltpu.VMEM(text, jnp.float32)] * 2, n_in=10
    )(torso_phi, cond, *torso_halo, *moved)
    current = ionic_current(states, membrane, ion_params)
    new_membrane = base - time_step * current

    right, rzlo, rzhi = call(
        right_body,
        (f32(S, TY, LANES), f32(2 * W, S * TY), f32(2 * W, S * TY)),
        "right", scratch=[pltpu.VMEM((2 * S * TY, LANES), jnp.float32)], n_in=3,
    )(arrived, recv_index, weight)
    (right_halo,), turned = exchange(place, ((right, weight),), rzlo, rzhi, False, "right")
    torso_out, returned = call(
        torso_body,
        (f32(TX, TY, LANES), f32(peers, cap)),
        "torso", scratch=[pltpu.VMEM(text, jnp.float32)] * 10, n_in=21,
    )(right, weight, *right_halo, *turned, arrived, recv_index, *faces)
    back = lax.all_to_all(returned, ("gx", "gy"), split_axis=0, concat_axis=0, tiled=True)
    heart_phi = call(
        final_body, f32(X, Y, LANES), "final",
        scratch=[pltpu.VMEM((2 * X // 4 * Y, LANES), jnp.float32)], smem=(0,), n_in=4,
    )(place, back, send_index, phi_new)
    return (new_membrane, heart_phi, torso_out)


def solution(mesh):
    placed = (
        P(None, "gx", "gy", "grp"),
        P("gx", "gy", "grp"),
        P("gx", "gy", "grp"),
        P(),
        P("gx", "gy", "grp"),
        P("gx", "gy", "grp"),
        P("gx", "gy", "grp"),
        P(),
        P("grp", "gx", "gy", None, None),
        P("grp", "gx", "gy", None),
        P("grp", "gx", "gy", None, None),
        P("grp", "gx", "gy", None),
    )
    return jax.shard_map(
        per_device,
        mesh=mesh,
        in_specs=placed,
        out_specs=(P("gx", "gy", "grp"), P("gx", "gy", "grp"), P("gx", "gy", "grp")),
        check_vma=False,
    )
```

```python
import functools

import jax
import jax.numpy as jnp
from jax import lax
from jax.experimental import pallas as pl
from jax.experimental.pallas import tpu as pltpu
from jax.sharding import PartitionSpec as P

LABELS = 4
SWEEPS_H = 3
SWEEPS_T = 4
W = 4
LANES = 128

time_step = 0.1
intra_cond = 0.25
extra_cond = 0.5
penalty = 2.0
cheb_low = 0.1
cheb_high = 2.0
VMEM_LIMIT = 40 << 20


def cheb_coeffs(sweeps):
    centre = 0.5 * (cheb_high + cheb_low)
    half_width = 0.5 * (cheb_high - cheb_low)
    scaled = centre / half_width
    coeffs = [(0.0, 1.0 / centre)]
    rho_old = 1.0 / scaled
    for number in range(1, sweeps):
        rho_new = 1.0 / (2.0 * scaled - rho_old)
        coeffs.append((rho_new * rho_old, 2.0 * rho_new / half_width))
        rho_old = rho_new
    return coeffs


def f32(*shape):
    return jax.ShapeDtypeStruct(shape, jnp.float32)


def call(body, outs, name, n_in, scratch=(), smem=(), hbm=(), after=()):
    spaces = [
        pltpu.SMEM if i in smem else pltpu.HBM if i in hbm else pltpu.VMEM for i in range(n_in)
    ] + [pl.ANY] * len(after)

    def run(*refs):
        body(*refs[:n_in], *refs[n_in + len(after) :])

    made = pl.pallas_call(
        run,
        out_shape=outs,
        in_specs=[pl.BlockSpec(memory_space=space) for space in spaces],
        out_specs=jax.tree.map(lambda _: pl.BlockSpec(memory_space=pltpu.VMEM), outs),
        scratch_shapes=list(scratch),
        name=name,
        compiler_params=pltpu.CompilerParams(vmem_limit_bytes=VMEM_LIMIT),
    )
    return lambda *args: made(*args, *after)


def loop(first, last, body, unroll=2):
    def step(i, carry):
        for u in range(unroll):
            body(i * unroll + u + first)
        return carry

    lax.fori_loop(0, (last - first + 1) // unroll, step, 0)


def lane_iota(rows):
    return lax.broadcasted_iota(jnp.int32, (rows, LANES), 1)


def z_faces(values, zlo, zhi):
    for number, value in enumerate(values):
        turned = value.T
        zlo[W * number : W * (number + 1), :] = turned[:W]
        zhi[W * number : W * (number + 1), :] = turned[LANES - W :]


def lane_pack(slices):
    rows = slices[0].shape[0]
    lane = lane_iota(rows)
    packed = jnp.zeros((rows, LANES), jnp.float32)
    for x, item in enumerate(slices):
        spot = (lane >= 2 * W * x) & (lane < 2 * W * (x + 1))
        packed = jnp.where(spot, pltpu.roll(item, (2 * W * x + W) % LANES, 1), packed)
    return packed


def lane_unpack(packed, x):
    lane = lane_iota(packed.shape[0])
    moved = pltpu.roll(packed, (2 * LANES - (2 * W * x + W)) % LANES, 1)
    return jnp.where((lane < W) | (lane >= LANES - W), moved, 0.0)


def edges(place):
    j, g, ny, nz, rows = place[0], place[1], place[2], place[3], place[4]
    return (j > 0, (j + 1) * rows < ny), (g > 0, (g + 1) * LANES < nz)


def y_part(f0, f1, rl, rr, h0, h1, ylo, yhi, near):
    X, Y, _ = f0.shape
    for number, h in enumerate((h0, h1)):
        part = slice(W * number, W * (number + 1))
        left = jnp.where(near[0], rl[part, :], 0.0)
        right = jnp.where(near[1], rr[part, :], 0.0)
        rows = jnp.concatenate([left, right], 0).T
        wide = jnp.concatenate([rows, jnp.zeros((X * Y, LANES - 2 * W), jnp.float32)], 1)
        h[...] = pltpu.roll(wide, LANES - W, 1).reshape(X, Y, LANES)
    for out, part in ((ylo, slice(0, W)), (yhi, slice(Y - W, Y))):
        out[0:X] = jnp.concatenate([f0[:, part, :], f1[:, part, :]], 1)
        out[X] = lane_pack([jnp.concatenate([h0[x, part], h1[x, part]], 0) for x in range(X)])


def x_sides(ryl, ryr, ym0, ym1, yh0, yh1, near):
    X = ym0.shape[0]
    for number, (ym, yh) in enumerate(((ym0, yh0), (ym1, yh1))):
        part = slice(W * number, W * (number + 1))
        right = jnp.where(near[1], ryr[:, part], 0.0)
        left = jnp.where(near[0], ryl[:, part], 0.0)
        both = jnp.concatenate([right, left], 1)
        ym[...] = both[0:X]
        for x in range(X):
            yh[x] = lane_unpack(both[X], x)


def x_face(f0, f1, h0, h1, ym0, ym1, yh0, yh1, start, out):
    Y = f0.shape[1]
    for number, (f, h, ym, yh) in enumerate(((f0, h0, ym0, yh0), (f1, h1, ym1, yh1))):
        base = (W + 1) * number
        for x in range(W):
            out[base + x, 0:Y] = f[start + x]
            out[base + x, Y:] = ym[start + x]
        out[base + W, 0:Y] = lane_pack([h[start + x] for x in range(W)])
        out[base + W, Y:] = lane_pack([yh[start + x] for x in range(W)])


def y_body(groups, place, *refs):
    fields, rest = refs[: 2 * groups], refs[2 * groups :]
    rl, rr, halos, ylo, yhi = rest[0], rest[1], rest[2:-2], rest[-2], rest[-1]
    near = edges(place)[1]
    col = row = 0
    for k in range(groups):
        f0, f1 = fields[2 * k : 2 * k + 2]
        X, Y, _ = f0.shape
        cols, rows = pl.ds(col, X * Y), pl.ds(row, X + 1)
        y_part(
            f0, f1, rl.at[:, cols], rr.at[:, cols], halos[2 * k], halos[2 * k + 1],
            ylo.at[rows], yhi.at[rows], near,
        )
        col, row = col + X * Y, row + X + 1


def heart_x_body(place, f0, f1, h0, h1, ryl, ryr, ym0, ym1, yh0, yh1, high):
    X = f0.shape[0]
    rows = pl.ds(0, X + 1)
    sides = (ym0, ym1, yh0, yh1)
    x_sides(ryl.at[rows], ryr.at[rows], *sides, edges(place)[0])
    x_face(f0, f1, h0, h1, *sides, X - W, high)


def torso_x_body(
    place, a0, a1, g0, g1, b0, b1, k0, k1, f0, f1, h0, h1, ryl, ryr, ym0, ym1, yh0, yh1, high, low
):
    HX, HY, _ = a0.shape
    X, Y, _ = f0.shape
    rows = pl.ds(HX + 1, X + 1)
    sides = (ym0, ym1, yh0, yh1)
    x_sides(ryl.at[rows], ryr.at[rows], *sides, edges(place)[0])
    x_face(f0, f1, h0, h1, *sides, X - W, high)
    x_face(a0, a1, g0, g1, b0, b1, k0, k1, 0, low.at[:, pl.ds(0, HY + 2 * W)])
    x_face(f0, f1, h0, h1, *sides, 0, low.at[:, pl.ds(HY + 2 * W, Y + 2 * W)])


def right_x_body(place, f0, f1, h0, h1, ryl, ryr, ym0, ym1, yh0, yh1, low):
    sides = (ym0, ym1, yh0, yh1)
    x_sides(ryl, ryr, *sides, edges(place)[0])
    x_face(f0, f1, h0, h1, *sides, 0, low)


def from_next(value, axis):
    count = lax.axis_size(axis)
    return lax.ppermute(value, axis, [((i + 1) % count, i) for i in range(count)])


def from_last(value, axis):
    count = lax.axis_size(axis)
    return lax.ppermute(value, axis, [(i, (i + 1) % count) for i in range(count)])


def two_stages(place, groups, zlo, zhi, name, after=()):
    count = len(groups)
    fields = [f for group in groups for f in group]
    rr, rl = from_next(zlo, "grp"), from_last(zhi, "grp")
    tall = f32(sum(group[0].shape[0] + 1 for group in groups), 2 * W, LANES)
    *halos, ylo, yhi = call(
        functools.partial(y_body, count),
        tuple(f32(*f.shape) for f in fields) + (tall, tall),
        name, 3 + len(fields), smem=(0,), after=after,
    )(place, *fields, rl, rr)
    return halos, from_last(yhi, "gy"), from_next(ylo, "gy")


def sides_of(X):
    return (f32(X, 2 * W, LANES),) * 4


def face_of(rows):
    return f32(2 * (W + 1), rows + 2 * W, LANES)


def assemble(M, H, number, f, h, ym, yh, rxl, rxr):
    X, Y, _ = f.shape
    base = (W + 1) * number
    M[0:X, 0:Y] = f[...]
    M[0:X, Y:] = ym[...]
    H[0:X, 0:Y] = h[...]
    H[0:X, Y:] = yh[...]
    top = M.shape[0] - 2 * W
    for start, source in ((top, rxr), (top + W, rxl)):
        if source is None:
            continue
        M[start : start + W] = source[base : base + W]
        for x in range(W):
            H[start + x] = lane_unpack(source[base + W], x)


def y_next(v):
    return pltpu.roll(v, v.shape[0] - 1, 0)


def y_last(v):
    return pltpu.roll(v, 1, 0)


def z_next(m, h):
    end = lane_iota(m.shape[0]) == LANES - 1
    rm, rh = pltpu.roll(m, LANES - 1, 1), pltpu.roll(h, LANES - 1, 1)
    return jnp.where(end, rh, rm), jnp.where(end, rm, rh)


def z_last(m, h):
    end = lane_iota(m.shape[0]) == 0
    rm, rh = pltpu.roll(m, 1, 1), pltpu.roll(h, 1, 1)
    return jnp.where(end, rh, rm), jnp.where(end, rm, rh)


def wrapped(x, count):
    return jnp.where(x >= count, x - count, jnp.where(x < 0, x + count, x))


def around(M, H, x, count):
    xn, xl = wrapped(x + 1, count), wrapped(x - 1, count)
    m, h = M[x], H[x]
    zn, zl = z_next(m, h), z_last(m, h)
    sm = M[xn] + M[xl] + y_next(m) + y_last(m) + zn[0] + zl[0]
    sh = H[xn] + H[xl] + y_next(h) + y_last(h) + zn[1] + zl[1]
    return m, h, sm, sh


def gather_rows(table, index, store):
    rows_n = table.shape[0]

    def tile(i, carry):
        top = pl.multiple_of(i * 8, 8)
        for j in range(index.shape[1] // LANES):
            spot = (pl.ds(top, 8), slice(j * LANES, (j + 1) * LANES))
            where = index[spot[0], spot[1]]
            cols, rows = where & (LANES - 1), where >> 7
            total = jnp.zeros((8, LANES), jnp.float32)
            for r in range(rows_n):
                line = jnp.broadcast_to(table[r : r + 1, :], (8, LANES))
                got = jnp.take_along_axis(line, cols, axis=1, mode="promise_in_bounds")
                total = jnp.where(rows == r, got, total)
            store(spot, where, total)
        return carry

    lax.fori_loop(0, index.shape[0] // 8, tile, 0)


def scatter_rows(values, index, rows_n, total, unroll):
    cap = index.shape[1]
    total[...] = jnp.zeros_like(total)

    def hot(count, key, weight):
        same = lax.broadcasted_iota(jnp.int32, (count, cap), 0) == key
        return jnp.where(same, weight, 0.0).astype(jnp.bfloat16)

    def one(s):
        where = index[pl.ds(s, 1), :]
        rows, cols = where >> 7, where & (LANES - 1)
        if values is None:
            left = hot(rows_n, rows, 1.0)
        else:
            value = values[pl.ds(s, 1), :]
            high = value.astype(jnp.bfloat16).astype(jnp.float32)
            left = jnp.concatenate([hot(rows_n, rows, high), hot(rows_n, rows, value - high)], 0)
        return lax.dot_general(
            left, hot(LANES, cols, 1.0), (((1,), (1,)), ((), ())), preferred_element_type=jnp.float32
        )

    def step(i, carry):
        part = one(i * unroll)
        for u in range(1, unroll):
            part = part + one(i * unroll + u)
        total[...] += part
        return carry

    lax.fori_loop(0, index.shape[0] // unroll, step, 0)


def start_body(
    table, hm, hp, hphi, hscale, hlabels, cond, zlo, zhi, m, p, phi, scale, labels, sems
):
    X, Y, _ = m.shape
    TX, TY, _ = phi.shape
    copies = [
        pltpu.make_async_copy(source, target, sems.at[k])
        for k, (source, target) in enumerate(
            ((hm, m), (hp, p), (hphi, phi), (hscale, scale), (hlabels, labels))
        )
    ]
    for copy in copies:
        copy.start()
    cols, more = pl.ds(0, X * Y), pl.ds(X * Y, TX * TY)
    copies[0].wait()
    copies[1].wait()
    z_faces(
        [m[...].reshape(X * Y, LANES), p[...].reshape(X * Y, LANES)], zlo.at[:, cols], zhi.at[:, cols]
    )
    for copy in copies[2:]:
        copy.wait()
    picked = jnp.zeros(labels.shape, jnp.float32)
    for number in range(LABELS):
        picked = jnp.where(labels[...] == number, table[number], picked)
    value = scale[...] * picked
    cond[...] = value
    z_faces(
        [phi[...].reshape(TX * TY, LANES), value.reshape(TX * TY, LANES)], zlo.at[:, more], zhi.at[:, more]
    )


def weight_body(index, weight, total):
    scatter_rows(None, index, total.shape[0], total, 8)
    weight[...] = (penalty * total[...]).reshape(weight.shape)


def heart_tiles(place, Y):
    j, g = place[0], place[1]
    row = lax.broadcasted_iota(jnp.int32, (Y + 2 * W, LANES), 0)
    lane = lane_iota(Y + 2 * W)
    yg = j * Y + jnp.where(row >= Y + W, row - Y - 2 * W, row)
    tiles = []
    for zl in (lane, jnp.where(lane >= LANES // 2, lane - LANES, lane + LANES)):
        zg = g * LANES + zl
        ny, nz = place[2], place[3]
        one = lambda cond: cond.astype(jnp.float32)
        inside = one((yg >= 0) & (yg < ny) & (zg >= 0) & (zg < nz))
        diag = 2.0 + one(yg + 1 < ny) + one(yg - 1 >= 0) + one(zg + 1 < nz) + one(zg - 1 >= 0)
        tiles.append((diag, inside / diag, inside))
    return tiles


def heart_surface_body(
    place, m, p, hm, hp, ymm, ymp, yhm, yhp, rxl, index,
    sent, table, mM, mH, uM, uH, wM, wH, vM, vH, fM, fH,
):
    X, Y, _ = m.shape
    S = X // 4
    for number, (M, H, f, h, ym, yh) in enumerate(
        ((mM, mH, m, hm, ymm, yhm), (uM, uH, p, hp, ymp, yhp))
    ):
        base = (W + 1) * number
        M[0:W] = rxl[base : base + W]
        for x in range(W):
            H[x] = lane_unpack(rxl[base + W], x)
        M[W:, 0:Y] = f[0 : 2 * W]
        M[W:, Y:] = ym[0 : 2 * W]
        H[W:, 0:Y] = h[0 : 2 * W]
        H[W:, Y:] = yh[0 : 2 * W]
    count = 3 * W
    (_, qm, im), (_, qh, ih) = heart_tiles(place, Y)
    ratio = intra_cond / (intra_cond + extra_cond)
    old, new = (uM, uH), (wM, wH)
    for number, (carry_coef, resid_coef) in enumerate(cheb_coeffs(SWEEPS_H)):
        reach = SWEEPS_H - 1 - number
        for x in range(W - reach, W + S + reach):
            a, b, sa, sb = around(old[0], old[1], x, count)
            if number == 0:
                c, d, sc, sd = around(mM, mH, x, count)
                fa, fb = -ratio * (c * im - sc * qm), -ratio * (d * ih - sd * qh)
                fM[x], fH[x] = fa, fb
            else:
                fa, fb = fM[x], fH[x]
            va = resid_coef * (fa + sa * qm - a)
            vb = resid_coef * (fb + sb * qh - b)
            if number > 0:
                va, vb = carry_coef * vM[x] + va, carry_coef * vH[x] + vb
            if number < SWEEPS_H - 1:
                vM[x], vH[x] = va, vb
                new[0][x], new[1][x] = a + va, b + vb
            else:
                table[(x - W) * Y : (x - W + 1) * Y, :] = (a + va)[0:Y]
        old, new = new, old

    def store(spot, where, value):
        sent[spot[0], spot[1]] = value

    gather_rows(table, index, store)


def heart_body(
    place, m, p, hm, hp, ymm, ymp, yhm, yhp, rxl, rxr,
    phi_out, base_out, mM, mH, uM, uH, wM, wH, vM, vH, fM, fH,
):
    X, Y, _ = m.shape
    count = X + 2 * W
    near = pl.ds(0, Y + 2 * W)
    assemble(mM, mH, 0, m, hm, ymm, yhm, rxl, rxr.at[:, near])
    assemble(uM, uH, 1, p, hp, ymp, yhp, rxl, rxr.at[:, near])
    (dm, qm, im), (_, qh, ih) = heart_tiles(place, Y)
    ratio = intra_cond / (intra_cond + extra_cond)
    old, new = (uM, uH), (wM, wH)
    for number, (carry_coef, resid_coef) in enumerate(cheb_coeffs(SWEEPS_H)):

        def sweep(x, old=old, new=new, cc=carry_coef, rc=resid_coef, number=number):
            x = wrapped(x, count)
            a, b, sa, sb = around(old[0], old[1], x, count)
            if number == 0:
                c, d, sc, sd = around(mM, mH, x, count)
                fa, fb = -ratio * (c * im - sc * qm), -ratio * (d * ih - sd * qh)
                fM[x], fH[x] = fa, fb
            else:
                fa, fb = fM[x], fH[x]
            va = rc * (fa + sa * qm - a)
            vb = rc * (fb + sb * qh - b)
            if number > 0:
                va, vb = cc * vM[x] + va, cc * vH[x] + vb
            vM[x], vH[x] = va, vb
            new[0][x], new[1][x] = a + va, b + vb

        reach = SWEEPS_H - number
        loop(-reach, X - 1 + reach, sweep)
        old, new = new, old
    phi_out[...] = old[0][0:X, 0:Y]

    def finish(x):
        a, _, sa, _ = around(mM, mH, x, count)
        c, _, sc, _ = around(old[0], old[1], x, count)
        lap = dm * (a + c) - (sa + sc)
        base_out[x] = (a - time_step * intra_cond * lap)[0:Y]

    loop(0, X - 1, finish)


def right_body(arrived, index, weight, right, zlo, zhi, total):
    rows = index_rows = weight.shape[0] * weight.shape[1]
    scatter_rows(arrived, index, rows, total, 8)
    value = penalty * (total[0:rows] + total[rows : 2 * rows])
    right[...] = value.reshape(right.shape)
    z_faces([value, weight[...].reshape(index_rows, LANES)], zlo, zhi)


def faces_body(
    p, c, hp, hc, ymp, ymc, yhp, yhc, rxl, rxr,
    uM, uH, fxM, fxH, fyM, fyH, fzM, fzH, dM, dH, cM, cH,
):
    X, Y, _ = p.shape
    count = X + 2 * W
    far = pl.ds(rxr.shape[1] - Y - 2 * W, Y + 2 * W)
    assemble(uM, uH, 0, p, hp, ymp, yhp, rxl, rxr.at[:, far])
    assemble(cM, cH, 1, c, hc, ymc, yhc, rxl, rxr.at[:, far])

    def harmonic(a, b):
        total = a + b
        return jnp.where(total > 0.0, 2.0 * a * b / jnp.where(total > 0.0, total, 1.0), 0.0)

    def prepare(x):
        xn = wrapped(x + 1, count)
        a, b = cM[x], cH[x]
        za, zb = z_next(a, b)
        fxM[x], fxH[x] = harmonic(a, cM[xn]), harmonic(b, cH[xn])
        fyM[x], fyH[x] = harmonic(a, y_next(a)), harmonic(b, y_next(b))
        fzM[x], fzH[x] = harmonic(a, za), harmonic(b, zb)

    loop(0, count - 1, prepare)

    def total(x):
        xl = wrapped(x - 1, count)
        za, zb = z_last(fzM[x], fzH[x])
        dM[x] = fxM[x] + fxM[xl] + fyM[x] + y_last(fyM[x]) + fzM[x] + za
        dH[x] = fxH[x] + fxH[xl] + fyH[x] + y_last(fyH[x]) + fzH[x] + zb

    loop(0, count - 1, total)


def reciprocal(value):
    return jnp.where(value > 0.0, 1.0 / jnp.where(value > 0.0, value, 1.0), 0.0)


def flow(m, h, nM, nH, lM, lH, fxM, fxH, gxM, gxH, fy, gy, fz, gz):
    zn = z_next(m, h)
    zl = z_last(fz * m, gz * h)
    sm = fxM * nM + gxM * lM + fy * y_next(m) + y_last(fy * m)
    sh = fxH * nH + gxH * lH + gy * y_next(h) + y_last(gy * h)
    return sm + fz * zn[0] + zl[0], sh + gz * zn[1] + zl[1]


def torso_surface_body(
    right, weight, hr, hw, ymr, ymw, yhr, yhw, arrived, index,
    uM, uH, fxM, fxH, fyM, fyH, fzM, fzH, dM, dH,
    surface, returned, aM, aH, bM, bH, vM, vH, iM, iH,
):
    S, Y, _ = right.shape
    count = uM.shape[0]
    old, new = None, (aM, aH)
    for number, (carry_coef, resid_coef) in enumerate(cheb_coeffs(SWEEPS_T)):
        reach = SWEEPS_T - 1 - number

        def value(x, tile, old=old):
            return (uM, uH)[tile][x % count] if old is None else old[tile][x + W]

        for x in range(-reach, S + reach):
            at, last = x % count, (x - 1) % count
            m, h = value(x, 0), value(x, 1)
            sm, sh = flow(
                m, h, value(x + 1, 0), value(x + 1, 1), value(x - 1, 0), value(x - 1, 1),
                fxM[at], fxH[at], fxM[last], fxH[last], fyM[at], fyH[at], fzM[at], fzH[at],
            )
            inside = 0 <= x < S
            if number == 0:
                wm, wh = dM[at], dH[at]
                if inside:
                    wm = wm + jnp.concatenate([weight[x], ymw[x]], 0)
                    wh = wh + jnp.concatenate([hw[x], yhw[x]], 0)
                wm, wh = reciprocal(wm), reciprocal(wh)
                iM[x + W], iH[x + W] = wm, wh
            else:
                wm, wh = iM[x + W], iH[x + W]
            if inside:
                sm = sm + jnp.concatenate([right[x], ymr[x]], 0)
                sh = sh + jnp.concatenate([hr[x], yhr[x]], 0)
            va, vb = resid_coef * (sm * wm - m), resid_coef * (sh * wh - h)
            if number > 0:
                va, vb = carry_coef * vM[x + W] + va, carry_coef * vH[x + W] + vb
            if number < SWEEPS_T - 1:
                vM[x + W], vH[x + W] = va, vb
                new[0][x + W], new[1][x + W] = m + va, h + vb
            else:
                surface[x] = (m + va)[0:Y]
        old, new = new, ((bM, bH) if number == 0 else old)
    table = surface[...].reshape(S * Y, LANES)

    def store(spot, where, value):
        returned[spot[0], spot[1]] = jnp.where(
            where >= 0, penalty * (arrived[spot[0], spot[1]] - value), 0.0
        )

    gather_rows(table, index, store)


def torso_body(
    surface, right, weight, hr, hw, ymr, ymw, yhr, yhw, rxr,
    uM, uH, fxM, fxH, fyM, fyH, fzM, fzH, dM, dH,
    torso_out, aM, aH, bM, bH, vM, vH, rM, rH, iM, iH,
):
    X, Y = torso_out.shape[0], torso_out.shape[1]
    S = right.shape[0]
    for ref in (rM, rH, iM, iH):
        ref[S:X] = jnp.zeros((X - S,) + ref.shape[1:], jnp.float32)
    assemble(rM, rH, 0, right, hr, ymr, yhr, None, rxr)
    assemble(iM, iH, 1, weight, hw, ymw, yhw, None, rxr)

    old, new = (uM, uH), (aM, aH)
    for number, (carry_coef, resid_coef) in enumerate(cheb_coeffs(SWEEPS_T)):

        def sweep(x, old=old, new=new, cc=carry_coef, rc=resid_coef, number=number):
            xn, xl = x + 1, x - 1
            m, h = old[0][x], old[1][x]
            if number == 0:
                iM[x], iH[x] = reciprocal(dM[x] + iM[x]), reciprocal(dH[x] + iH[x])
            sm, sh = flow(
                m, h, old[0][xn], old[1][xn], old[0][xl], old[1][xl],
                fxM[x], fxH[x], fxM[xl], fxH[xl], fyM[x], fyH[x], fzM[x], fzH[x],
            )
            va = rc * ((rM[x] + sm) * iM[x] - m)
            vb = rc * ((rH[x] + sh) * iH[x] - h)
            if number > 0:
                va, vb = cc * vM[x] + va, cc * vH[x] + vb
            vM[x], vH[x] = va, vb
            new[0][x], new[1][x] = m + va, h + vb

        reach = SWEEPS_T - 1 - number
        loop(S - reach, X - 1 + reach, sweep)
        old, new = new, ((bM, bH) if number == 0 else old)
    torso_out[0:S] = surface[...]
    torso_out[S:X] = old[0][S:X, 0:Y]


def final_body(place, back, index, phi, out, total):
    X, Y, _ = phi.shape
    rows = X // 4 * Y
    scatter_rows(back, index, rows, total, 8)
    flux = (total[0:rows] + total[rows : 2 * rows]).reshape(X // 4, Y, LANES)
    (dm, _, _), _ = heart_tiles(place, Y)
    out[X // 4 :] = phi[X // 4 :]
    scale = (1.0 / ((intra_cond + extra_cond) * dm))[0:Y]
    for x in range(X // 4):
        out[x] = phi[x] - flux[x] * scale


def ionic_current(states, membrane, ion_params):
    params_col = ion_params[:, :, None, None, None]
    gate_vals = states.astype(jnp.float32)
    voltage = membrane[None]
    steady = jax.nn.sigmoid((voltage - params_col[0]) / params_col[1])
    gate_vals = steady + (gate_vals - steady) * jnp.exp(-time_step * params_col[2])
    return jnp.sum(params_col[3] * gate_vals * (voltage - params_col[4]), axis=0)


def per_device(
    states, membrane, phi_heart, ion_params, torso_phi, tissue_scale, labels, cond_table,
    send_node, send_count, recv_voxel, recv_count,
):
    X, Y, _ = membrane.shape
    TX, TY, _ = torso_phi.shape
    peers = lax.axis_size("gx") * lax.axis_size("gy")
    cap = send_node.shape[-1]
    place = jnp.stack([
        lax.axis_index("gy"), lax.axis_index("grp"),
        jnp.int32(Y * lax.axis_size("gy")), jnp.int32(LANES * lax.axis_size("grp")), jnp.int32(Y),
    ])
    slots = jnp.arange(cap, dtype=jnp.int32)[None, :]
    send_index = jnp.where(slots < send_count.reshape(peers, 1), send_node.reshape(peers, cap), -1)
    recv_index = jnp.where(slots < recv_count.reshape(peers, 1), recv_voxel.reshape(peers, cap), -1)

    S = TX // 4
    wide = f32(2 * W, X * Y + TX * TY)
    hfield, tfield = pltpu.VMEM((X, Y, LANES), jnp.float32), pltpu.VMEM((TX, TY, LANES), jnp.float32)
    cond, zlo, zhi = call(
        start_body, (f32(TX, TY, LANES), wide, wide), "start", 6,
        scratch=[
            hfield, hfield, tfield, tfield,
            pltpu.VMEM((TX, TY, LANES), jnp.int32), pltpu.SemaphoreType.DMA((5,)),
        ],
        smem=(0,), hbm=(1, 2, 3, 4, 5),
    )(cond_table, membrane, phi_heart, torso_phi, tissue_scale, labels)
    weight = call(
        weight_body, f32(S, TY, LANES), "weight", 1,
        scratch=[pltpu.VMEM((S * TY, LANES), jnp.float32)], after=(zlo,),
    )(recv_index)

    heart, torso = (membrane, phi_heart), (torso_phi, cond)
    halos, ryl, ryr = two_stages(place, (heart, torso), zlo, zhi, "static_y", after=(weight,))
    *heart_sides, high = call(
        heart_x_body, sides_of(X) + (face_of(Y),), "heart_x", 7, smem=(0,)
    )(place, *heart, *halos[:2], ryl, ryr)
    heart_halo = (*halos[:2], *heart_sides)
    hxl = from_last(high, "gx")
    *torso_sides, high, low = call(
        torso_x_body, sides_of(TX) + (face_of(TY), face_of(Y + 2 * W + TY)), "torso_x", 15,
        smem=(0,), after=(hxl,),
    )(place, *heart, *heart_halo, *torso, *halos[2:], ryl, ryr)
    torso_halo = (*halos[2:], *torso_sides)
    txl, xr = from_last(high, "gx"), from_next(low, "gx")

    thin = pltpu.VMEM((3 * W, Y + 2 * W, LANES), jnp.float32)
    sent = call(
        heart_surface_body, f32(peers, cap), "heart_surface", 11,
        scratch=[pltpu.VMEM((X // 4 * Y, LANES), jnp.float32)] + [thin] * 10, smem=(0,),
    )(place, *heart, *heart_halo, hxl, send_index)
    arrived = lax.all_to_all(sent, ("gx", "gy"), split_axis=0, concat_axis=0, tiled=True)

    text = (TX + 2 * W, TY + 2 * W, LANES)
    big = pltpu.VMEM(text, jnp.float32)
    faces = call(
        faces_body, (f32(*text),) * 10, "faces", 10, scratch=[big] * 2, after=(sent,)
    )(*torso, *torso_halo, txl, xr)

    right, rzlo, rzhi = call(
        right_body,
        (f32(S, TY, LANES), f32(2 * W, S * TY), f32(2 * W, S * TY)),
        "right", 3, scratch=[pltpu.VMEM((2 * S * TY, LANES), jnp.float32)], after=(faces[0],),
    )(arrived, recv_index, weight)
    ext = pltpu.VMEM((X + 2 * W, Y + 2 * W, LANES), jnp.float32)
    phi_new, base = call(
        heart_body, (f32(X, Y, LANES), f32(X, Y, LANES)), "heart", 11,
        scratch=[ext] * 10, smem=(0,), after=(rzlo,),
    )(place, *heart, *heart_halo, hxl, xr)
    halos, ryl, ryr = two_stages(place, ((right, weight),), rzlo, rzhi, "right_y", after=(base,))
    *sides, low = call(
        right_x_body, sides_of(S) + (face_of(TY),), "right_x", 7, smem=(0,)
    )(place, right, weight, *halos, ryl, ryr)
    rxr = from_next(low, "gx")
    flat = pltpu.VMEM((3 * W, TY + 2 * W, LANES), jnp.float32)
    surface, returned = call(
        torso_surface_body, (f32(S, TY, LANES), f32(peers, cap)), "torso_surface", 20,
        scratch=[flat] * 8,
    )(right, weight, *halos, *sides, arrived, recv_index, *faces)
    back = lax.all_to_all(returned, ("gx", "gy"), split_axis=0, concat_axis=0, tiled=True)
    torso_out = call(
        torso_body, f32(TX, TY, LANES), "torso", 20, scratch=[big] * 10,
    )(surface, right, weight, *halos, *sides, rxr, *faces)
    current = ionic_current(states, membrane, ion_params)
    new_membrane = base - time_step * current
    heart_phi = call(
        final_body, f32(X, Y, LANES), "final", 4,
        scratch=[pltpu.VMEM((2 * X // 4 * Y, LANES), jnp.float32)], smem=(0,),
    )(place, back, send_index, phi_new)
    return (new_membrane, heart_phi, torso_out)


def solution(mesh):
    placed = (
        P(None, "gx", "gy", "grp"),
        P("gx", "gy", "grp"),
        P("gx", "gy", "grp"),
        P(),
        P("gx", "gy", "grp"),
        P("gx", "gy", "grp"),
        P("gx", "gy", "grp"),
        P(),
        P("grp", "gx", "gy", None, None),
        P("grp", "gx", "gy", None),
        P("grp", "gx", "gy", None, None),
        P("grp", "gx", "gy", None),
    )
    return jax.shard_map(
        per_device,
        mesh=mesh,
        in_specs=placed,
        out_specs=(P("gx", "gy", "grp"), P("gx", "gy", "grp"), P("gx", "gy", "grp")),
        check_vma=False,
    )
```

```python
import functools

import jax
import jax.numpy as jnp
from jax import lax
from jax.experimental import pallas as pl
from jax.experimental.pallas import tpu as pltpu
from jax.sharding import PartitionSpec as P


LABELS = 4
SWEEPS_H = 3
SWEEPS_T = 4
W = 4
LANES = 128

time_step = 0.1
intra_cond = 0.25
extra_cond = 0.5
penalty = 2.0
cheb_low = 0.1
cheb_high = 2.0
VMEM_LIMIT = 24 << 20
VMEM_WHOLE = 60 * 1024 * 1024


def cheb_coeffs(sweeps):
    centre = 0.5 * (cheb_high + cheb_low)
    half_width = 0.5 * (cheb_high - cheb_low)
    scaled = centre / half_width
    coeffs = [(0.0, 1.0 / centre)]
    rho_old = 1.0 / scaled
    for _ in range(1, sweeps):
        rho_new = 1.0 / (2.0 * scaled - rho_old)
        coeffs.append((rho_new * rho_old, 2.0 * rho_new / half_width))
        rho_old = rho_new
    return coeffs


def f32(*shape):
    return jax.ShapeDtypeStruct(shape, jnp.float32)


def call(body, outs, n_in, scratch=(), smem=(), after=(), whole=False):
    spaces = [pltpu.SMEM if i in smem else pltpu.VMEM for i in range(n_in)] + [pl.ANY] * len(after)

    def run(*refs):
        body(*refs[:n_in], *refs[n_in + len(after) :])

    made = pl.pallas_call(
        run,
        out_shape=outs,
        in_specs=[pl.BlockSpec(memory_space=space) for space in spaces],
        out_specs=jax.tree.map(lambda _: pl.BlockSpec(memory_space=pltpu.VMEM), outs),
        scratch_shapes=list(scratch),
        compiler_params=pltpu.CompilerParams(vmem_limit_bytes=VMEM_WHOLE if whole else VMEM_LIMIT),
    )

    def placed(*args):
        return made(*args, *after)

    return placed


def loop(first, last, body, unroll=2):
    def step(i, carry):
        for u in range(unroll):
            body(i * unroll + u + first)
        return carry

    lax.fori_loop(0, (last - first + 1) // unroll, step, 0)


def lane_iota(rows):
    return lax.broadcasted_iota(jnp.int32, (rows, LANES), 1)


def z_faces(values, zlo, zhi):
    for number, value in enumerate(values):
        turned = value.T
        zlo[W * number : W * (number + 1), :] = turned[:W]
        zhi[W * number : W * (number + 1), :] = turned[LANES - W :]


def lane_pack(slices):
    rows = slices[0].shape[0]
    lane = lane_iota(rows)
    packed = jnp.zeros((rows, LANES), jnp.float32)
    for x, item in enumerate(slices):
        spot = (lane >= 2 * W * x) & (lane < 2 * W * (x + 1))
        packed = jnp.where(spot, pltpu.roll(item, (2 * W * x + W) % LANES, 1), packed)
    return packed


def lane_unpack(packed, x):
    lane = lane_iota(packed.shape[0])
    moved = pltpu.roll(packed, (2 * LANES - (2 * W * x + W)) % LANES, 1)
    return jnp.where((lane < W) | (lane >= LANES - W), moved, 0.0)


def edges(place):
    j, g, ny, nz, rows = place[0], place[1], place[2], place[3], place[4]
    return (j > 0, (j + 1) * rows < ny), (g > 0, (g + 1) * LANES < nz)


def y_part(f0, f1, rl, rr, h0, h1, ylo, yhi, near):
    X, Y, _ = f0.shape
    for number, h in enumerate((h0, h1)):
        part = slice(W * number, W * (number + 1))
        left = jnp.where(near[0], rl[part, :], 0.0)
        right = jnp.where(near[1], rr[part, :], 0.0)
        rows = jnp.concatenate([left, right], 0).T
        wide = jnp.concatenate([rows, jnp.zeros((X * Y, LANES - 2 * W), jnp.float32)], 1)
        h[...] = pltpu.roll(wide, LANES - W, 1).reshape(X, Y, LANES)
    for out, part in ((ylo, slice(0, W)), (yhi, slice(Y - W, Y))):
        out[0:X] = jnp.concatenate([f0[:, part, :], f1[:, part, :]], 1)
        out[X] = lane_pack([jnp.concatenate([h0[x, part], h1[x, part]], 0) for x in range(X)])


def fill(E, f0, f1, h0, h1, ryl, ryr, near):
    X, Y, _ = f0.shape
    for number, (f, h) in enumerate(((f0, h0), (f1, h1))):
        part = slice(W * number, W * (number + 1))
        right = jnp.where(near[1], ryr[:, part], 0.0)
        left = jnp.where(near[0], ryl[:, part], 0.0)
        both = jnp.concatenate([right, left], 1)
        E[2 * number, :, 0:Y] = f[...]
        E[2 * number, :, Y:] = both[0:X]
        E[2 * number + 1, :, 0:Y] = h[...]
        for x in range(X):
            E[2 * number + 1, x, Y:] = lane_unpack(both[X], x)


def x_face(E, start, out):
    for number in range(2):
        base = (W + 1) * number
        out[base : base + W] = E[2 * number, start : start + W]
        out[base + W] = lane_pack([E[2 * number + 1, start + x] for x in range(W)])


def y_body(groups, place, *refs):
    fields, rest = refs[: 2 * groups], refs[2 * groups :]
    rl, rr, halos, ylo, yhi = rest[0], rest[1], rest[2:-2], rest[-2], rest[-1]
    near = edges(place)[1]
    col = row = 0
    for k in range(groups):
        f0, f1 = fields[2 * k : 2 * k + 2]
        X, Y, _ = f0.shape
        cols, rows = pl.ds(col, X * Y), pl.ds(row, X + 1)
        y_part(
            f0, f1, rl.at[:, cols], rr.at[:, cols], halos[2 * k], halos[2 * k + 1],
            ylo.at[rows], yhi.at[rows], near,
        )
        col, row = col + X * Y, row + X + 1


def heart_x_body(place, f0, f1, h0, h1, ryl, ryr, E, high):
    X = f0.shape[0]
    rows = pl.ds(0, X + 1)
    fill(E, f0, f1, h0, h1, ryl.at[rows], ryr.at[rows], edges(place)[0])
    x_face(E, X - W, high)


def torso_x_body(place, heart, f0, f1, h0, h1, ryl, ryr, E, high, low):
    X = f0.shape[0]
    rows = pl.ds(heart.shape[1] + 1, X + 1)
    fill(E, f0, f1, h0, h1, ryl.at[rows], ryr.at[rows], edges(place)[0])
    x_face(E, X - W, high)
    x_face(heart, 0, low.at[:, pl.ds(0, heart.shape[2])])
    x_face(E, 0, low.at[:, pl.ds(heart.shape[2], E.shape[2])])


def right_x_body(place, f0, f1, h0, h1, ryl, ryr, E, low):
    fill(E, f0, f1, h0, h1, ryl, ryr, edges(place)[0])
    x_face(E, 0, low)


def from_next(value, axis):
    count = lax.axis_size(axis)
    return lax.ppermute(value, axis, [((i + 1) % count, i) for i in range(count)])


def from_last(value, axis):
    count = lax.axis_size(axis)
    return lax.ppermute(value, axis, [(i, (i + 1) % count) for i in range(count)])


def swap(value):
    return lax.all_to_all(value, ("gx", "gy"), split_axis=0, concat_axis=0, tiled=True)


def two_stages(place, groups, zlo, zhi):
    count = len(groups)
    fields = [f for group in groups for f in group]
    rr, rl = from_next(zlo, "grp"), from_last(zhi, "grp")
    tall = f32(sum(group[0].shape[0] + 1 for group in groups), 2 * W, LANES)
    *halos, ylo, yhi = call(
        functools.partial(y_body, count),
        tuple(f32(*f.shape) for f in fields) + (tall, tall),
        3 + len(fields), smem=(0,),
    )(place, *fields, rl, rr)
    return halos, from_last(yhi, "gy"), from_next(ylo, "gy")


def wide_of(X, Y):
    return f32(4, X, Y + 2 * W, LANES)


def face_of(rows):
    return f32(2 * (W + 1), rows + 2 * W, LANES)


def assemble(M, H, number, E, rxl, rxr):
    X = E.shape[1]
    base = (W + 1) * number
    M[0:X] = E[2 * number]
    H[0:X] = E[2 * number + 1]
    top = M.shape[0] - 2 * W
    for start, source in ((top, rxr), (top + W, rxl)):
        if source is None:
            continue
        M[start : start + W] = source[base : base + W]
        for x in range(W):
            H[start + x] = lane_unpack(source[base + W], x)


def y_next(v):
    return pltpu.roll(v, v.shape[0] - 1, 0)


def y_last(v):
    return pltpu.roll(v, 1, 0)


def z_next(m, h):
    end = lane_iota(m.shape[0]) == LANES - 1
    rm, rh = pltpu.roll(m, LANES - 1, 1), pltpu.roll(h, LANES - 1, 1)
    return jnp.where(end, rh, rm), jnp.where(end, rm, rh)


def z_last(m, h):
    end = lane_iota(m.shape[0]) == 0
    rm, rh = pltpu.roll(m, 1, 1), pltpu.roll(h, 1, 1)
    return jnp.where(end, rh, rm), jnp.where(end, rm, rh)


def wrapped(x, count):
    return jnp.where(x >= count, x - count, jnp.where(x < 0, x + count, x))


def around(M, H, x, count):
    xn, xl = wrapped(x + 1, count), wrapped(x - 1, count)
    m, h = M[x], H[x]
    zn, zl = z_next(m, h), z_last(m, h)
    sm = M[xn] + M[xl] + y_next(m) + y_last(m) + zn[0] + zl[0]
    sh = H[xn] + H[xl] + y_next(h) + y_last(h) + zn[1] + zl[1]
    return m, h, sm, sh


def gather_rows(table, index, store):
    rows_n = table.shape[0]

    def tile(i, carry):
        top = pl.multiple_of(i * 8, 8)
        for j in range(index.shape[1] // LANES):
            spot = (pl.ds(top, 8), slice(j * LANES, (j + 1) * LANES))
            where = index[spot[0], spot[1]]
            cols, rows = where & (LANES - 1), where >> 7
            total = jnp.zeros((8, LANES), jnp.float32)
            for r in range(rows_n):
                line = jnp.broadcast_to(table[r : r + 1, :], (8, LANES))
                got = jnp.take_along_axis(line, cols, axis=1, mode="promise_in_bounds")
                total = jnp.where(rows == r, got, total)
            store(spot, where, total)
        return carry

    lax.fori_loop(0, index.shape[0] // 8, tile, 0)


def scatter_rows(values, index, rows_n, total, unroll):
    cap = index.shape[1]
    total[...] = jnp.zeros_like(total)

    def hot(count, key, weight):
        same = lax.broadcasted_iota(jnp.int32, (count, cap), 0) == key
        return jnp.where(same, weight, 0.0).astype(jnp.bfloat16)

    def one(s):
        where = index[pl.ds(s, 1), :]
        rows, cols = where >> 7, where & (LANES - 1)
        if values is None:
            left = hot(rows_n, rows, 1.0)
        else:
            value = values[pl.ds(s, 1), :]
            high = value.astype(jnp.bfloat16).astype(jnp.float32)
            left = jnp.concatenate([hot(rows_n, rows, high), hot(rows_n, rows, value - high)], 0)
        return lax.dot_general(
            left, hot(LANES, cols, 1.0), (((1,), (1,)), ((), ())), preferred_element_type=jnp.float32
        )

    def step(i, carry):
        part = one(i * unroll)
        for u in range(1, unroll):
            part = part + one(i * unroll + u)
        total[...] += part
        return carry

    lax.fori_loop(0, index.shape[0] // unroll, step, 0)


def start_body(table, m, p, phi, scale, labels, cond, zlo, zhi):
    X, Y, _ = m.shape
    TX, TY, _ = phi.shape
    cols, more = pl.ds(0, X * Y), pl.ds(X * Y, TX * TY)
    z_faces(
        [m[...].reshape(X * Y, LANES), p[...].reshape(X * Y, LANES)], zlo.at[:, cols], zhi.at[:, cols]
    )
    picked = jnp.zeros(labels.shape, jnp.float32)
    for number in range(LABELS):
        picked = jnp.where(labels[...] == number, table[number], picked)
    value = scale[...] * picked
    cond[...] = value
    z_faces(
        [phi[...].reshape(TX * TY, LANES), value.reshape(TX * TY, LANES)], zlo.at[:, more], zhi.at[:, more]
    )


def weight_body(index, weight, total):
    scatter_rows(None, index, total.shape[0], total, 8)
    weight[...] = (penalty * total[...]).reshape(weight.shape)


def heart_tiles(place, Y):
    j, g = place[0], place[1]
    row = lax.broadcasted_iota(jnp.int32, (Y + 2 * W, LANES), 0)
    lane = lane_iota(Y + 2 * W)
    yg = j * Y + jnp.where(row >= Y + W, row - Y - 2 * W, row)
    tiles = []
    for zl in (lane, jnp.where(lane >= LANES // 2, lane - LANES, lane + LANES)):
        zg = g * LANES + zl
        ny, nz = place[2], place[3]
        one = lambda cond: cond.astype(jnp.float32)
        inside = one((yg >= 0) & (yg < ny) & (zg >= 0) & (zg < nz))
        diag = 2.0 + one(yg + 1 < ny) + one(yg - 1 >= 0) + one(zg + 1 < nz) + one(zg - 1 >= 0)
        tiles.append((diag, inside / diag, inside))
    return tiles


def heart_surface_body(place, E, rxl, index, sent, table, mM, mH, uM, uH, wM, wH, vM, vH, fM, fH):
    S, Y = E.shape[1] // 4, E.shape[2] - 2 * W
    for number, (M, H) in enumerate(((mM, mH), (uM, uH))):
        base = (W + 1) * number
        M[0:W] = rxl[base : base + W]
        for x in range(W):
            H[x] = lane_unpack(rxl[base + W], x)
        M[W:] = E[2 * number, 0 : 2 * W]
        H[W:] = E[2 * number + 1, 0 : 2 * W]
    count = 3 * W
    (_, qm, im), (_, qh, ih) = heart_tiles(place, Y)
    ratio = intra_cond / (intra_cond + extra_cond)
    old, new = (uM, uH), (wM, wH)
    for number, (carry_coef, resid_coef) in enumerate(cheb_coeffs(SWEEPS_H)):
        reach = SWEEPS_H - 1 - number
        for x in range(W - reach, W + S + reach):
            a, b, sa, sb = around(old[0], old[1], x, count)
            if number == 0:
                c, d, sc, sd = around(mM, mH, x, count)
                fa, fb = -ratio * (c * im - sc * qm), -ratio * (d * ih - sd * qh)
                fM[x], fH[x] = fa, fb
            else:
                fa, fb = fM[x], fH[x]
            va = resid_coef * (fa + sa * qm - a)
            vb = resid_coef * (fb + sb * qh - b)
            if number > 0:
                va, vb = carry_coef * vM[x] + va, carry_coef * vH[x] + vb
            if number < SWEEPS_H - 1:
                vM[x], vH[x] = va, vb
                new[0][x], new[1][x] = a + va, b + vb
            else:
                table[(x - W) * Y : (x - W + 1) * Y, :] = (a + va)[0:Y]
        old, new = new, old

    def store(spot, where, value):
        sent[spot[0], spot[1]] = value

    gather_rows(table, index, store)


def heart_body(
    place, current, E, rxl, rxr, phi_out, new_out, mM, mH, uM, uH, wM, wH, vM, vH, fM, fH
):
    X, Y, _ = phi_out.shape
    count = X + 2 * W
    near = pl.ds(0, Y + 2 * W)
    assemble(mM, mH, 0, E, rxl, rxr.at[:, near])
    assemble(uM, uH, 1, E, rxl, rxr.at[:, near])
    (dm, qm, im), (_, qh, ih) = heart_tiles(place, Y)
    ratio = intra_cond / (intra_cond + extra_cond)
    old, new = (uM, uH), (wM, wH)
    for number, (carry_coef, resid_coef) in enumerate(cheb_coeffs(SWEEPS_H)):

        def sweep(x, old=old, new=new, cc=carry_coef, rc=resid_coef, number=number):
            x = wrapped(x, count)
            a, b, sa, sb = around(old[0], old[1], x, count)
            if number == 0:
                c, d, sc, sd = around(mM, mH, x, count)
                fa, fb = -ratio * (c * im - sc * qm), -ratio * (d * ih - sd * qh)
                fM[x], fH[x] = fa, fb
            else:
                fa, fb = fM[x], fH[x]
            va = rc * (fa + sa * qm - a)
            vb = rc * (fb + sb * qh - b)
            if number > 0:
                va, vb = cc * vM[x] + va, cc * vH[x] + vb
            vM[x], vH[x] = va, vb
            new[0][x], new[1][x] = a + va, b + vb

        reach = SWEEPS_H - number
        loop(-reach, X - 1 + reach, sweep)
        old, new = new, old
    phi_out[...] = old[0][0:X, 0:Y]

    def finish(x):
        a, _, sa, _ = around(mM, mH, x, count)
        c, _, sc, _ = around(old[0], old[1], x, count)
        lap = dm * (a + c) - (sa + sc)
        new_out[x] = (a - time_step * intra_cond * lap)[0:Y] - time_step * current[x]

    loop(0, X - 1, finish)


def right_body(arrived, index, weight, right, zlo, zhi, total):
    rows = index_rows = weight.shape[0] * weight.shape[1]
    scatter_rows(arrived, index, rows, total, 8)
    value = penalty * (total[0:rows] + total[rows : 2 * rows])
    right[...] = value.reshape(right.shape)
    z_faces([value, weight[...].reshape(index_rows, LANES)], zlo, zhi)


def faces_body(E, rxl, rxr, F, cM, cH):
    uM, uH, fxM, fxH, fyM, fyH, fzM, fzH, dM, dH = (F.at[k] for k in range(10))
    X, rows = E.shape[1], E.shape[2]
    count = X + 2 * W
    far = pl.ds(rxr.shape[1] - rows, rows)
    assemble(uM, uH, 0, E, rxl, rxr.at[:, far])
    assemble(cM, cH, 1, E, rxl, rxr.at[:, far])

    def harmonic(a, b):
        total = a + b
        return jnp.where(total > 0.0, 2.0 * a * b / jnp.where(total > 0.0, total, 1.0), 0.0)

    def prepare(x):
        xn = wrapped(x + 1, count)
        a, b = cM[x], cH[x]
        za, zb = z_next(a, b)
        fxM[x], fxH[x] = harmonic(a, cM[xn]), harmonic(b, cH[xn])
        fyM[x], fyH[x] = harmonic(a, y_next(a)), harmonic(b, y_next(b))
        fzM[x], fzH[x] = harmonic(a, za), harmonic(b, zb)

    loop(0, count - 1, prepare)

    def total(x):
        xl = wrapped(x - 1, count)
        za, zb = z_last(fzM[x], fzH[x])
        dM[x] = fxM[x] + fxM[xl] + fyM[x] + y_last(fyM[x]) + fzM[x] + za
        dH[x] = fxH[x] + fxH[xl] + fyH[x] + y_last(fyH[x]) + fzH[x] + zb

    loop(0, count - 1, total)


def reciprocal(value):
    return jnp.where(value > 0.0, 1.0 / jnp.where(value > 0.0, value, 1.0), 0.0)


def flow(m, h, nM, nH, lM, lH, fxM, fxH, gxM, gxH, fy, gy, fz, gz):
    zn = z_next(m, h)
    zl = z_last(fz * m, gz * h)
    sm = fxM * nM + gxM * lM + fy * y_next(m) + y_last(fy * m)
    sh = fxH * nH + gxH * lH + gy * y_next(h) + y_last(gy * h)
    return sm + fz * zn[0] + zl[0], sh + gz * zn[1] + zl[1]


def torso_surface_body(
    R, arrived, index, F, surface, returned, aM, aH, bM, bH, vM, vH, iM, iH
):
    uM, uH, fxM, fxH, fyM, fyH, fzM, fzH, dM, dH = (F.at[k] for k in range(10))
    S, Y, _ = surface.shape
    count = F.shape[1]
    old, new = None, (aM, aH)
    for number, (carry_coef, resid_coef) in enumerate(cheb_coeffs(SWEEPS_T)):
        reach = SWEEPS_T - 1 - number

        def value(x, tile, old=old):
            return (uM, uH)[tile][x % count] if old is None else old[tile][x + W]

        for x in range(-reach, S + reach):
            at, last = x % count, (x - 1) % count
            m, h = value(x, 0), value(x, 1)
            sm, sh = flow(
                m, h, value(x + 1, 0), value(x + 1, 1), value(x - 1, 0), value(x - 1, 1),
                fxM[at], fxH[at], fxM[last], fxH[last], fyM[at], fyH[at], fzM[at], fzH[at],
            )
            inside = 0 <= x < S
            if number == 0:
                wm, wh = dM[at], dH[at]
                if inside:
                    wm, wh = wm + R[2, x], wh + R[3, x]
                wm, wh = reciprocal(wm), reciprocal(wh)
                iM[x + W], iH[x + W] = wm, wh
            else:
                wm, wh = iM[x + W], iH[x + W]
            if inside:
                sm, sh = sm + R[0, x], sh + R[1, x]
            va, vb = resid_coef * (sm * wm - m), resid_coef * (sh * wh - h)
            if number > 0:
                va, vb = carry_coef * vM[x + W] + va, carry_coef * vH[x + W] + vb
            if number < SWEEPS_T - 1:
                vM[x + W], vH[x + W] = va, vb
                new[0][x + W], new[1][x + W] = m + va, h + vb
            else:
                surface[x] = (m + va)[0:Y]
        old, new = new, ((bM, bH) if number == 0 else old)
    table = surface[...].reshape(S * Y, LANES)

    def store(spot, where, value):
        returned[spot[0], spot[1]] = jnp.where(
            where >= 0, penalty * (arrived[spot[0], spot[1]] - value), 0.0
        )

    gather_rows(table, index, store)


def torso_body(
    surface, R, rxr, F, torso_out, aM, aH, bM, bH, vM, vH, rM, rH, iM, iH
):
    uM, uH, fxM, fxH, fyM, fyH, fzM, fzH, dM, dH = (F.at[k] for k in range(10))
    X, Y = torso_out.shape[0], torso_out.shape[1]
    S = surface.shape[0]
    for ref in (rM, rH, iM, iH):
        ref[S:X] = jnp.zeros((X - S,) + ref.shape[1:], jnp.float32)
    assemble(rM, rH, 0, R, None, rxr)
    assemble(iM, iH, 1, R, None, rxr)

    old, new = (uM, uH), (aM, aH)
    for number, (carry_coef, resid_coef) in enumerate(cheb_coeffs(SWEEPS_T)):

        def sweep(x, old=old, new=new, cc=carry_coef, rc=resid_coef, number=number):
            xn, xl = x + 1, x - 1
            m, h = old[0][x], old[1][x]
            if number == 0:
                iM[x], iH[x] = reciprocal(dM[x] + iM[x]), reciprocal(dH[x] + iH[x])
            sm, sh = flow(
                m, h, old[0][xn], old[1][xn], old[0][xl], old[1][xl],
                fxM[x], fxH[x], fxM[xl], fxH[xl], fyM[x], fyH[x], fzM[x], fzH[x],
            )
            va = rc * ((rM[x] + sm) * iM[x] - m)
            vb = rc * ((rH[x] + sh) * iH[x] - h)
            if number > 0:
                va, vb = cc * vM[x] + va, cc * vH[x] + vb
            vM[x], vH[x] = va, vb
            new[0][x], new[1][x] = m + va, h + vb

        reach = SWEEPS_T - 1 - number
        loop(S - reach, X - 1 + reach, sweep)
        old, new = new, ((bM, bH) if number == 0 else old)
    torso_out[0:S] = surface[...]
    torso_out[S:X] = old[0][S:X, 0:Y]


def final_body(place, back, index, phi, out, total):
    X, Y, _ = phi.shape
    rows = X // 4 * Y
    scatter_rows(back, index, rows, total, 8)
    flux = (total[0:rows] + total[rows : 2 * rows]).reshape(X // 4, Y, LANES)
    (dm, _, _), _ = heart_tiles(place, Y)
    out[X // 4 :] = phi[X // 4 :]
    scale = (1.0 / ((intra_cond + extra_cond) * dm))[0:Y]
    for x in range(X // 4):
        out[x] = phi[x] - flux[x] * scale


def ionic_current(states, membrane, ion_params):
    params_col = ion_params[:, :, None, None, None]
    gate_vals = states.astype(jnp.float32)
    voltage = membrane[None]
    steady = jax.nn.sigmoid((voltage - params_col[0]) / params_col[1])
    gate_vals = steady + (gate_vals - steady) * jnp.exp(-time_step * params_col[2])
    return jnp.sum(params_col[3] * gate_vals * (voltage - params_col[4]), axis=0)


def per_device(
    states, membrane, phi_heart, ion_params, torso_phi, tissue_scale, labels, cond_table,
    send_node, send_count, recv_voxel, recv_count,
):
    X, Y, _ = membrane.shape
    TX, TY, _ = torso_phi.shape
    peers = lax.axis_size("gx") * lax.axis_size("gy")
    cap = send_node.shape[-1]
    place = jnp.stack([
        lax.axis_index("gy"), lax.axis_index("grp"),
        jnp.int32(Y * lax.axis_size("gy")), jnp.int32(LANES * lax.axis_size("grp")), jnp.int32(Y),
    ])
    slots = jnp.arange(cap, dtype=jnp.int32)[None, :]
    send_index = jnp.where(slots < send_count.reshape(peers, 1), send_node.reshape(peers, cap), -1)
    recv_index = jnp.where(slots < recv_count.reshape(peers, 1), recv_voxel.reshape(peers, cap), -1)

    S = TX // 4
    wide = f32(2 * W, X * Y + TX * TY)
    cond, zlo, zhi = call(
        start_body, (f32(TX, TY, LANES), wide, wide), 6, smem=(0,), whole=True,
    )(cond_table, membrane, phi_heart, torso_phi, tissue_scale, labels)
    weight = call(
        weight_body, f32(S, TY, LANES), 1, scratch=[pltpu.VMEM((S * TY, LANES), jnp.float32)]
    )(recv_index)
    current = ionic_current(states, membrane, ion_params)

    heart, torso = (membrane, phi_heart), (torso_phi, cond)
    halos, ryl, ryr = two_stages(place, (heart, torso), zlo, zhi)
    heart_wide, high = call(
        heart_x_body, (wide_of(X, Y), face_of(Y)), 7, smem=(0,)
    )(place, *heart, *halos[:2], ryl, ryr)
    hxl = from_last(high, "gx")
    torso_wide, high, low = call(
        torso_x_body, (wide_of(TX, TY), face_of(TY), face_of(Y + 2 * W + TY)), 8,
        smem=(0,), after=(hxl,),
    )(place, heart_wide, *torso, *halos[2:], ryl, ryr)
    txl, xr = from_last(high, "gx"), from_next(low, "gx")

    thin = pltpu.VMEM((3 * W, Y + 2 * W, LANES), jnp.float32)
    sent = call(
        heart_surface_body, f32(peers, cap), 4,
        scratch=[pltpu.VMEM((X // 4 * Y, LANES), jnp.float32)] + [thin] * 10, smem=(0,),
    )(place, heart_wide, hxl, send_index)
    arrived = swap(sent)

    ext = pltpu.VMEM((X + 2 * W, Y + 2 * W, LANES), jnp.float32)
    phi_new, new_membrane = call(
        heart_body, (f32(X, Y, LANES), f32(X, Y, LANES)), 5,
        scratch=[ext] * 10, smem=(0,), whole=True,
    )(place, current, heart_wide, hxl, xr)
    right, rzlo, rzhi = call(
        right_body,
        (f32(S, TY, LANES), f32(2 * W, S * TY), f32(2 * W, S * TY)),
        3, scratch=[pltpu.VMEM((2 * S * TY, LANES), jnp.float32)],
    )(arrived, recv_index, weight)
    text = (TX + 2 * W, TY + 2 * W, LANES)
    big = pltpu.VMEM(text, jnp.float32)
    faces = call(faces_body, f32(10, *text), 3, scratch=[big] * 2)(torso_wide, txl, xr)
    halos, ryl, ryr = two_stages(place, ((right, weight),), rzlo, rzhi)
    right_wide, low = call(
        right_x_body, (wide_of(S, TY), face_of(TY)), 7, smem=(0,)
    )(place, right, weight, *halos, ryl, ryr)
    rxr = from_next(low, "gx")
    flat = pltpu.VMEM((3 * W, TY + 2 * W, LANES), jnp.float32)
    surface, returned = call(
        torso_surface_body, (f32(S, TY, LANES), f32(peers, cap)), 4,
        scratch=[flat] * 8,
    )(right_wide, arrived, recv_index, faces)
    back = swap(returned)
    torso_out = call(
        torso_body, f32(TX, TY, LANES), 4, scratch=[big] * 10, whole=True,
    )(surface, right_wide, rxr, faces)
    heart_phi = call(
        final_body, f32(X, Y, LANES), 4,
        scratch=[pltpu.VMEM((2 * X // 4 * Y, LANES), jnp.float32)], smem=(0,),
    )(place, back, send_index, phi_new)
    return (new_membrane, heart_phi, torso_out)


def solution(mesh):
    placed = (
        P(None, "gx", "gy", "grp"),
        P("gx", "gy", "grp"),
        P("gx", "gy", "grp"),
        P(),
        P("gx", "gy", "grp"),
        P("gx", "gy", "grp"),
        P("gx", "gy", "grp"),
        P(),
        P("grp", "gx", "gy", None, None),
        P("grp", "gx", "gy", None),
        P("grp", "gx", "gy", None, None),
        P("grp", "gx", "gy", None),
    )
    return jax.shard_map(
        per_device,
        mesh=mesh,
        in_specs=placed,
        out_specs=(P("gx", "gy", "grp"), P("gx", "gy", "grp"), P("gx", "gy", "grp")),
        check_vma=False,
    )
```

```python
import functools

import jax
import jax.numpy as jnp
from jax import lax
from jax.experimental import pallas as pl
from jax.experimental.pallas import tpu as pltpu
from jax.sharding import PartitionSpec as P


LABELS = 4
SWEEPS_H = 3
SWEEPS_T = 4
W = 4
LANES = 128

time_step = 0.1
intra_cond = 0.25
extra_cond = 0.5
penalty = 2.0
cheb_low = 0.1
cheb_high = 2.0
VMEM_LIMIT = 24 << 20
VMEM_WHOLE = 60 * 1024 * 1024


def cheb_coeffs(sweeps):
    centre = 0.5 * (cheb_high + cheb_low)
    half_width = 0.5 * (cheb_high - cheb_low)
    scaled = centre / half_width
    coeffs = [(0.0, 1.0 / centre)]
    rho_old = 1.0 / scaled
    for _ in range(1, sweeps):
        rho_new = 1.0 / (2.0 * scaled - rho_old)
        coeffs.append((rho_new * rho_old, 2.0 * rho_new / half_width))
        rho_old = rho_new
    return coeffs


def f32(*shape):
    return jax.ShapeDtypeStruct(shape, jnp.float32)


def call(body, outs, n_in, scratch=(), smem=(), left=(), whole=False):
    spaces = [pltpu.SMEM if i in smem else pl.ANY if i in left else pltpu.VMEM for i in range(n_in)]
    return pl.pallas_call(
        body,
        out_shape=outs,
        in_specs=[pl.BlockSpec(memory_space=space) for space in spaces],
        out_specs=jax.tree.map(lambda _: pl.BlockSpec(memory_space=pltpu.VMEM), outs),
        scratch_shapes=list(scratch),
        compiler_params=pltpu.CompilerParams(vmem_limit_bytes=VMEM_WHOLE if whole else VMEM_LIMIT),
    )


def loop(first, last, body, steps=2):
    unroll = (last - first + 1) // steps

    def step(i, carry):
        for u in range(unroll):
            body(i * unroll + u + first)
        return carry

    lax.fori_loop(0, steps, step, 0)


def lane_iota(rows):
    return lax.broadcasted_iota(jnp.int32, (rows, LANES), 1)


def z_faces(values, zlo, zhi):
    for number, value in enumerate(values):
        turned = value.T
        zlo[W * number : W * (number + 1), :] = turned[:W]
        zhi[W * number : W * (number + 1), :] = turned[LANES - W :]


def lane_pack(slices):
    rows = slices[0].shape[0]
    lane = lane_iota(rows)
    packed = jnp.zeros((rows, LANES), jnp.float32)
    for x, item in enumerate(slices):
        spot = (lane >= 2 * W * x) & (lane < 2 * W * (x + 1))
        packed = jnp.where(spot, pltpu.roll(item, (2 * W * x + W) % LANES, 1), packed)
    return packed


def lane_unpack(packed, x):
    lane = lane_iota(packed.shape[0])
    moved = pltpu.roll(packed, (2 * LANES - (2 * W * x + W)) % LANES, 1)
    return jnp.where((lane < W) | (lane >= LANES - W), moved, 0.0)


def edges(place):
    j, g, ny, nz, rows = place[0], place[1], place[2], place[3], place[4]
    return (j > 0, (j + 1) * rows < ny), (g > 0, (g + 1) * LANES < nz)


def y_part(f0, f1, rl, rr, h0, h1, ylo, yhi, near):
    X, Y, _ = f0.shape
    for number, h in enumerate((h0, h1)):
        part = slice(W * number, W * (number + 1))
        left = jnp.where(near[0], rl[part, :], 0.0)
        right = jnp.where(near[1], rr[part, :], 0.0)
        rows = jnp.concatenate([left, right], 0).T
        wide = jnp.concatenate([rows, jnp.zeros((X * Y, LANES - 2 * W), jnp.float32)], 1)
        h[...] = pltpu.roll(wide, LANES - W, 1).reshape(X, Y, LANES)
    for out, part in ((ylo, slice(0, W)), (yhi, slice(Y - W, Y))):
        out[0:X] = jnp.concatenate([f0[:, part, :], f1[:, part, :]], 1)
        out[X] = lane_pack([jnp.concatenate([h0[x, part], h1[x, part]], 0) for x in range(X)])


def fill(E, f0, f1, h0, h1, ryl, ryr, near):
    X, Y, _ = f0.shape
    for number, (f, h) in enumerate(((f0, h0), (f1, h1))):
        part = slice(W * number, W * (number + 1))
        right = jnp.where(near[1], ryr[:, part], 0.0)
        left = jnp.where(near[0], ryl[:, part], 0.0)
        both = jnp.concatenate([right, left], 1)
        E[2 * number, :, 0:Y] = f[...]
        E[2 * number, :, Y:] = both[0:X]
        E[2 * number + 1, :, 0:Y] = h[...]
        for x in range(X):
            E[2 * number + 1, x, Y:] = lane_unpack(both[X], x)


def x_face(E, start, out):
    for number in range(2):
        base = (W + 1) * number
        out[base : base + W] = E[2 * number, start : start + W]
        out[base + W] = lane_pack([E[2 * number + 1, start + x] for x in range(W)])


def y_body(groups, place, *refs):
    fields, rest = refs[: 2 * groups], refs[2 * groups :]
    rl, rr, halos, ylo, yhi = rest[0], rest[1], rest[2:-2], rest[-2], rest[-1]
    near = edges(place)[1]
    col = row = 0
    for k in range(groups):
        f0, f1 = fields[2 * k : 2 * k + 2]
        X, Y, _ = f0.shape
        cols, rows = pl.ds(col, X * Y), pl.ds(row, X + 1)
        y_part(
            f0, f1, rl.at[:, cols], rr.at[:, cols], halos[2 * k], halos[2 * k + 1],
            ylo.at[rows], yhi.at[rows], near,
        )
        col, row = col + X * Y, row + X + 1


def heart_x_body(place, f0, f1, h0, h1, ryl, ryr, E, high):
    X = f0.shape[0]
    rows = pl.ds(0, X + 1)
    fill(E, f0, f1, h0, h1, ryl.at[rows], ryr.at[rows], edges(place)[0])
    x_face(E, X - W, high)


def torso_x_body(place, heart, f0, f1, h0, h1, ryl, ryr, E, high, low):
    X = f0.shape[0]
    rows = pl.ds(heart.shape[1] + 1, X + 1)
    fill(E, f0, f1, h0, h1, ryl.at[rows], ryr.at[rows], edges(place)[0])
    x_face(E, X - W, high)
    x_face(heart, 0, low.at[:, pl.ds(0, heart.shape[2])])
    x_face(E, 0, low.at[:, pl.ds(heart.shape[2], E.shape[2])])


def right_x_body(place, f0, f1, h0, h1, ryl, ryr, E, low):
    fill(E, f0, f1, h0, h1, ryl, ryr, edges(place)[0])
    x_face(E, 0, low)


def from_next(value, axis):
    count = lax.axis_size(axis)
    return lax.ppermute(value, axis, [((i + 1) % count, i) for i in range(count)])


def from_last(value, axis):
    count = lax.axis_size(axis)
    return lax.ppermute(value, axis, [(i, (i + 1) % count) for i in range(count)])


def swap(value):
    return lax.all_to_all(value, ("gx", "gy"), split_axis=0, concat_axis=0, tiled=True)


def two_stages(place, groups, zlo, zhi):
    count = len(groups)
    fields = [f for group in groups for f in group]
    rr, rl = from_next(zlo, "grp"), from_last(zhi, "grp")
    tall = f32(sum(group[0].shape[0] + 1 for group in groups), 2 * W, LANES)
    *halos, ylo, yhi = call(
        functools.partial(y_body, count),
        tuple(f32(*f.shape) for f in fields) + (tall, tall),
        3 + len(fields), smem=(0,),
    )(place, *fields, rl, rr)
    return halos, from_last(yhi, "gy"), from_next(ylo, "gy")


def wide_of(X, Y):
    return f32(4, X, Y + 2 * W, LANES)


def face_of(rows):
    return f32(2 * (W + 1), rows + 2 * W, LANES)


def assemble(M, H, number, E, rxl, rxr):
    X = E.shape[1]
    base = (W + 1) * number
    M[0:X] = E[2 * number]
    H[0:X] = E[2 * number + 1]
    top = M.shape[0] - 2 * W
    for start, source in ((top, rxr), (top + W, rxl)):
        if source is None:
            continue
        M[start : start + W] = source[base : base + W]
        for x in range(W):
            H[start + x] = lane_unpack(source[base + W], x)


def y_next(v):
    return pltpu.roll(v, v.shape[0] - 1, 0)


def y_last(v):
    return pltpu.roll(v, 1, 0)


def z_next(m, h):
    end = lane_iota(m.shape[0]) == LANES - 1
    rm, rh = pltpu.roll(m, LANES - 1, 1), pltpu.roll(h, LANES - 1, 1)
    return jnp.where(end, rh, rm), jnp.where(end, rm, rh)


def z_last(m, h):
    end = lane_iota(m.shape[0]) == 0
    rm, rh = pltpu.roll(m, 1, 1), pltpu.roll(h, 1, 1)
    return jnp.where(end, rh, rm), jnp.where(end, rm, rh)


def wrapped(x, count):
    return jnp.where(x >= count, x - count, jnp.where(x < 0, x + count, x))


def around(M, H, x, count):
    xn, xl = wrapped(x + 1, count), wrapped(x - 1, count)
    m, h = M[x], H[x]
    zn, zl = z_next(m, h), z_last(m, h)
    sm = M[xn] + M[xl] + y_next(m) + y_last(m) + zn[0] + zl[0]
    sh = H[xn] + H[xl] + y_next(h) + y_last(h) + zn[1] + zl[1]
    return m, h, sm, sh


def gather_rows(table, index, out):
    rows_n = table.shape[0]

    def tile(i, carry):
        top = pl.multiple_of(i * 8, 8)
        for j in range(index.shape[1] // LANES):
            spot = (pl.ds(top, 8), slice(j * LANES, (j + 1) * LANES))
            where = index[spot[0], spot[1]]
            cols, rows = where & (LANES - 1), where >> 7
            total = jnp.zeros((8, LANES), jnp.float32)
            for r in range(rows_n):
                line = jnp.broadcast_to(table[r : r + 1, :], (8, LANES))
                got = jnp.take_along_axis(line, cols, axis=1, mode="promise_in_bounds")
                total = jnp.where(rows == r, got, total)
            out[spot[0], 0, spot[1]] = total
        return carry

    lax.fori_loop(0, index.shape[0] // 8, tile, 0)


def scatter_rows(value_of, index, rows_n, total, batch):
    cap = index.shape[1]
    total[...] = jnp.zeros_like(total)
    half = jnp.bfloat16

    def rows_iota(count):
        return lax.broadcasted_iota(jnp.int32, (count, cap), 0).astype(jnp.float32).astype(half)

    row_ids, col_ids = rows_iota(rows_n), rows_iota(LANES)
    ones = jnp.ones((1, cap), half)

    def hot(ids, key, weight):
        key = jnp.broadcast_to(key.astype(jnp.float32).astype(half), ids.shape)
        return jnp.where(ids == key, jnp.broadcast_to(weight, ids.shape), jnp.zeros((), half))

    def one(s):
        where = index[pl.ds(s, 1), :]
        rows, cols = where >> 7, where & (LANES - 1)
        if value_of is None:
            left = hot(row_ids, rows, ones)
        else:
            value = value_of(s)
            high = value.astype(half)
            low = (value - high.astype(jnp.float32)).astype(half)
            left = jnp.concatenate([hot(row_ids, rows, high), hot(row_ids, rows, low)], 0)
        return left, hot(col_ids, cols, ones)

    def step(i, carry):
        part = None
        for b in range(batch):
            sides = [one(i * (8 * batch) + 8 * b + k) for k in range(8)]
            product = lax.dot_general(
                jnp.concatenate([side[0] for side in sides], 1),
                jnp.concatenate([side[1] for side in sides], 1),
                (((1,), (1,)), ((), ())),
                preferred_element_type=jnp.float32,
            )
            part = product if part is None else part + product
        total[...] += part
        return carry

    lax.fori_loop(0, index.shape[0] // (8 * batch), step, 0)


def start_body(table, m, p, phi, scale, labels, cond, zlo, zhi):
    X, Y, _ = m.shape
    TX, TY, _ = phi.shape
    cols, more = pl.ds(0, X * Y), pl.ds(X * Y, TX * TY)
    z_faces(
        [m[...].reshape(X * Y, LANES), p[...].reshape(X * Y, LANES)], zlo.at[:, cols], zhi.at[:, cols]
    )
    picked = jnp.zeros(labels.shape, jnp.float32)
    for number in range(LABELS):
        picked = jnp.where(labels[...] == number, table[number], picked)
    value = scale[...] * picked
    cond[...] = value
    z_faces(
        [phi[...].reshape(TX * TY, LANES), value.reshape(TX * TY, LANES)], zlo.at[:, more], zhi.at[:, more]
    )


def weight_body(index, weight, total):
    scatter_rows(None, index, total.shape[0], total, 2)
    weight[...] = (penalty * total[...]).reshape(weight.shape)


def heart_tiles(place, Y):
    j, g = place[0], place[1]
    row = lax.broadcasted_iota(jnp.int32, (Y + 2 * W, LANES), 0)
    lane = lane_iota(Y + 2 * W)
    yg = j * Y + jnp.where(row >= Y + W, row - Y - 2 * W, row)
    tiles = []
    for zl in (lane, jnp.where(lane >= LANES // 2, lane - LANES, lane + LANES)):
        zg = g * LANES + zl
        ny, nz = place[2], place[3]
        one = lambda cond: cond.astype(jnp.float32)
        inside = one((yg >= 0) & (yg < ny) & (zg >= 0) & (zg < nz))
        diag = 2.0 + one(yg + 1 < ny) + one(yg - 1 >= 0) + one(zg + 1 < nz) + one(zg - 1 >= 0)
        tiles.append((diag, inside / diag, inside))
    return tiles


def heart_surface_body(place, E, rxl, index, sent, table, mM, mH, uM, uH, wM, wH, vM, vH, fM, fH):
    S, Y = E.shape[1] // 4, E.shape[2] - 2 * W
    for number, (M, H) in enumerate(((mM, mH), (uM, uH))):
        base = (W + 1) * number
        M[0:W] = rxl[base : base + W]
        for x in range(W):
            H[x] = lane_unpack(rxl[base + W], x)
        M[W:] = E[2 * number, 0 : 2 * W]
        H[W:] = E[2 * number + 1, 0 : 2 * W]
    count = 3 * W
    (_, qm, im), (_, qh, ih) = heart_tiles(place, Y)
    ratio = intra_cond / (intra_cond + extra_cond)
    old, new = (uM, uH), (wM, wH)
    for number, (carry_coef, resid_coef) in enumerate(cheb_coeffs(SWEEPS_H)):
        reach = SWEEPS_H - 1 - number
        for x in range(W - reach, W + S + reach):
            a, b, sa, sb = around(old[0], old[1], x, count)
            if number == 0:
                c, d, sc, sd = around(mM, mH, x, count)
                fa, fb = -ratio * (c * im - sc * qm), -ratio * (d * ih - sd * qh)
                fM[x], fH[x] = fa, fb
            else:
                fa, fb = fM[x], fH[x]
            va = resid_coef * (fa + sa * qm - a)
            vb = resid_coef * (fb + sb * qh - b)
            if number > 0:
                va, vb = carry_coef * vM[x] + va, carry_coef * vH[x] + vb
            if number < SWEEPS_H - 1:
                vM[x], vH[x] = va, vb
                new[0][x], new[1][x] = a + va, b + vb
            else:
                table[(x - W) * Y : (x - W + 1) * Y, :] = (a + va)[0:Y]
        old, new = new, old

    gather_rows(table, index, sent)


def heart_body(
    place, current, E, rxl, rxr, phi_out, new_out, mM, mH, uM, uH, wM, wH, vM, vH, fM, fH
):
    X, Y, _ = phi_out.shape
    count = X + 2 * W
    near = pl.ds(0, Y + 2 * W)
    assemble(mM, mH, 0, E, rxl, rxr.at[:, near])
    assemble(uM, uH, 1, E, rxl, rxr.at[:, near])
    (dm, qm, im), (_, qh, ih) = heart_tiles(place, Y)
    ratio = intra_cond / (intra_cond + extra_cond)
    old, new = (uM, uH), (wM, wH)
    for number, (carry_coef, resid_coef) in enumerate(cheb_coeffs(SWEEPS_H)):

        def sweep(x, old=old, new=new, cc=carry_coef, rc=resid_coef, number=number):
            x = wrapped(x, count)
            a, b, sa, sb = around(old[0], old[1], x, count)
            if number == 0:
                c, d, sc, sd = around(mM, mH, x, count)
                fa, fb = -ratio * (c * im - sc * qm), -ratio * (d * ih - sd * qh)
                fM[x], fH[x] = fa, fb
            else:
                fa, fb = fM[x], fH[x]
            va = rc * (fa + sa * qm - a)
            vb = rc * (fb + sb * qh - b)
            if number > 0:
                va, vb = cc * vM[x] + va, cc * vH[x] + vb
            vM[x], vH[x] = va, vb
            new[0][x], new[1][x] = a + va, b + vb

        reach = SWEEPS_H - number
        loop(-reach, X - 1 + reach, sweep)
        old, new = new, old
    phi_out[...] = old[0][0:X, 0:Y]

    def finish(x):
        a, _, sa, _ = around(mM, mH, x, count)
        c, _, sc, _ = around(old[0], old[1], x, count)
        lap = dm * (a + c) - (sa + sc)
        new_out[x] = (a - time_step * intra_cond * lap)[0:Y] - time_step * current[x]

    loop(0, X - 1, finish)


def right_body(arrived, index, weight, right, zlo, zhi, total):
    rows = index_rows = weight.shape[0] * weight.shape[1]
    scatter_rows(lambda s: arrived[pl.ds(s, 1), 0, :], index, rows, total, 4)
    value = penalty * (total[0:rows] + total[rows : 2 * rows])
    right[...] = value.reshape(right.shape)
    z_faces([value, weight[...].reshape(index_rows, LANES)], zlo, zhi)


def faces_body(E, rxl, rxr, F, middle, cM, cH, aM, aH, bM, bH, vM, vH, iM, iH):
    uM, uH, fxM, fxH, fyM, fyH, fzM, fzH, dM, dH = (F.at[k] for k in range(10))
    X, rows = E.shape[1], E.shape[2]
    count = X + 2 * W
    far = pl.ds(rxr.shape[1] - rows, rows)
    assemble(uM, uH, 0, E, rxl, rxr.at[:, far])
    assemble(cM, cH, 1, E, rxl, rxr.at[:, far])

    def harmonic(a, b):
        total = a + b
        return jnp.where(total > 0.0, 2.0 * a * b / jnp.where(total > 0.0, total, 1.0), 0.0)

    def prepare(x):
        xn = wrapped(x + 1, count)
        a, b = cM[x], cH[x]
        za, zb = z_next(a, b)
        fxM[x], fxH[x] = harmonic(a, cM[xn]), harmonic(b, cH[xn])
        fyM[x], fyH[x] = harmonic(a, y_next(a)), harmonic(b, y_next(b))
        fzM[x], fzH[x] = harmonic(a, za), harmonic(b, zb)

    loop(0, count - 1, prepare, 4)

    def total(x):
        xl = wrapped(x - 1, count)
        za, zb = z_last(fzM[x], fzH[x])
        dM[x] = fxM[x] + fxM[xl] + fyM[x] + y_last(fyM[x]) + fzM[x] + za
        dH[x] = fxH[x] + fxH[xl] + fyH[x] + y_last(fyH[x]) + fzH[x] + zb

    loop(0, count - 1, total, 4)

    first = 2 * W - 1
    last = first + middle.shape[0] - 1
    old, new = (uM, uH), (aM, aH)
    for number, (carry_coef, resid_coef) in enumerate(cheb_coeffs(SWEEPS_T)):

        def sweep(x, old=old, new=new, cc=carry_coef, rc=resid_coef, number=number):
            xn, xl = x + 1, x - 1
            m, h = old[0][x], old[1][x]
            if number == 0:
                iM[x], iH[x] = reciprocal(dM[x]), reciprocal(dH[x])
            sm, sh = flow(
                m, h, old[0][xn], old[1][xn], old[0][xl], old[1][xl],
                fxM[x], fxH[x], fxM[xl], fxH[xl], fyM[x], fyH[x], fzM[x], fzH[x],
            )
            va, vb = rc * (sm * iM[x] - m), rc * (sh * iH[x] - h)
            if number > 0:
                va, vb = cc * vM[x] + va, cc * vH[x] + vb
            vM[x], vH[x] = va, vb
            new[0][x], new[1][x] = m + va, h + vb

        reach = SWEEPS_T - 1 - number
        loop(first - reach, last + reach, sweep)
        old, new = new, ((bM, bH) if number == 0 else old)
    middle[...] = old[0][first : last + 1, 0 : middle.shape[1]]


def reciprocal(value):
    return jnp.where(value > 0.0, 1.0 / jnp.where(value > 0.0, value, 1.0), 0.0)


def flow(m, h, nM, nH, lM, lH, fxM, fxH, gxM, gxH, fy, gy, fz, gz):
    zn = z_next(m, h)
    zl = z_last(fz * m, gz * h)
    sm = fxM * nM + gxM * lM + fy * y_next(m) + y_last(fy * m)
    sh = fxH * nH + gxH * lH + gy * y_next(h) + y_last(gy * h)
    return sm + fz * zn[0] + zl[0], sh + gz * zn[1] + zl[1]


def torso_surface_body(
    R, index, F, surface, returned, aM, aH, bM, bH, vM, vH, iM, iH
):
    uM, uH, fxM, fxH, fyM, fyH, fzM, fzH, dM, dH = (F.at[k] for k in range(10))
    S, Y = R.shape[1], surface.shape[1]
    N = surface.shape[0]
    count = F.shape[1]
    old, new = None, (aM, aH)
    for number, (carry_coef, resid_coef) in enumerate(cheb_coeffs(SWEEPS_T)):
        reach = SWEEPS_T - 1 - number

        def value(x, tile, old=old):
            return (uM, uH)[tile][x % count] if old is None else old[tile][x + W]

        for x in range(-reach, N + reach):
            at, last = x % count, (x - 1) % count
            m, h = value(x, 0), value(x, 1)
            sm, sh = flow(
                m, h, value(x + 1, 0), value(x + 1, 1), value(x - 1, 0), value(x - 1, 1),
                fxM[at], fxH[at], fxM[last], fxH[last], fyM[at], fyH[at], fzM[at], fzH[at],
            )
            inside = 0 <= x < S
            if number == 0:
                wm, wh = dM[at], dH[at]
                if inside:
                    wm, wh = wm + R[2, x], wh + R[3, x]
                wm, wh = reciprocal(wm), reciprocal(wh)
                iM[x + W], iH[x + W] = wm, wh
            else:
                wm, wh = iM[x + W], iH[x + W]
            if inside:
                sm, sh = sm + R[0, x], sh + R[1, x]
            va, vb = resid_coef * (sm * wm - m), resid_coef * (sh * wh - h)
            if number > 0:
                va, vb = carry_coef * vM[x + W] + va, carry_coef * vH[x + W] + vb
            if number < SWEEPS_T - 1:
                vM[x + W], vH[x + W] = va, vb
                new[0][x + W], new[1][x + W] = m + va, h + vb
            else:
                surface[x] = (m + va)[0:Y]
        old, new = new, ((bM, bH) if number == 0 else old)
    table = surface[0:S].reshape(S * Y, LANES)

    gather_rows(table, index, returned)


def torso_body(
    surface, middle, rxr, F, torso_out, G, aM, aH, bM, bH, vM, vH, iM, iH, sem
):
    N, M = surface.shape[0], middle.shape[0]
    X, Y, _ = torso_out.shape
    first = N + M - W
    copy = pltpu.make_async_copy(F.at[:, pl.ds(first, G.shape[1])], G, sem)
    copy.start()
    torso_out[0:N] = surface[...]
    torso_out[N : N + M] = middle[...]
    copy.wait()
    uM, uH, fxM, fxH, fyM, fyH, fzM, fzH, dM, dH = (G.at[k] for k in range(10))
    old, new = (uM, uH), (aM, aH)
    for number, (carry_coef, resid_coef) in enumerate(cheb_coeffs(SWEEPS_T)):
        reach = SWEEPS_T - 1 - number
        for x in range(N + M - reach, X + reach):
            at = x - first
            m, h = old[0][at], old[1][at]
            sm, sh = flow(
                m, h, old[0][at + 1], old[1][at + 1], old[0][at - 1], old[1][at - 1],
                fxM[at], fxH[at], fxM[at - 1], fxH[at - 1], fyM[at], fyH[at], fzM[at], fzH[at],
            )
            beyond = x - X
            if number == 0:
                wm, wh = dM[at], dH[at]
                if beyond >= 0:
                    wm = wm + rxr[W + 1 + beyond]
                    wh = wh + lane_unpack(rxr[2 * W + 1], beyond)
                wm, wh = reciprocal(wm), reciprocal(wh)
                iM[at], iH[at] = wm, wh
            else:
                wm, wh = iM[at], iH[at]
            if beyond >= 0:
                sm = sm + rxr[beyond]
                sh = sh + lane_unpack(rxr[W], beyond)
            va, vb = resid_coef * (sm * wm - m), resid_coef * (sh * wh - h)
            if number > 0:
                va, vb = carry_coef * vM[at] + va, carry_coef * vH[at] + vb
            if number < SWEEPS_T - 1:
                vM[at], vH[at] = va, vb
                new[0][at], new[1][at] = m + va, h + vb
            else:
                torso_out[x] = (m + va)[0:Y]
        old, new = new, ((bM, bH) if number == 0 else old)


def final_body(place, sent, back, index, phi, out, total):
    X, Y, _ = phi.shape
    rows = X // 4 * Y
    scatter_rows(
        lambda s: penalty * (sent[pl.ds(s, 1), 0, :] - back[pl.ds(s, 1), 0, :]), index, rows, total, 2
    )
    flux = (total[0:rows] + total[rows : 2 * rows]).reshape(X // 4, Y, LANES)
    (dm, _, _), _ = heart_tiles(place, Y)
    out[X // 4 :] = phi[X // 4 :]
    scale = (1.0 / ((intra_cond + extra_cond) * dm))[0:Y]
    for x in range(X // 4):
        out[x] = phi[x] - flux[x] * scale


def ionic_current(states, membrane, ion_params):
    params_col = ion_params[:, :, None, None, None]
    gate_vals = states.astype(jnp.float32)
    voltage = membrane[None]
    steady = jax.nn.sigmoid((voltage - params_col[0]) / params_col[1])
    gate_vals = steady + (gate_vals - steady) * jnp.exp(-time_step * params_col[2])
    return jnp.sum(params_col[3] * gate_vals * (voltage - params_col[4]), axis=0)


def per_device(
    states, membrane, phi_heart, ion_params, torso_phi, tissue_scale, labels, cond_table,
    send_node, send_count, recv_voxel, recv_count,
):
    X, Y, _ = membrane.shape
    TX, TY, _ = torso_phi.shape
    peers = lax.axis_size("gx") * lax.axis_size("gy")
    cap = send_node.shape[-1]
    place = jnp.stack([
        lax.axis_index("gy"), lax.axis_index("grp"),
        jnp.int32(Y * lax.axis_size("gy")), jnp.int32(LANES * lax.axis_size("grp")), jnp.int32(Y),
    ])
    slots = jnp.arange(cap, dtype=jnp.int32)[None, :]
    send_index = jnp.where(slots < send_count.reshape(peers, 1), send_node.reshape(peers, cap), -1)
    recv_index = jnp.where(slots < recv_count.reshape(peers, 1), recv_voxel.reshape(peers, cap), -1)

    S = TX // 4
    wide = f32(2 * W, X * Y + TX * TY)
    cond, zlo, zhi = call(
        start_body, (f32(TX, TY, LANES), wide, wide), 6, smem=(0,), whole=True,
    )(cond_table, membrane, phi_heart, torso_phi, tissue_scale, labels)
    weight = call(
        weight_body, f32(S, TY, LANES), 1, scratch=[pltpu.VMEM((S * TY, LANES), jnp.float32)]
    )(recv_index)
    current = ionic_current(states, membrane, ion_params)

    heart, torso = (membrane, phi_heart), (torso_phi, cond)
    halos, ryl, ryr = two_stages(place, (heart, torso), zlo, zhi)
    heart_wide, high = call(
        heart_x_body, (wide_of(X, Y), face_of(Y)), 7, smem=(0,)
    )(place, *heart, *halos[:2], ryl, ryr)
    hxl = from_last(high, "gx")
    torso_wide, high, low = call(
        torso_x_body, (wide_of(TX, TY), face_of(TY), face_of(Y + 2 * W + TY)), 8,
        smem=(0,),
    )(place, heart_wide, *torso, *halos[2:], ryl, ryr)
    txl, xr = from_last(high, "gx"), from_next(low, "gx")

    thin = pltpu.VMEM((3 * W, Y + 2 * W, LANES), jnp.float32)
    sent = call(
        heart_surface_body, f32(peers, 1, cap), 4,
        scratch=[pltpu.VMEM((X // 4 * Y, LANES), jnp.float32)] + [thin] * 10, smem=(0,),
    )(place, heart_wide, hxl, send_index)
    arrived = swap(sent)

    ext = pltpu.VMEM((X + 2 * W, Y + 2 * W, LANES), jnp.float32)
    phi_new, new_membrane = call(
        heart_body, (f32(X, Y, LANES), f32(X, Y, LANES)), 5,
        scratch=[ext] * 10, smem=(0,),
    )(place, current, heart_wide, hxl, xr)
    right, rzlo, rzhi = call(
        right_body,
        (f32(S, TY, LANES), f32(2 * W, S * TY), f32(2 * W, S * TY)),
        3, scratch=[pltpu.VMEM((2 * S * TY, LANES), jnp.float32)],
    )(arrived, recv_index, weight)
    text = (TX + 2 * W, TY + 2 * W, LANES)
    big = pltpu.VMEM(text, jnp.float32)
    N = S + SWEEPS_T - 1
    middle_n = TX - S - 2 * (SWEEPS_T - 1)
    faces, middle = call(
        faces_body, (f32(10, *text), f32(middle_n, TY, LANES)), 3, scratch=[big] * 10
    )(torso_wide, txl, xr)
    halos, ryl, ryr = two_stages(place, ((right, weight),), rzlo, rzhi)
    right_wide, low = call(
        right_x_body, (wide_of(S, TY), face_of(TY)), 7, smem=(0,)
    )(place, right, weight, *halos, ryl, ryr)
    rxr = from_next(low, "gx")
    flat = pltpu.VMEM((N + 2 * W, TY + 2 * W, LANES), jnp.float32)
    surface, returned = call(
        torso_surface_body, (f32(N, TY, LANES), f32(peers, 1, cap)), 3,
        scratch=[flat] * 8,
    )(right_wide, recv_index, faces)
    back = swap(returned)
    last_n = TX - N - middle_n + 2 * W
    thin = pltpu.VMEM((last_n, TY + 2 * W, LANES), jnp.float32)
    torso_out = call(
        torso_body, f32(TX, TY, LANES), 4,
        scratch=[pltpu.VMEM((10, last_n, TY + 2 * W, LANES), jnp.float32)]
        + [thin] * 8 + [pltpu.SemaphoreType.DMA(())],
        left=(3,), whole=True,
    )(surface, middle, rxr, faces)
    heart_phi = call(
        final_body, f32(X, Y, LANES), 5,
        scratch=[pltpu.VMEM((2 * X // 4 * Y, LANES), jnp.float32)], smem=(0,),
    )(place, sent, back, send_index, phi_new)
    return (new_membrane, heart_phi, torso_out)


def solution(mesh):
    placed = (
        P(None, "gx", "gy", "grp"),
        P("gx", "gy", "grp"),
        P("gx", "gy", "grp"),
        P(),
        P("gx", "gy", "grp"),
        P("gx", "gy", "grp"),
        P("gx", "gy", "grp"),
        P(),
        P("grp", "gx", "gy", None, None),
        P("grp", "gx", "gy", None),
        P("grp", "gx", "gy", None, None),
        P("grp", "gx", "gy", None),
    )
    return jax.shard_map(
        per_device,
        mesh=mesh,
        in_specs=placed,
        out_specs=(P("gx", "gy", "grp"), P("gx", "gy", "grp"), P("gx", "gy", "grp")),
        check_vma=False,
    )
```

```python
import jax
import jax.numpy as jnp
from jax import lax
from jax.experimental import pallas as pl
from jax.experimental.pallas import tpu as pltpu
from jax.sharding import PartitionSpec as P


LABELS = 4
SWEEPS_H = 3
SWEEPS_T = 4
W = 4
LANES = 128

time_step = 0.1
intra_cond = 0.25
extra_cond = 0.5
penalty = 2.0
cheb_low = 0.1
cheb_high = 2.0
VMEM_LIMIT = 24 << 20
VMEM_WHOLE = 60 * 1024 * 1024


def cheb_coeffs(sweeps):
    centre = 0.5 * (cheb_high + cheb_low)
    half_width = 0.5 * (cheb_high - cheb_low)
    scaled = centre / half_width
    coeffs = [(0.0, 1.0 / centre)]
    rho_old = 1.0 / scaled
    for _ in range(1, sweeps):
        rho_new = 1.0 / (2.0 * scaled - rho_old)
        coeffs.append((rho_new * rho_old, 2.0 * rho_new / half_width))
        rho_old = rho_new
    return coeffs


def f32(*shape):
    return jax.ShapeDtypeStruct(shape, jnp.float32)


def call(body, outs, n_in, scratch=(), smem=(), left=(), whole=False):
    spaces = [pltpu.SMEM if i in smem else pl.ANY if i in left else pltpu.VMEM for i in range(n_in)]
    return pl.pallas_call(
        body,
        out_shape=outs,
        in_specs=[pl.BlockSpec(memory_space=space) for space in spaces],
        out_specs=jax.tree.map(lambda _: pl.BlockSpec(memory_space=pltpu.VMEM), outs),
        scratch_shapes=list(scratch),
        compiler_params=pltpu.CompilerParams(vmem_limit_bytes=VMEM_WHOLE if whole else VMEM_LIMIT),
    )


def loop(first, last, body, steps=2):
    unroll = (last - first + 1) // steps

    def step(i, carry):
        for u in range(unroll):
            body(i * unroll + u + first)
        return carry

    lax.fori_loop(0, steps, step, 0)


def lane_iota(rows):
    return lax.broadcasted_iota(jnp.int32, (rows, LANES), 1)


def z_faces(values, zlo, zhi):
    for number, value in enumerate(values):
        turned = value.T
        zlo[W * number : W * (number + 1), :] = turned[:W]
        zhi[W * number : W * (number + 1), :] = turned[LANES - W :]


def lane_pack(slices):
    rows = slices[0].shape[0]
    lane = lane_iota(rows)
    packed = jnp.zeros((rows, LANES), jnp.float32)
    for x, item in enumerate(slices):
        spot = (lane >= 2 * W * x) & (lane < 2 * W * (x + 1))
        packed = jnp.where(spot, pltpu.roll(item, (2 * W * x + W) % LANES, 1), packed)
    return packed


def lane_unpack(packed, x):
    lane = lane_iota(packed.shape[0])
    moved = pltpu.roll(packed, (2 * LANES - (2 * W * x + W)) % LANES, 1)
    return jnp.where((lane < W) | (lane >= LANES - W), moved, 0.0)


def edges(place):
    j, g, ny, nz, rows = place[0], place[1], place[2], place[3], place[4]
    return (j > 0, (j + 1) * rows < ny), (g > 0, (g + 1) * LANES < nz)


def y_part(f0, f1, rl, rr, h0, h1, ylo, yhi, near):
    X, Y, _ = f0.shape
    for number, h in enumerate((h0, h1)):
        part = slice(W * number, W * (number + 1))
        left = jnp.where(near[0], rl[part, :], 0.0)
        right = jnp.where(near[1], rr[part, :], 0.0)
        rows = jnp.concatenate([left, right], 0).T
        wide = jnp.concatenate([rows, jnp.zeros((X * Y, LANES - 2 * W), jnp.float32)], 1)
        h[...] = pltpu.roll(wide, LANES - W, 1).reshape(X, Y, LANES)
    for out, part in ((ylo, slice(0, W)), (yhi, slice(Y - W, Y))):
        out[0:X] = jnp.concatenate([f0[:, part, :], f1[:, part, :]], 1)
        out[X] = lane_pack([jnp.concatenate([h0[x, part], h1[x, part]], 0) for x in range(X)])


def fill(E, f0, f1, h0, h1, ryl, ryr, near):
    X, Y, _ = f0.shape
    for number, (f, h) in enumerate(((f0, h0), (f1, h1))):
        part = slice(W * number, W * (number + 1))
        right = jnp.where(near[1], ryr[:, part], 0.0)
        left = jnp.where(near[0], ryl[:, part], 0.0)
        both = jnp.concatenate([right, left], 1)
        E[2 * number, :, 0:Y] = f[...]
        E[2 * number, :, Y:] = both[0:X]
        E[2 * number + 1, :, 0:Y] = h[...]
        for x in range(X):
            E[2 * number + 1, x, Y:] = lane_unpack(both[X], x)


def x_face(E, start, out):
    for number in range(2):
        base = (W + 1) * number
        out[base : base + W] = E[2 * number, start : start + W]
        out[base + W] = lane_pack([E[2 * number + 1, start + x] for x in range(W)])


def static_y_body(place, table, m, p, phi, scale, labels, rl, rr, h0, h1, g0, g1, cond, ylo, yhi):
    near = edges(place)[1]
    X, Y, _ = m.shape
    TX, TY, _ = phi.shape
    cond[...] = conductivity(table, scale, labels)
    cols, rows = pl.ds(0, X * Y), pl.ds(0, X + 1)
    y_part(m, p, rl.at[:, cols], rr.at[:, cols], h0, h1, ylo.at[rows], yhi.at[rows], near)
    cols, rows = pl.ds(X * Y, TX * TY), pl.ds(X + 1, TX + 1)
    y_part(phi, cond, rl.at[:, cols], rr.at[:, cols], g0, g1, ylo.at[rows], yhi.at[rows], near)


def right_y_body(place, right, weight, rl, rr, h0, h1, ylo, yhi):
    y_part(right, weight, rl, rr, h0, h1, ylo, yhi, edges(place)[1])


def heart_x_body(place, f0, f1, h0, h1, ryl, ryr, E, high):
    X = f0.shape[0]
    rows = pl.ds(0, X + 1)
    fill(E, f0, f1, h0, h1, ryl.at[rows], ryr.at[rows], edges(place)[0])
    x_face(E, X - W, high)


def torso_x_body(place, heart, f0, f1, h0, h1, ryl, ryr, E, high, low):
    X = f0.shape[0]
    rows = pl.ds(heart.shape[1] + 1, X + 1)
    fill(E, f0, f1, h0, h1, ryl.at[rows], ryr.at[rows], edges(place)[0])
    x_face(E, X - W, high)
    x_face(heart, 0, low.at[:, pl.ds(0, heart.shape[2])])
    x_face(E, 0, low.at[:, pl.ds(heart.shape[2], E.shape[2])])


def right_x_body(place, f0, f1, h0, h1, ryl, ryr, E, low):
    fill(E, f0, f1, h0, h1, ryl, ryr, edges(place)[0])
    x_face(E, 0, low)


def from_next(value, axis):
    count = lax.axis_size(axis)
    return lax.ppermute(value, axis, [((i + 1) % count, i) for i in range(count)])


def from_last(value, axis):
    count = lax.axis_size(axis)
    return lax.ppermute(value, axis, [(i, (i + 1) % count) for i in range(count)])


def swap(value):
    return lax.all_to_all(value, ("gx", "gy"), split_axis=0, concat_axis=0, tiled=True)


def both_ways(low, high, axis):
    after = from_next(low, axis)
    return from_last(high, axis), after


def wide_of(X, Y):
    return f32(4, X, Y + 2 * W, LANES)


def face_of(rows):
    return f32(2 * (W + 1), rows + 2 * W, LANES)


def assemble(M, H, number, E, rxl, rxr):
    X = E.shape[1]
    base = (W + 1) * number
    M[0:X] = E[2 * number]
    H[0:X] = E[2 * number + 1]
    top = M.shape[0] - 2 * W
    for start, source in ((top, rxr), (top + W, rxl)):
        if source is None:
            continue
        M[start : start + W] = source[base : base + W]
        for x in range(W):
            H[start + x] = lane_unpack(source[base + W], x)


def y_next(v):
    return pltpu.roll(v, v.shape[0] - 1, 0)


def y_last(v):
    return pltpu.roll(v, 1, 0)


def z_next(m, h):
    end = lane_iota(m.shape[0]) == LANES - 1
    rm, rh = pltpu.roll(m, LANES - 1, 1), pltpu.roll(h, LANES - 1, 1)
    return jnp.where(end, rh, rm), jnp.where(end, rm, rh)


def z_last(m, h):
    end = lane_iota(m.shape[0]) == 0
    rm, rh = pltpu.roll(m, 1, 1), pltpu.roll(h, 1, 1)
    return jnp.where(end, rh, rm), jnp.where(end, rm, rh)


def wrapped(x, count):
    return jnp.where(x >= count, x - count, jnp.where(x < 0, x + count, x))


def around(M, H, x, count):
    xn, xl = wrapped(x + 1, count), wrapped(x - 1, count)
    m, h = M[x], H[x]
    zn, zl = z_next(m, h), z_last(m, h)
    sm = M[xn] + M[xl] + y_next(m) + y_last(m) + zn[0] + zl[0]
    sh = H[xn] + H[xl] + y_next(h) + y_last(h) + zn[1] + zl[1]
    return m, h, sm, sh


def gather_rows(table, index, out):
    rows_n = table.shape[0]

    def tile(i, carry):
        top = pl.multiple_of(i * 8, 8)
        for j in range(index.shape[1] // LANES):
            spot = (pl.ds(top, 8), slice(j * LANES, (j + 1) * LANES))
            where = index[spot[0], spot[1]]
            cols, rows = where & (LANES - 1), where >> 7
            total = jnp.zeros((8, LANES), jnp.float32)
            for r in range(rows_n):
                line = jnp.broadcast_to(table[r : r + 1, :], (8, LANES))
                got = jnp.take_along_axis(line, cols, axis=1, mode="promise_in_bounds")
                total = jnp.where(rows == r, got, total)
            out[spot[0], 0, spot[1]] = total
        return carry

    lax.fori_loop(0, index.shape[0] // 8, tile, 0)


def scatter_rows(value_of, index, rows_n, total, batch):
    cap = index.shape[1]
    total[...] = jnp.zeros_like(total)
    half = jnp.bfloat16

    def rows_iota(count):
        return lax.broadcasted_iota(jnp.int32, (count, cap), 0).astype(jnp.float32).astype(half)

    row_ids, col_ids = rows_iota(rows_n), rows_iota(LANES)
    ones = jnp.ones((1, cap), half)

    def hot(ids, key, weight):
        key = jnp.broadcast_to(key.astype(jnp.float32).astype(half), ids.shape)
        return jnp.where(ids == key, jnp.broadcast_to(weight, ids.shape), jnp.zeros((), half))

    def one(s):
        where = index[pl.ds(s, 1), :]
        rows, cols = where >> 7, where & (LANES - 1)
        if value_of is None:
            left = hot(row_ids, rows, ones)
        else:
            value = value_of(s)
            high = value.astype(half)
            low = (value - high.astype(jnp.float32)).astype(half)
            left = jnp.concatenate([hot(row_ids, rows, high), hot(row_ids, rows, low)], 0)
        return left, hot(col_ids, cols, ones)

    def step(i, carry):
        part = None
        for b in range(batch):
            sides = [one(i * (8 * batch) + 8 * b + k) for k in range(8)]
            product = lax.dot_general(
                jnp.concatenate([side[0] for side in sides], 1),
                jnp.concatenate([side[1] for side in sides], 1),
                (((1,), (1,)), ((), ())),
                preferred_element_type=jnp.float32,
            )
            part = product if part is None else part + product
        total[...] += part
        return carry

    lax.fori_loop(0, index.shape[0] // (8 * batch), step, 0)


def conductivity(table, scale, labels):
    picked = jnp.zeros(labels.shape, jnp.float32)
    for number in range(LABELS):
        picked = jnp.where(labels[...] == number, table[number], picked)
    return scale[...] * picked


def start_body(table, m, p, phi, scale, labels, zlo, zhi):
    X, Y, _ = m.shape
    TX, TY, _ = phi.shape
    cols, more = pl.ds(0, X * Y), pl.ds(X * Y, TX * TY)
    z_faces(
        [m[...].reshape(X * Y, LANES), p[...].reshape(X * Y, LANES)], zlo.at[:, cols], zhi.at[:, cols]
    )
    value = conductivity(table, scale, labels)
    z_faces(
        [phi[...].reshape(TX * TY, LANES), value.reshape(TX * TY, LANES)], zlo.at[:, more], zhi.at[:, more]
    )


def weight_body(index, weight, total):
    scatter_rows(None, index, total.shape[0], total, 2)
    weight[...] = (penalty * total[...]).reshape(weight.shape)


def heart_tiles(place, Y):
    j, g = place[0], place[1]
    row = lax.broadcasted_iota(jnp.int32, (Y + 2 * W, LANES), 0)
    lane = lane_iota(Y + 2 * W)
    yg = j * Y + jnp.where(row >= Y + W, row - Y - 2 * W, row)
    tiles = []
    for zl in (lane, jnp.where(lane >= LANES // 2, lane - LANES, lane + LANES)):
        zg = g * LANES + zl
        ny, nz = place[2], place[3]
        one = lambda cond: cond.astype(jnp.float32)
        inside = one((yg >= 0) & (yg < ny) & (zg >= 0) & (zg < nz))
        diag = 2.0 + one(yg + 1 < ny) + one(yg - 1 >= 0) + one(zg + 1 < nz) + one(zg - 1 >= 0)
        tiles.append((diag, inside / diag, inside))
    return tiles


def heart_surface_body(place, E, rxl, index, sent, table, mM, mH, uM, uH, wM, wH, vM, vH, fM, fH):
    S, Y = E.shape[1] // 4, E.shape[2] - 2 * W
    for number, (M, H) in enumerate(((mM, mH), (uM, uH))):
        base = (W + 1) * number
        M[0:W] = rxl[base : base + W]
        for x in range(W):
            H[x] = lane_unpack(rxl[base + W], x)
        M[W:] = E[2 * number, 0 : 2 * W]
        H[W:] = E[2 * number + 1, 0 : 2 * W]
    count = 3 * W
    (_, qm, im), (_, qh, ih) = heart_tiles(place, Y)
    ratio = intra_cond / (intra_cond + extra_cond)
    old, new = (uM, uH), (wM, wH)
    for number, (carry_coef, resid_coef) in enumerate(cheb_coeffs(SWEEPS_H)):
        reach = SWEEPS_H - 1 - number
        for x in range(W - reach, W + S + reach):
            a, b, sa, sb = around(old[0], old[1], x, count)
            if number == 0:
                c, d, sc, sd = around(mM, mH, x, count)
                fa, fb = -ratio * (c * im - sc * qm), -ratio * (d * ih - sd * qh)
                fM[x], fH[x] = fa, fb
            else:
                fa, fb = fM[x], fH[x]
            va = resid_coef * (fa + sa * qm - a)
            vb = resid_coef * (fb + sb * qh - b)
            if number > 0:
                va, vb = carry_coef * vM[x] + va, carry_coef * vH[x] + vb
            if number < SWEEPS_H - 1:
                vM[x], vH[x] = va, vb
                new[0][x], new[1][x] = a + va, b + vb
            else:
                table[(x - W) * Y : (x - W + 1) * Y, :] = (a + va)[0:Y]
        old, new = new, old

    gather_rows(table, index, sent)


def heart_body(
    place, current, E, rxl, rxr, phi_out, new_out, mM, mH, uM, uH, wM, wH, vM, vH, fM, fH
):
    X, Y, _ = phi_out.shape
    count = X + 2 * W
    near = pl.ds(0, Y + 2 * W)
    assemble(mM, mH, 0, E, rxl, rxr.at[:, near])
    assemble(uM, uH, 1, E, rxl, rxr.at[:, near])
    (dm, qm, im), (_, qh, ih) = heart_tiles(place, Y)
    ratio = intra_cond / (intra_cond + extra_cond)
    old, new = (uM, uH), (wM, wH)
    for number, (carry_coef, resid_coef) in enumerate(cheb_coeffs(SWEEPS_H)):

        def sweep(x, old=old, new=new, cc=carry_coef, rc=resid_coef, number=number):
            x = wrapped(x, count)
            a, b, sa, sb = around(old[0], old[1], x, count)
            if number == 0:
                c, d, sc, sd = around(mM, mH, x, count)
                fa, fb = -ratio * (c * im - sc * qm), -ratio * (d * ih - sd * qh)
                fM[x], fH[x] = fa, fb
            else:
                fa, fb = fM[x], fH[x]
            va = rc * (fa + sa * qm - a)
            vb = rc * (fb + sb * qh - b)
            if number > 0:
                va, vb = cc * vM[x] + va, cc * vH[x] + vb
            vM[x], vH[x] = va, vb
            new[0][x], new[1][x] = a + va, b + vb

        reach = SWEEPS_H - number
        loop(-reach, X - 1 + reach, sweep)
        old, new = new, old
    phi_out[...] = old[0][0:X, 0:Y]

    def finish(x):
        a, _, sa, _ = around(mM, mH, x, count)
        c, _, sc, _ = around(old[0], old[1], x, count)
        lap = dm * (a + c) - (sa + sc)
        new_out[x] = (a - time_step * intra_cond * lap)[0:Y] - time_step * current[x]

    loop(0, X - 1, finish)


def right_body(arrived, index, weight, right, zlo, zhi, total):
    rows = index_rows = weight.shape[0] * weight.shape[1]
    scatter_rows(lambda s: arrived[pl.ds(s, 1), 0, :], index, rows, total, 4)
    value = penalty * (total[0:rows] + total[rows : 2 * rows])
    right[...] = value.reshape(right.shape)
    z_faces([value, weight[...].reshape(index_rows, LANES)], zlo, zhi)


def faces_body(E, rxl, rxr, F, middle, cM, cH, aM, aH, bM, bH, vM, vH, iM, iH):
    uM, uH, fxM, fxH, fyM, fyH, fzM, fzH, dM, dH = (F.at[k] for k in range(10))
    X, rows = E.shape[1], E.shape[2]
    count = X + 2 * W
    far = pl.ds(rxr.shape[1] - rows, rows)
    assemble(uM, uH, 0, E, rxl, rxr.at[:, far])
    assemble(cM, cH, 1, E, rxl, rxr.at[:, far])

    def harmonic(a, b):
        total = a + b
        return jnp.where(total > 0.0, 2.0 * a * b / jnp.where(total > 0.0, total, 1.0), 0.0)

    def prepare(x):
        xn = wrapped(x + 1, count)
        a, b = cM[x], cH[x]
        za, zb = z_next(a, b)
        fxM[x], fxH[x] = harmonic(a, cM[xn]), harmonic(b, cH[xn])
        fyM[x], fyH[x] = harmonic(a, y_next(a)), harmonic(b, y_next(b))
        fzM[x], fzH[x] = harmonic(a, za), harmonic(b, zb)

    loop(0, count - 1, prepare, 4)

    def total(x):
        xl = wrapped(x - 1, count)
        za, zb = z_last(fzM[x], fzH[x])
        dM[x] = fxM[x] + fxM[xl] + fyM[x] + y_last(fyM[x]) + fzM[x] + za
        dH[x] = fxH[x] + fxH[xl] + fyH[x] + y_last(fyH[x]) + fzH[x] + zb

    loop(0, count - 1, total, 4)

    first = 2 * W - 1
    last = first + middle.shape[0] - 1
    old, new = (uM, uH), (aM, aH)
    for number, (carry_coef, resid_coef) in enumerate(cheb_coeffs(SWEEPS_T)):

        def sweep(x, old=old, new=new, cc=carry_coef, rc=resid_coef, number=number):
            xn, xl = x + 1, x - 1
            m, h = old[0][x], old[1][x]
            if number == 0:
                iM[x], iH[x] = reciprocal(dM[x]), reciprocal(dH[x])
            sm, sh = flow(
                m, h, old[0][xn], old[1][xn], old[0][xl], old[1][xl],
                fxM[x], fxH[x], fxM[xl], fxH[xl], fyM[x], fyH[x], fzM[x], fzH[x],
            )
            va, vb = rc * (sm * iM[x] - m), rc * (sh * iH[x] - h)
            if number > 0:
                va, vb = cc * vM[x] + va, cc * vH[x] + vb
            vM[x], vH[x] = va, vb
            new[0][x], new[1][x] = m + va, h + vb

        reach = SWEEPS_T - 1 - number
        loop(first - reach, last + reach, sweep)
        old, new = new, ((bM, bH) if number == 0 else old)
    middle[...] = old[0][first : last + 1, 0 : middle.shape[1]]


def reciprocal(value):
    return jnp.where(value > 0.0, 1.0 / jnp.where(value > 0.0, value, 1.0), 0.0)


def flow(m, h, nM, nH, lM, lH, fxM, fxH, gxM, gxH, fy, gy, fz, gz):
    zn = z_next(m, h)
    zl = z_last(fz * m, gz * h)
    sm = fxM * nM + gxM * lM + fy * y_next(m) + y_last(fy * m)
    sh = fxH * nH + gxH * lH + gy * y_next(h) + y_last(gy * h)
    return sm + fz * zn[0] + zl[0], sh + gz * zn[1] + zl[1]


def torso_surface_body(
    R, index, F, surface, returned, aM, aH, bM, bH, vM, vH, iM, iH
):
    uM, uH, fxM, fxH, fyM, fyH, fzM, fzH, dM, dH = (F.at[k] for k in range(10))
    S, Y = R.shape[1], surface.shape[1]
    N = surface.shape[0]
    count = F.shape[1]
    old, new = None, (aM, aH)
    for number, (carry_coef, resid_coef) in enumerate(cheb_coeffs(SWEEPS_T)):
        reach = SWEEPS_T - 1 - number

        def value(x, tile, old=old):
            return (uM, uH)[tile][x % count] if old is None else old[tile][x + W]

        for x in range(-reach, N + reach):
            at, last = x % count, (x - 1) % count
            m, h = value(x, 0), value(x, 1)
            sm, sh = flow(
                m, h, value(x + 1, 0), value(x + 1, 1), value(x - 1, 0), value(x - 1, 1),
                fxM[at], fxH[at], fxM[last], fxH[last], fyM[at], fyH[at], fzM[at], fzH[at],
            )
            inside = 0 <= x < S
            if number == 0:
                wm, wh = dM[at], dH[at]
                if inside:
                    wm, wh = wm + R[2, x], wh + R[3, x]
                wm, wh = reciprocal(wm), reciprocal(wh)
                iM[x + W], iH[x + W] = wm, wh
            else:
                wm, wh = iM[x + W], iH[x + W]
            if inside:
                sm, sh = sm + R[0, x], sh + R[1, x]
            va, vb = resid_coef * (sm * wm - m), resid_coef * (sh * wh - h)
            if number > 0:
                va, vb = carry_coef * vM[x + W] + va, carry_coef * vH[x + W] + vb
            if number < SWEEPS_T - 1:
                vM[x + W], vH[x + W] = va, vb
                new[0][x + W], new[1][x + W] = m + va, h + vb
            else:
                surface[x] = (m + va)[0:Y]
        old, new = new, ((bM, bH) if number == 0 else old)
    table = surface[0:S].reshape(S * Y, LANES)

    gather_rows(table, index, returned)


def torso_body(
    surface, middle, rxr, F, torso_out, G, aM, aH, bM, bH, vM, vH, iM, iH, sem
):
    N, M = surface.shape[0], middle.shape[0]
    X, Y, _ = torso_out.shape
    first = N + M - W
    copy = pltpu.make_async_copy(F.at[:, pl.ds(first, G.shape[1])], G, sem)
    copy.start()
    torso_out[0:N] = surface[...]
    torso_out[N : N + M] = middle[...]
    copy.wait()
    uM, uH, fxM, fxH, fyM, fyH, fzM, fzH, dM, dH = (G.at[k] for k in range(10))
    old, new = (uM, uH), (aM, aH)
    for number, (carry_coef, resid_coef) in enumerate(cheb_coeffs(SWEEPS_T)):
        reach = SWEEPS_T - 1 - number
        for x in range(N + M - reach, X + reach):
            at = x - first
            m, h = old[0][at], old[1][at]
            sm, sh = flow(
                m, h, old[0][at + 1], old[1][at + 1], old[0][at - 1], old[1][at - 1],
                fxM[at], fxH[at], fxM[at - 1], fxH[at - 1], fyM[at], fyH[at], fzM[at], fzH[at],
            )
            beyond = x - X
            if number == 0:
                wm, wh = dM[at], dH[at]
                if beyond >= 0:
                    wm = wm + rxr[W + 1 + beyond]
                    wh = wh + lane_unpack(rxr[2 * W + 1], beyond)
                wm, wh = reciprocal(wm), reciprocal(wh)
                iM[at], iH[at] = wm, wh
            else:
                wm, wh = iM[at], iH[at]
            if beyond >= 0:
                sm = sm + rxr[beyond]
                sh = sh + lane_unpack(rxr[W], beyond)
            va, vb = resid_coef * (sm * wm - m), resid_coef * (sh * wh - h)
            if number > 0:
                va, vb = carry_coef * vM[at] + va, carry_coef * vH[at] + vb
            if number < SWEEPS_T - 1:
                vM[at], vH[at] = va, vb
                new[0][at], new[1][at] = m + va, h + vb
            else:
                torso_out[x] = (m + va)[0:Y]
        old, new = new, ((bM, bH) if number == 0 else old)


def final_body(place, sent, back, index, phi, out, total):
    X, Y, _ = phi.shape
    rows = X // 4 * Y
    scatter_rows(
        lambda s: penalty * (sent[pl.ds(s, 1), 0, :] - back[pl.ds(s, 1), 0, :]), index, rows, total, 2
    )
    flux = (total[0:rows] + total[rows : 2 * rows]).reshape(X // 4, Y, LANES)
    (dm, _, _), _ = heart_tiles(place, Y)
    out[X // 4 :] = phi[X // 4 :]
    scale = (1.0 / ((intra_cond + extra_cond) * dm))[0:Y]
    for x in range(X // 4):
        out[x] = phi[x] - flux[x] * scale


def ionic_current(states, membrane, ion_params):
    params_col = ion_params[:, :, None, None, None]
    gate_vals = states.astype(jnp.float32)
    voltage = membrane[None]
    steady = jax.nn.sigmoid((voltage - params_col[0]) / params_col[1])
    gate_vals = steady + (gate_vals - steady) * jnp.exp(-time_step * params_col[2])
    return jnp.sum(params_col[3] * gate_vals * (voltage - params_col[4]), axis=0)


def per_device(
    states, membrane, phi_heart, ion_params, torso_phi, tissue_scale, labels, cond_table,
    send_node, send_count, recv_voxel, recv_count,
):
    X, Y, _ = membrane.shape
    TX, TY, _ = torso_phi.shape
    peers = lax.axis_size("gx") * lax.axis_size("gy")
    cap = send_node.shape[-1]
    place = jnp.stack([
        lax.axis_index("gy"), lax.axis_index("grp"),
        jnp.int32(Y * lax.axis_size("gy")), jnp.int32(LANES * lax.axis_size("grp")), jnp.int32(Y),
    ])
    slots = jnp.arange(cap, dtype=jnp.int32)[None, :]
    send_index = jnp.where(slots < send_count.reshape(peers, 1), send_node.reshape(peers, cap), -1)
    recv_index = jnp.where(slots < recv_count.reshape(peers, 1), recv_voxel.reshape(peers, cap), -1)

    S = TX // 4
    wide = f32(2 * W, X * Y + TX * TY)
    zlo, zhi = call(start_body, (wide, wide), 6, smem=(0,), whole=True)(
        cond_table, membrane, phi_heart, torso_phi, tissue_scale, labels
    )
    weight = call(
        weight_body, f32(S, TY, LANES), 1, scratch=[pltpu.VMEM((S * TY, LANES), jnp.float32)]
    )(recv_index)
    current = ionic_current(states, membrane, ion_params)

    hbox, tbox, tall = f32(X, Y, LANES), f32(TX, TY, LANES), f32(X + TX + 2, 2 * W, LANES)
    *halos, cond, ylo, yhi = call(
        static_y_body, (hbox, hbox, tbox, tbox, tbox, tall, tall), 9, smem=(0, 1),
    )(
        place, cond_table, membrane, phi_heart, torso_phi, tissue_scale, labels,
        *both_ways(zlo, zhi, "grp"),
    )
    heart, torso = (membrane, phi_heart), (torso_phi, cond)
    ryl, ryr = both_ways(ylo, yhi, "gy")
    heart_wide, high = call(
        heart_x_body, (wide_of(X, Y), face_of(Y)), 7, smem=(0,)
    )(place, *heart, *halos[:2], ryl, ryr)
    hxl = from_last(high, "gx")
    torso_wide, high, low = call(
        torso_x_body, (wide_of(TX, TY), face_of(TY), face_of(Y + 2 * W + TY)), 8,
        smem=(0,),
    )(place, heart_wide, *torso, *halos[2:], ryl, ryr)
    txl, xr = from_last(high, "gx"), from_next(low, "gx")

    thin = pltpu.VMEM((3 * W, Y + 2 * W, LANES), jnp.float32)
    sent = call(
        heart_surface_body, f32(peers, 1, cap), 4,
        scratch=[pltpu.VMEM((X // 4 * Y, LANES), jnp.float32)] + [thin] * 10, smem=(0,),
    )(place, heart_wide, hxl, send_index)
    arrived = swap(sent)

    ext = pltpu.VMEM((X + 2 * W, Y + 2 * W, LANES), jnp.float32)
    phi_new, new_membrane = call(
        heart_body, (f32(X, Y, LANES), f32(X, Y, LANES)), 5,
        scratch=[ext] * 10, smem=(0,),
    )(place, current, heart_wide, hxl, xr)
    right, rzlo, rzhi = call(
        right_body,
        (f32(S, TY, LANES), f32(2 * W, S * TY), f32(2 * W, S * TY)),
        3, scratch=[pltpu.VMEM((2 * S * TY, LANES), jnp.float32)],
    )(arrived, recv_index, weight)
    text = (TX + 2 * W, TY + 2 * W, LANES)
    big = pltpu.VMEM(text, jnp.float32)
    N = S + SWEEPS_T - 1
    middle_n = TX - S - 2 * (SWEEPS_T - 1)
    faces, middle = call(
        faces_body, (f32(10, *text), f32(middle_n, TY, LANES)), 3, scratch=[big] * 10
    )(torso_wide, txl, xr)
    tall = f32(S + 1, 2 * W, LANES)
    *halos, ylo, yhi = call(
        right_y_body, (f32(S, TY, LANES),) * 2 + (tall, tall), 5, smem=(0,),
    )(place, right, weight, *both_ways(rzlo, rzhi, "grp"))
    ryl, ryr = both_ways(ylo, yhi, "gy")
    right_wide, low = call(
        right_x_body, (wide_of(S, TY), face_of(TY)), 7, smem=(0,)
    )(place, right, weight, *halos, ryl, ryr)
    rxr = from_next(low, "gx")
    flat = pltpu.VMEM((N + 2 * W, TY + 2 * W, LANES), jnp.float32)
    surface, returned = call(
        torso_surface_body, (f32(N, TY, LANES), f32(peers, 1, cap)), 3,
        scratch=[flat] * 8,
    )(right_wide, recv_index, faces)
    back = swap(returned)
    last_n = TX - N - middle_n + 2 * W
    thin = pltpu.VMEM((last_n, TY + 2 * W, LANES), jnp.float32)
    torso_out = call(
        torso_body, f32(TX, TY, LANES), 4,
        scratch=[pltpu.VMEM((10, last_n, TY + 2 * W, LANES), jnp.float32)]
        + [thin] * 8 + [pltpu.SemaphoreType.DMA(())],
        left=(3,),
    )(surface, middle, rxr, faces)
    heart_phi = call(
        final_body, f32(X, Y, LANES), 5,
        scratch=[pltpu.VMEM((2 * X // 4 * Y, LANES), jnp.float32)], smem=(0,),
    )(place, sent, back, send_index, phi_new)
    return (new_membrane, heart_phi, torso_out)


def solution(mesh):
    placed = (
        P(None, "gx", "gy", "grp"),
        P("gx", "gy", "grp"),
        P("gx", "gy", "grp"),
        P(),
        P("gx", "gy", "grp"),
        P("gx", "gy", "grp"),
        P("gx", "gy", "grp"),
        P(),
        P("grp", "gx", "gy", None, None),
        P("grp", "gx", "gy", None),
        P("grp", "gx", "gy", None, None),
        P("grp", "gx", "gy", None),
    )
    return jax.shard_map(
        per_device,
        mesh=mesh,
        in_specs=placed,
        out_specs=(P("gx", "gy", "grp"), P("gx", "gy", "grp"), P("gx", "gy", "grp")),
        check_vma=False,
    )
```

```python
import jax
import jax.numpy as jnp
from jax import lax
from jax.experimental import pallas as pl
from jax.experimental.pallas import tpu as pltpu
from jax.sharding import PartitionSpec as P


LABELS = 4
SWEEPS_H = 3
SWEEPS_T = 4
W = 4
LANES = 128

time_step = 0.1
intra_cond = 0.25
extra_cond = 0.5
penalty = 2.0
cheb_low = 0.1
cheb_high = 2.0
VMEM_LIMIT = 24 << 20
VMEM_WHOLE = 60 * 1024 * 1024


def cheb_coeffs(sweeps):
    centre = 0.5 * (cheb_high + cheb_low)
    half_width = 0.5 * (cheb_high - cheb_low)
    scaled = centre / half_width
    coeffs = [(0.0, 1.0 / centre)]
    rho_old = 1.0 / scaled
    for _ in range(1, sweeps):
        rho_new = 1.0 / (2.0 * scaled - rho_old)
        coeffs.append((rho_new * rho_old, 2.0 * rho_new / half_width))
        rho_old = rho_new
    return coeffs


def f32(*shape):
    return jax.ShapeDtypeStruct(shape, jnp.float32)


def call(body, outs, n_in, scratch=(), smem=(), left=(), whole=False):
    spaces = [pltpu.SMEM if i in smem else pl.ANY if i in left else pltpu.VMEM for i in range(n_in)]
    return pl.pallas_call(
        body,
        out_shape=outs,
        in_specs=[pl.BlockSpec(memory_space=space) for space in spaces],
        out_specs=jax.tree.map(lambda _: pl.BlockSpec(memory_space=pltpu.VMEM), outs),
        scratch_shapes=list(scratch),
        compiler_params=pltpu.CompilerParams(vmem_limit_bytes=VMEM_WHOLE if whole else VMEM_LIMIT),
    )


def loop(first, last, body, steps=2):
    unroll = (last - first + 1) // steps

    def step(i, carry):
        for u in range(unroll):
            body(i * unroll + u + first)
        return carry

    lax.fori_loop(0, steps, step, 0)


def lane_iota(rows):
    return lax.broadcasted_iota(jnp.int32, (rows, LANES), 1)


def z_faces(values, zlo, zhi):
    for number, value in enumerate(values):
        turned = value.T
        zlo[W * number : W * (number + 1), :] = turned[:W]
        zhi[W * number : W * (number + 1), :] = turned[LANES - W :]


def lane_pack(slices):
    rows = slices[0].shape[0]
    lane = lane_iota(rows)
    packed = jnp.zeros((rows, LANES), jnp.float32)
    for x, item in enumerate(slices):
        spot = (lane >= 2 * W * x) & (lane < 2 * W * (x + 1))
        packed = jnp.where(spot, pltpu.roll(item, (2 * W * x + W) % LANES, 1), packed)
    return packed


def lane_unpack(packed, x):
    lane = lane_iota(packed.shape[0])
    moved = pltpu.roll(packed, (2 * LANES - (2 * W * x + W)) % LANES, 1)
    return jnp.where((lane < W) | (lane >= LANES - W), moved, 0.0)


def edges(place):
    j, g, ny, nz, rows = place[0], place[1], place[2], place[3], place[4]
    return (j > 0, (j + 1) * rows < ny), (g > 0, (g + 1) * LANES < nz)


def y_part(f0, f1, rl, rr, h0, h1, ylo, yhi, near):
    X, Y, _ = f0.shape
    for number, h in enumerate((h0, h1)):
        part = slice(W * number, W * (number + 1))
        left = jnp.where(near[0], rl[part, :], 0.0)
        right = jnp.where(near[1], rr[part, :], 0.0)
        rows = jnp.concatenate([left, right], 0).T
        wide = jnp.concatenate([rows, jnp.zeros((X * Y, LANES - 2 * W), jnp.float32)], 1)
        h[...] = pltpu.roll(wide, LANES - W, 1).reshape(X, Y, LANES)
    for out, part in ((ylo, slice(0, W)), (yhi, slice(Y - W, Y))):
        out[0:X] = jnp.concatenate([f0[:, part, :], f1[:, part, :]], 1)
        out[X] = lane_pack([jnp.concatenate([h0[x, part], h1[x, part]], 0) for x in range(X)])


def fill(E, f0, f1, h0, h1, ryl, ryr, near):
    X, Y, _ = f0.shape
    for number, (f, h) in enumerate(((f0, h0), (f1, h1))):
        part = slice(W * number, W * (number + 1))
        right = jnp.where(near[1], ryr[:, part], 0.0)
        left = jnp.where(near[0], ryl[:, part], 0.0)
        both = jnp.concatenate([right, left], 1)
        E[2 * number, :, 0:Y] = f[...]
        E[2 * number, :, Y:] = both[0:X]
        E[2 * number + 1, :, 0:Y] = h[...]
        for x in range(X):
            E[2 * number + 1, x, Y:] = lane_unpack(both[X], x)


def x_face(E, start, out):
    for number in range(2):
        base = (W + 1) * number
        out[base : base + W] = E[2 * number, start : start + W]
        out[base + W] = lane_pack([E[2 * number + 1, start + x] for x in range(W)])


def static_y_body(place, table, m, p, phi, scale, labels, rl, rr, h0, h1, g0, g1, cond, ylo, yhi):
    near = edges(place)[1]
    X, Y, _ = m.shape
    TX, TY, _ = phi.shape
    cond[...] = conductivity(table, scale, labels)
    cols, rows = pl.ds(0, X * Y), pl.ds(0, X + 1)
    y_part(m, p, rl.at[:, cols], rr.at[:, cols], h0, h1, ylo.at[rows], yhi.at[rows], near)
    cols, rows = pl.ds(X * Y, TX * TY), pl.ds(X + 1, TX + 1)
    y_part(phi, cond, rl.at[:, cols], rr.at[:, cols], g0, g1, ylo.at[rows], yhi.at[rows], near)


def right_y_body(place, right, weight, rl, rr, h0, h1, ylo, yhi):
    y_part(right, weight, rl, rr, h0, h1, ylo, yhi, edges(place)[1])


def heart_x_body(place, f0, f1, h0, h1, ryl, ryr, E, high):
    X = f0.shape[0]
    rows = pl.ds(0, X + 1)
    fill(E, f0, f1, h0, h1, ryl.at[rows], ryr.at[rows], edges(place)[0])
    x_face(E, X - W, high)


def torso_x_body(place, heart, f0, f1, h0, h1, ryl, ryr, E, high, low):
    X = f0.shape[0]
    rows = pl.ds(heart.shape[1] + 1, X + 1)
    fill(E, f0, f1, h0, h1, ryl.at[rows], ryr.at[rows], edges(place)[0])
    x_face(E, X - W, high)
    x_face(heart, 0, low.at[:, pl.ds(0, heart.shape[2])])
    x_face(E, 0, low.at[:, pl.ds(heart.shape[2], E.shape[2])])


def right_x_body(place, f0, f1, h0, h1, ryl, ryr, E, low):
    fill(E, f0, f1, h0, h1, ryl, ryr, edges(place)[0])
    x_face(E, 0, low)


def from_next(value, axis):
    count = lax.axis_size(axis)
    return lax.ppermute(value, axis, [((i + 1) % count, i) for i in range(count)])


def from_last(value, axis):
    count = lax.axis_size(axis)
    return lax.ppermute(value, axis, [(i, (i + 1) % count) for i in range(count)])


def swap(value):
    return lax.all_to_all(value, ("gx", "gy"), split_axis=0, concat_axis=0, tiled=True)


def both_ways(low, high, axis):
    after = from_next(low, axis)
    return from_last(high, axis), after


def wide_of(X, Y):
    return f32(4, X, Y + 2 * W, LANES)


def face_of(rows):
    return f32(2 * (W + 1), rows + 2 * W, LANES)


def assemble(M, H, number, E, rxl, rxr):
    X = E.shape[1]
    base = (W + 1) * number
    M[0:X] = E[2 * number]
    H[0:X] = E[2 * number + 1]
    top = M.shape[0] - 2 * W
    for start, source in ((top, rxr), (top + W, rxl)):
        if source is None:
            continue
        M[start : start + W] = source[base : base + W]
        for x in range(W):
            H[start + x] = lane_unpack(source[base + W], x)


def y_next(v):
    return pltpu.roll(v, v.shape[0] - 1, 0)


def y_last(v):
    return pltpu.roll(v, 1, 0)


def z_next(m, h):
    end = lane_iota(m.shape[0]) == LANES - 1
    rm, rh = pltpu.roll(m, LANES - 1, 1), pltpu.roll(h, LANES - 1, 1)
    return jnp.where(end, rh, rm), jnp.where(end, rm, rh)


def z_last(m, h):
    end = lane_iota(m.shape[0]) == 0
    rm, rh = pltpu.roll(m, 1, 1), pltpu.roll(h, 1, 1)
    return jnp.where(end, rh, rm), jnp.where(end, rm, rh)


def wrapped(x, count):
    return jnp.where(x >= count, x - count, jnp.where(x < 0, x + count, x))


def around(M, H, x, count):
    xn, xl = wrapped(x + 1, count), wrapped(x - 1, count)
    m, h = M[x], H[x]
    zn, zl = z_next(m, h), z_last(m, h)
    sm = M[xn] + M[xl] + y_next(m) + y_last(m) + zn[0] + zl[0]
    sh = H[xn] + H[xl] + y_next(h) + y_last(h) + zn[1] + zl[1]
    return m, h, sm, sh


def gather_rows(table, index, out):
    rows_n = table.shape[0]

    def tile(i, carry):
        top = pl.multiple_of(i * 8, 8)
        for j in range(index.shape[1] // LANES):
            spot = (pl.ds(top, 8), slice(j * LANES, (j + 1) * LANES))
            where = index[spot[0], spot[1]]
            cols, rows = where & (LANES - 1), where >> 7
            total = jnp.zeros((8, LANES), jnp.float32)
            for r in range(rows_n):
                line = jnp.broadcast_to(table[r : r + 1, :], (8, LANES))
                got = jnp.take_along_axis(line, cols, axis=1, mode="promise_in_bounds")
                total = jnp.where(rows == r, got, total)
            out[spot[0], 0, spot[1]] = total
        return carry

    lax.fori_loop(0, index.shape[0] // 8, tile, 0)


def scatter_rows(value_of, index, rows_n, total, batch):
    cap = index.shape[1]
    total[...] = jnp.zeros_like(total)
    half = jnp.bfloat16

    def rows_iota(count):
        return lax.broadcasted_iota(jnp.int32, (count, cap), 0).astype(jnp.float32).astype(half)

    row_ids, col_ids = rows_iota(rows_n), rows_iota(LANES)
    ones = jnp.ones((1, cap), half)

    def hot(ids, key, weight):
        key = jnp.broadcast_to(key.astype(jnp.float32).astype(half), ids.shape)
        return jnp.where(ids == key, jnp.broadcast_to(weight, ids.shape), jnp.zeros((), half))

    def one(s):
        where = index[pl.ds(s, 1), :]
        rows, cols = where >> 7, where & (LANES - 1)
        if value_of is None:
            left = hot(row_ids, rows, ones)
        else:
            value = value_of(s)
            high = value.astype(half)
            low = (value - high.astype(jnp.float32)).astype(half)
            left = jnp.concatenate([hot(row_ids, rows, high), hot(row_ids, rows, low)], 0)
        return left, hot(col_ids, cols, ones)

    def step(i, carry):
        part = None
        for b in range(batch):
            sides = [one(i * (8 * batch) + 8 * b + k) for k in range(8)]
            product = lax.dot_general(
                jnp.concatenate([side[0] for side in sides], 1),
                jnp.concatenate([side[1] for side in sides], 1),
                (((1,), (1,)), ((), ())),
                preferred_element_type=jnp.float32,
            )
            part = product if part is None else part + product
        total[...] += part
        return carry

    lax.fori_loop(0, index.shape[0] // (8 * batch), step, 0)


def conductivity(table, scale, labels):
    picked = jnp.zeros(labels.shape, jnp.float32)
    for number in range(LABELS):
        picked = jnp.where(labels[...] == number, table[number], picked)
    return scale[...] * picked


def start_body(table, m, p, phi, scale, labels, zlo, zhi):
    X, Y, _ = m.shape
    TX, TY, _ = phi.shape
    cols, more = pl.ds(0, X * Y), pl.ds(X * Y, TX * TY)
    z_faces(
        [m[...].reshape(X * Y, LANES), p[...].reshape(X * Y, LANES)], zlo.at[:, cols], zhi.at[:, cols]
    )
    value = conductivity(table, scale, labels)
    z_faces(
        [phi[...].reshape(TX * TY, LANES), value.reshape(TX * TY, LANES)], zlo.at[:, more], zhi.at[:, more]
    )


def weight_body(index, weight, total):
    scatter_rows(None, index, total.shape[0], total, 2)
    weight[...] = (penalty * total[...]).reshape(weight.shape)


def heart_tiles(place, Y):
    j, g = place[0], place[1]
    row = lax.broadcasted_iota(jnp.int32, (Y + 2 * W, LANES), 0)
    lane = lane_iota(Y + 2 * W)
    yg = j * Y + jnp.where(row >= Y + W, row - Y - 2 * W, row)
    tiles = []
    for zl in (lane, jnp.where(lane >= LANES // 2, lane - LANES, lane + LANES)):
        zg = g * LANES + zl
        ny, nz = place[2], place[3]
        one = lambda cond: cond.astype(jnp.float32)
        inside = one((yg >= 0) & (yg < ny) & (zg >= 0) & (zg < nz))
        diag = 2.0 + one(yg + 1 < ny) + one(yg - 1 >= 0) + one(zg + 1 < nz) + one(zg - 1 >= 0)
        tiles.append((diag, inside / diag, inside))
    return tiles


def heart_surface_body(place, E, rxl, index, sent, table, mM, mH, uM, uH, wM, wH, vM, vH, fM, fH):
    S, Y = E.shape[1] // 4, E.shape[2] - 2 * W
    for number, (M, H) in enumerate(((mM, mH), (uM, uH))):
        base = (W + 1) * number
        M[0:W] = rxl[base : base + W]
        for x in range(W):
            H[x] = lane_unpack(rxl[base + W], x)
        M[W:] = E[2 * number, 0 : 2 * W]
        H[W:] = E[2 * number + 1, 0 : 2 * W]
    count = 3 * W
    (_, qm, im), (_, qh, ih) = heart_tiles(place, Y)
    ratio = intra_cond / (intra_cond + extra_cond)
    old, new = (uM, uH), (wM, wH)
    for number, (carry_coef, resid_coef) in enumerate(cheb_coeffs(SWEEPS_H)):
        reach = SWEEPS_H - 1 - number
        for x in range(W - reach, W + S + reach):
            a, b, sa, sb = around(old[0], old[1], x, count)
            if number == 0:
                c, d, sc, sd = around(mM, mH, x, count)
                fa, fb = -ratio * (c * im - sc * qm), -ratio * (d * ih - sd * qh)
                fM[x], fH[x] = fa, fb
            else:
                fa, fb = fM[x], fH[x]
            va = resid_coef * (fa + sa * qm - a)
            vb = resid_coef * (fb + sb * qh - b)
            if number > 0:
                va, vb = carry_coef * vM[x] + va, carry_coef * vH[x] + vb
            if number < SWEEPS_H - 1:
                vM[x], vH[x] = va, vb
                new[0][x], new[1][x] = a + va, b + vb
            else:
                table[(x - W) * Y : (x - W + 1) * Y, :] = (a + va)[0:Y]
        old, new = new, old

    gather_rows(table, index, sent)


def heart_body(
    place, current, E, rxl, rxr, phi_out, new_out, mM, mH, uM, uH, wM, wH, vM, vH, fM, fH
):
    X, Y, _ = phi_out.shape
    count = X + 2 * W
    near = pl.ds(0, Y + 2 * W)
    assemble(mM, mH, 0, E, rxl, rxr.at[:, near])
    assemble(uM, uH, 1, E, rxl, rxr.at[:, near])
    (dm, qm, im), (_, qh, ih) = heart_tiles(place, Y)
    ratio = intra_cond / (intra_cond + extra_cond)
    old, new = (uM, uH), (wM, wH)
    for number, (carry_coef, resid_coef) in enumerate(cheb_coeffs(SWEEPS_H)):

        def sweep(x, old=old, new=new, cc=carry_coef, rc=resid_coef, number=number):
            x = wrapped(x, count)
            a, b, sa, sb = around(old[0], old[1], x, count)
            if number == 0:
                c, d, sc, sd = around(mM, mH, x, count)
                fa, fb = -ratio * (c * im - sc * qm), -ratio * (d * ih - sd * qh)
                fM[x], fH[x] = fa, fb
            else:
                fa, fb = fM[x], fH[x]
            va = rc * (fa + sa * qm - a)
            vb = rc * (fb + sb * qh - b)
            if number > 0:
                va, vb = cc * vM[x] + va, cc * vH[x] + vb
            vM[x], vH[x] = va, vb
            new[0][x], new[1][x] = a + va, b + vb

        reach = SWEEPS_H - number
        loop(-reach, X - 1 + reach, sweep)
        old, new = new, old
    phi_out[...] = old[0][0:X, 0:Y]

    def finish(x):
        a, _, sa, _ = around(mM, mH, x, count)
        c, _, sc, _ = around(old[0], old[1], x, count)
        lap = dm * (a + c) - (sa + sc)
        new_out[x] = (a - time_step * intra_cond * lap)[0:Y] - time_step * current[x]

    loop(0, X - 1, finish)


def right_body(arrived, index, weight, right, zlo, zhi, total):
    rows = index_rows = weight.shape[0] * weight.shape[1]
    scatter_rows(lambda s: arrived[pl.ds(s, 1), 0, :], index, rows, total, 4)
    value = penalty * (total[0:rows] + total[rows : 2 * rows])
    right[...] = value.reshape(right.shape)
    z_faces([value, weight[...].reshape(index_rows, LANES)], zlo, zhi)


def faces_body(E, rxl, rxr, F, G, middle, cM, cH, aM, aH, bM, bH, vM, vH, iM, iH):
    uM, uH, fxM, fxH, fyM, fyH, fzM, fzH, dM, dH = (F.at[k] for k in range(10))
    X, rows = E.shape[1], E.shape[2]
    count = X + 2 * W
    far = pl.ds(rxr.shape[1] - rows, rows)
    assemble(uM, uH, 0, E, rxl, rxr.at[:, far])
    assemble(cM, cH, 1, E, rxl, rxr.at[:, far])

    def harmonic(a, b):
        total = a + b
        return jnp.where(total > 0.0, 2.0 * a * b / jnp.where(total > 0.0, total, 1.0), 0.0)

    def prepare(x):
        xn = wrapped(x + 1, count)
        a, b = cM[x], cH[x]
        za, zb = z_next(a, b)
        fxM[x], fxH[x] = harmonic(a, cM[xn]), harmonic(b, cH[xn])
        fyM[x], fyH[x] = harmonic(a, y_next(a)), harmonic(b, y_next(b))
        fzM[x], fzH[x] = harmonic(a, za), harmonic(b, zb)

    loop(0, count - 1, prepare, 4)

    def total(x):
        xl = wrapped(x - 1, count)
        za, zb = z_last(fzM[x], fzH[x])
        dM[x] = fxM[x] + fxM[xl] + fyM[x] + y_last(fyM[x]) + fzM[x] + za
        dH[x] = fxH[x] + fxH[xl] + fyH[x] + y_last(fyH[x]) + fzH[x] + zb

    loop(0, count - 1, total, 4)

    first = 2 * W - 1
    last = first + middle.shape[0] - 1
    old, new = (uM, uH), (aM, aH)
    for number, (carry_coef, resid_coef) in enumerate(cheb_coeffs(SWEEPS_T)):

        def sweep(x, old=old, new=new, cc=carry_coef, rc=resid_coef, number=number):
            xn, xl = x + 1, x - 1
            m, h = old[0][x], old[1][x]
            if number == 0:
                iM[x], iH[x] = reciprocal(dM[x]), reciprocal(dH[x])
            sm, sh = flow(
                m, h, old[0][xn], old[1][xn], old[0][xl], old[1][xl],
                fxM[x], fxH[x], fxM[xl], fxH[xl], fyM[x], fyH[x], fzM[x], fzH[x],
            )
            va, vb = rc * (sm * iM[x] - m), rc * (sh * iH[x] - h)
            if number > 0:
                va, vb = cc * vM[x] + va, cc * vH[x] + vb
            vM[x], vH[x] = va, vb
            new[0][x], new[1][x] = m + va, h + vb

        reach = SWEEPS_T - 1 - number
        loop(first - reach, last + reach, sweep)
        old, new = new, ((bM, bH) if number == 0 else old)
    middle[...] = old[0][first : last + 1, 0 : middle.shape[1]]
    G[...] = F[:, last + 1 - W : last + 1 - W + G.shape[1]]


def reciprocal(value):
    return jnp.where(value > 0.0, 1.0 / jnp.where(value > 0.0, value, 1.0), 0.0)


def flow(m, h, nM, nH, lM, lH, fxM, fxH, gxM, gxH, fy, gy, fz, gz):
    zn = z_next(m, h)
    zl = z_last(fz * m, gz * h)
    sm = fxM * nM + gxM * lM + fy * y_next(m) + y_last(fy * m)
    sh = fxH * nH + gxH * lH + gy * y_next(h) + y_last(gy * h)
    return sm + fz * zn[0] + zl[0], sh + gz * zn[1] + zl[1]


def torso_surface_body(
    R, index, F, surface, returned, aM, aH, bM, bH, vM, vH, iM, iH
):
    uM, uH, fxM, fxH, fyM, fyH, fzM, fzH, dM, dH = (F.at[k] for k in range(10))
    S, Y = R.shape[1], surface.shape[1]
    N = surface.shape[0]
    count = F.shape[1]
    old, new = None, (aM, aH)
    for number, (carry_coef, resid_coef) in enumerate(cheb_coeffs(SWEEPS_T)):
        reach = SWEEPS_T - 1 - number

        def value(x, tile, old=old):
            return (uM, uH)[tile][x % count] if old is None else old[tile][x + W]

        for x in range(-reach, N + reach):
            at, last = x % count, (x - 1) % count
            m, h = value(x, 0), value(x, 1)
            sm, sh = flow(
                m, h, value(x + 1, 0), value(x + 1, 1), value(x - 1, 0), value(x - 1, 1),
                fxM[at], fxH[at], fxM[last], fxH[last], fyM[at], fyH[at], fzM[at], fzH[at],
            )
            inside = 0 <= x < S
            if number == 0:
                wm, wh = dM[at], dH[at]
                if inside:
                    wm, wh = wm + R[2, x], wh + R[3, x]
                wm, wh = reciprocal(wm), reciprocal(wh)
                iM[x + W], iH[x + W] = wm, wh
            else:
                wm, wh = iM[x + W], iH[x + W]
            if inside:
                sm, sh = sm + R[0, x], sh + R[1, x]
            va, vb = resid_coef * (sm * wm - m), resid_coef * (sh * wh - h)
            if number > 0:
                va, vb = carry_coef * vM[x + W] + va, carry_coef * vH[x + W] + vb
            if number < SWEEPS_T - 1:
                vM[x + W], vH[x + W] = va, vb
                new[0][x + W], new[1][x + W] = m + va, h + vb
            else:
                surface[x] = (m + va)[0:Y]
        old, new = new, ((bM, bH) if number == 0 else old)
    table = surface[0:S].reshape(S * Y, LANES)

    gather_rows(table, index, returned)


def torso_body(
    surface, middle, rxr, G, torso_out, aM, aH, bM, bH, vM, vH, iM, iH
):
    N, M = surface.shape[0], middle.shape[0]
    X, Y, _ = torso_out.shape
    first = N + M - W
    torso_out[0:N] = surface[...]
    torso_out[N : N + M] = middle[...]
    uM, uH, fxM, fxH, fyM, fyH, fzM, fzH, dM, dH = (G.at[k] for k in range(10))
    old, new = (uM, uH), (aM, aH)
    for number, (carry_coef, resid_coef) in enumerate(cheb_coeffs(SWEEPS_T)):
        reach = SWEEPS_T - 1 - number
        for x in range(N + M - reach, X + reach):
            at = x - first
            m, h = old[0][at], old[1][at]
            sm, sh = flow(
                m, h, old[0][at + 1], old[1][at + 1], old[0][at - 1], old[1][at - 1],
                fxM[at], fxH[at], fxM[at - 1], fxH[at - 1], fyM[at], fyH[at], fzM[at], fzH[at],
            )
            beyond = x - X
            if number == 0:
                wm, wh = dM[at], dH[at]
                if beyond >= 0:
                    wm = wm + rxr[W + 1 + beyond]
                    wh = wh + lane_unpack(rxr[2 * W + 1], beyond)
                wm, wh = reciprocal(wm), reciprocal(wh)
                iM[at], iH[at] = wm, wh
            else:
                wm, wh = iM[at], iH[at]
            if beyond >= 0:
                sm = sm + rxr[beyond]
                sh = sh + lane_unpack(rxr[W], beyond)
            va, vb = resid_coef * (sm * wm - m), resid_coef * (sh * wh - h)
            if number > 0:
                va, vb = carry_coef * vM[at] + va, carry_coef * vH[at] + vb
            if number < SWEEPS_T - 1:
                vM[at], vH[at] = va, vb
                new[0][at], new[1][at] = m + va, h + vb
            else:
                torso_out[x] = (m + va)[0:Y]
        old, new = new, ((bM, bH) if number == 0 else old)


def final_body(place, sent, back, index, phi, out, total):
    X, Y, _ = phi.shape
    rows = X // 4 * Y
    scatter_rows(
        lambda s: penalty * (sent[pl.ds(s, 1), 0, :] - back[pl.ds(s, 1), 0, :]), index, rows, total, 2
    )
    flux = (total[0:rows] + total[rows : 2 * rows]).reshape(X // 4, Y, LANES)
    (dm, _, _), _ = heart_tiles(place, Y)
    out[X // 4 :] = phi[X // 4 :]
    scale = (1.0 / ((intra_cond + extra_cond) * dm))[0:Y]
    for x in range(X // 4):
        out[x] = phi[x] - flux[x] * scale


def ionic_current(states, membrane, ion_params):
    params_col = ion_params[:, :, None, None, None]
    gate_vals = states.astype(jnp.float32)
    voltage = membrane[None]
    steady = jax.nn.sigmoid((voltage - params_col[0]) / params_col[1])
    gate_vals = steady + (gate_vals - steady) * jnp.exp(-time_step * params_col[2])
    return jnp.sum(params_col[3] * gate_vals * (voltage - params_col[4]), axis=0)


def per_device(
    states, membrane, phi_heart, ion_params, torso_phi, tissue_scale, labels, cond_table,
    send_node, send_count, recv_voxel, recv_count,
):
    X, Y, _ = membrane.shape
    TX, TY, _ = torso_phi.shape
    peers = lax.axis_size("gx") * lax.axis_size("gy")
    cap = send_node.shape[-1]
    place = jnp.stack([
        lax.axis_index("gy"), lax.axis_index("grp"),
        jnp.int32(Y * lax.axis_size("gy")), jnp.int32(LANES * lax.axis_size("grp")), jnp.int32(Y),
    ])
    slots = jnp.arange(cap, dtype=jnp.int32)[None, :]
    send_index = jnp.where(slots < send_count.reshape(peers, 1), send_node.reshape(peers, cap), -1)
    recv_index = jnp.where(slots < recv_count.reshape(peers, 1), recv_voxel.reshape(peers, cap), -1)

    S = TX // 4
    wide = f32(2 * W, X * Y + TX * TY)
    zlo, zhi = call(start_body, (wide, wide), 6, smem=(0,), whole=True)(
        cond_table, membrane, phi_heart, torso_phi, tissue_scale, labels
    )
    weight = call(
        weight_body, f32(S, TY, LANES), 1, scratch=[pltpu.VMEM((S * TY, LANES), jnp.float32)]
    )(recv_index)
    current = ionic_current(states, membrane, ion_params)

    hbox, tbox, tall = f32(X, Y, LANES), f32(TX, TY, LANES), f32(X + TX + 2, 2 * W, LANES)
    *halos, cond, ylo, yhi = call(
        static_y_body, (hbox, hbox, tbox, tbox, tbox, tall, tall), 9, smem=(0, 1),
    )(
        place, cond_table, membrane, phi_heart, torso_phi, tissue_scale, labels,
        *both_ways(zlo, zhi, "grp"),
    )
    heart, torso = (membrane, phi_heart), (torso_phi, cond)
    ryl, ryr = both_ways(ylo, yhi, "gy")
    heart_wide, high = call(
        heart_x_body, (wide_of(X, Y), face_of(Y)), 7, smem=(0,)
    )(place, *heart, *halos[:2], ryl, ryr)
    hxl = from_last(high, "gx")
    torso_wide, high, low = call(
        torso_x_body, (wide_of(TX, TY), face_of(TY), face_of(Y + 2 * W + TY)), 8,
        smem=(0,),
    )(place, heart_wide, *torso, *halos[2:], ryl, ryr)
    txl, xr = from_last(high, "gx"), from_next(low, "gx")

    thin = pltpu.VMEM((3 * W, Y + 2 * W, LANES), jnp.float32)
    sent = call(
        heart_surface_body, f32(peers, 1, cap), 4,
        scratch=[pltpu.VMEM((X // 4 * Y, LANES), jnp.float32)] + [thin] * 10, smem=(0,),
    )(place, heart_wide, hxl, send_index)
    arrived = swap(sent)

    ext = pltpu.VMEM((X + 2 * W, Y + 2 * W, LANES), jnp.float32)
    phi_new, new_membrane = call(
        heart_body, (f32(X, Y, LANES), f32(X, Y, LANES)), 5,
        scratch=[ext] * 10, smem=(0,),
    )(place, current, heart_wide, hxl, xr)
    right, rzlo, rzhi = call(
        right_body,
        (f32(S, TY, LANES), f32(2 * W, S * TY), f32(2 * W, S * TY)),
        3, scratch=[pltpu.VMEM((2 * S * TY, LANES), jnp.float32)],
    )(arrived, recv_index, weight)
    text = (TX + 2 * W, TY + 2 * W, LANES)
    big = pltpu.VMEM(text, jnp.float32)
    N = S + SWEEPS_T - 1
    middle_n = TX - S - 2 * (SWEEPS_T - 1)
    last_n = TX - N - middle_n + 2 * W
    faces, last_faces, middle = call(
        faces_body,
        (f32(10, *text), f32(10, last_n, *text[1:]), f32(middle_n, TY, LANES)),
        3, scratch=[big] * 10,
    )(torso_wide, txl, xr)
    tall = f32(S + 1, 2 * W, LANES)
    *halos, ylo, yhi = call(
        right_y_body, (f32(S, TY, LANES),) * 2 + (tall, tall), 5, smem=(0,),
    )(place, right, weight, *both_ways(rzlo, rzhi, "grp"))
    ryl, ryr = both_ways(ylo, yhi, "gy")
    right_wide, low = call(
        right_x_body, (wide_of(S, TY), face_of(TY)), 7, smem=(0,)
    )(place, right, weight, *halos, ryl, ryr)
    rxr = from_next(low, "gx")
    flat = pltpu.VMEM((N + 2 * W, TY + 2 * W, LANES), jnp.float32)
    surface, returned = call(
        torso_surface_body, (f32(N, TY, LANES), f32(peers, 1, cap)), 3,
        scratch=[flat] * 8,
    )(right_wide, recv_index, faces)
    back = swap(returned)
    thin = pltpu.VMEM((last_n, TY + 2 * W, LANES), jnp.float32)
    torso_out = call(
        torso_body, f32(TX, TY, LANES), 4,
        scratch=[thin] * 8,
    )(surface, middle, rxr, last_faces)
    heart_phi = call(
        final_body, f32(X, Y, LANES), 5,
        scratch=[pltpu.VMEM((2 * X // 4 * Y, LANES), jnp.float32)], smem=(0,),
    )(place, sent, back, send_index, phi_new)
    return (new_membrane, heart_phi, torso_out)


def solution(mesh):
    placed = (
        P(None, "gx", "gy", "grp"),
        P("gx", "gy", "grp"),
        P("gx", "gy", "grp"),
        P(),
        P("gx", "gy", "grp"),
        P("gx", "gy", "grp"),
        P("gx", "gy", "grp"),
        P(),
        P("grp", "gx", "gy", None, None),
        P("grp", "gx", "gy", None),
        P("grp", "gx", "gy", None, None),
        P("grp", "gx", "gy", None),
    )
    return jax.shard_map(
        per_device,
        mesh=mesh,
        in_specs=placed,
        out_specs=(P("gx", "gy", "grp"), P("gx", "gy", "grp"), P("gx", "gy", "grp")),
        check_vma=False,
    )
```

```python
import jax
import jax.numpy as jnp
from jax import lax
from jax.experimental import pallas as pl
from jax.experimental.pallas import tpu as pltpu
from jax.sharding import PartitionSpec as P


LABELS = 4
SWEEPS_H = 3
SWEEPS_T = 4
W = 4
LANES = 128

time_step = 0.1
intra_cond = 0.25
extra_cond = 0.5
penalty = 2.0
cheb_low = 0.1
cheb_high = 2.0
VMEM_LIMIT = 24 << 20
VMEM_WHOLE = 60 * 1024 * 1024


def cheb_coeffs(sweeps):
    centre = 0.5 * (cheb_high + cheb_low)
    half_width = 0.5 * (cheb_high - cheb_low)
    scaled = centre / half_width
    coeffs = [(0.0, 1.0 / centre)]
    rho_old = 1.0 / scaled
    for _ in range(1, sweeps):
        rho_new = 1.0 / (2.0 * scaled - rho_old)
        coeffs.append((rho_new * rho_old, 2.0 * rho_new / half_width))
        rho_old = rho_new
    return coeffs


def f32(*shape):
    return jax.ShapeDtypeStruct(shape, jnp.float32)


def call(body, outs, n_in, scratch=(), smem=(), left=(), whole=False):
    spaces = [pltpu.SMEM if i in smem else pl.ANY if i in left else pltpu.VMEM for i in range(n_in)]
    return pl.pallas_call(
        body,
        out_shape=outs,
        in_specs=[pl.BlockSpec(memory_space=space) for space in spaces],
        out_specs=jax.tree.map(lambda _: pl.BlockSpec(memory_space=pltpu.VMEM), outs),
        scratch_shapes=list(scratch),
        compiler_params=pltpu.CompilerParams(vmem_limit_bytes=VMEM_WHOLE if whole else VMEM_LIMIT),
    )


def loop(first, last, body, steps=2):
    unroll = (last - first + 1) // steps

    def step(i, carry):
        for u in range(unroll):
            body(i * unroll + u + first)
        return carry

    lax.fori_loop(0, steps, step, 0)


def lane_iota(rows):
    return lax.broadcasted_iota(jnp.int32, (rows, LANES), 1)


def z_faces(values, zlo, zhi):
    for number, value in enumerate(values):
        turned = value.T
        zlo[W * number : W * (number + 1), :] = turned[:W]
        zhi[W * number : W * (number + 1), :] = turned[LANES - W :]


def lane_pack(slices):
    rows = slices[0].shape[0]
    lane = lane_iota(rows)
    packed = jnp.zeros((rows, LANES), jnp.float32)
    for x, item in enumerate(slices):
        spot = (lane >= 2 * W * x) & (lane < 2 * W * (x + 1))
        packed = jnp.where(spot, pltpu.roll(item, (2 * W * x + W) % LANES, 1), packed)
    return packed


def lane_unpack(packed, x):
    lane = lane_iota(packed.shape[0])
    moved = pltpu.roll(packed, (2 * LANES - (2 * W * x + W)) % LANES, 1)
    return jnp.where((lane < W) | (lane >= LANES - W), moved, 0.0)


def edges(place):
    j, g, ny, nz, rows = place[0], place[1], place[2], place[3], place[4]
    return (j > 0, (j + 1) * rows < ny), (g > 0, (g + 1) * LANES < nz)


def y_part(f0, f1, rl, rr, h0, h1, ylo, yhi, near):
    X, Y, _ = f0.shape
    for number, h in enumerate((h0, h1)):
        part = slice(W * number, W * (number + 1))
        left = jnp.where(near[0], rl[part, :], 0.0)
        right = jnp.where(near[1], rr[part, :], 0.0)
        rows = jnp.concatenate([left, right], 0).T
        wide = jnp.concatenate([rows, jnp.zeros((X * Y, LANES - 2 * W), jnp.float32)], 1)
        h[...] = pltpu.roll(wide, LANES - W, 1).reshape(X, Y, LANES)
    for out, part in ((ylo, slice(0, W)), (yhi, slice(Y - W, Y))):
        out[0:X] = jnp.concatenate([f0[:, part, :], f1[:, part, :]], 1)
        out[X] = lane_pack([jnp.concatenate([h0[x, part], h1[x, part]], 0) for x in range(X)])


def fill(E, f0, f1, h0, h1, ryl, ryr, near):
    X, Y, _ = f0.shape
    for number, (f, h) in enumerate(((f0, h0), (f1, h1))):
        part = slice(W * number, W * (number + 1))
        right = jnp.where(near[1], ryr[:, part], 0.0)
        left = jnp.where(near[0], ryl[:, part], 0.0)
        both = jnp.concatenate([right, left], 1)
        E[2 * number, :, 0:Y] = f[...]
        E[2 * number, :, Y:] = both[0:X]
        E[2 * number + 1, :, 0:Y] = h[...]
        for x in range(X):
            E[2 * number + 1, x, Y:] = lane_unpack(both[X], x)


def x_face(E, start, out):
    for number in range(2):
        base = (W + 1) * number
        out[base : base + W] = E[2 * number, start : start + W]
        out[base + W] = lane_pack([E[2 * number + 1, start + x] for x in range(W)])


def static_y_body(place, table, m, p, phi, scale, labels, rl, rr, h0, h1, g0, g1, cond, ylo, yhi):
    near = edges(place)[1]
    X, Y, _ = m.shape
    TX, TY, _ = phi.shape
    cond[...] = conductivity(table, scale, labels)
    cols, rows = pl.ds(0, X * Y), pl.ds(0, X + 1)
    y_part(m, p, rl.at[:, cols], rr.at[:, cols], h0, h1, ylo.at[rows], yhi.at[rows], near)
    cols, rows = pl.ds(X * Y, TX * TY), pl.ds(X + 1, TX + 1)
    y_part(phi, cond, rl.at[:, cols], rr.at[:, cols], g0, g1, ylo.at[rows], yhi.at[rows], near)


def right_y_body(place, right, weight, rl, rr, h0, h1, ylo, yhi):
    y_part(right, weight, rl, rr, h0, h1, ylo, yhi, edges(place)[1])


def heart_x_body(place, f0, f1, h0, h1, ryl, ryr, E, high):
    X = f0.shape[0]
    rows = pl.ds(0, X + 1)
    fill(E, f0, f1, h0, h1, ryl.at[rows], ryr.at[rows], edges(place)[0])
    x_face(E, X - W, high)


def torso_x_body(place, heart, f0, f1, h0, h1, ryl, ryr, E, high, low):
    X = f0.shape[0]
    rows = pl.ds(heart.shape[1] + 1, X + 1)
    fill(E, f0, f1, h0, h1, ryl.at[rows], ryr.at[rows], edges(place)[0])
    x_face(E, X - W, high)
    x_face(heart, 0, low.at[:, pl.ds(0, heart.shape[2])])
    x_face(E, 0, low.at[:, pl.ds(heart.shape[2], E.shape[2])])


def right_x_body(place, f0, f1, h0, h1, ryl, ryr, E, low):
    fill(E, f0, f1, h0, h1, ryl, ryr, edges(place)[0])
    x_face(E, 0, low)


def from_next(value, axis):
    count = lax.axis_size(axis)
    return lax.ppermute(value, axis, [((i + 1) % count, i) for i in range(count)])


def from_last(value, axis):
    count = lax.axis_size(axis)
    return lax.ppermute(value, axis, [(i, (i + 1) % count) for i in range(count)])


def swap(value):
    return lax.all_to_all(value, ("gx", "gy"), split_axis=0, concat_axis=0, tiled=True)


def both_ways(low, high, axis):
    after = from_next(low, axis)
    return from_last(high, axis), after


def wide_of(X, Y):
    return f32(4, X, Y + 2 * W, LANES)


def face_of(rows):
    return f32(2 * (W + 1), rows + 2 * W, LANES)


def assemble(M, H, number, E, rxl, rxr):
    X = E.shape[1]
    base = (W + 1) * number
    M[0:X] = E[2 * number]
    H[0:X] = E[2 * number + 1]
    top = M.shape[0] - 2 * W
    for start, source in ((top, rxr), (top + W, rxl)):
        if source is None:
            continue
        M[start : start + W] = source[base : base + W]
        for x in range(W):
            H[start + x] = lane_unpack(source[base + W], x)


def y_next(v):
    return pltpu.roll(v, v.shape[0] - 1, 0)


def y_last(v):
    return pltpu.roll(v, 1, 0)


def z_next(m, h):
    end = lane_iota(m.shape[0]) == LANES - 1
    rm, rh = pltpu.roll(m, LANES - 1, 1), pltpu.roll(h, LANES - 1, 1)
    return jnp.where(end, rh, rm), jnp.where(end, rm, rh)


def z_last(m, h):
    end = lane_iota(m.shape[0]) == 0
    rm, rh = pltpu.roll(m, 1, 1), pltpu.roll(h, 1, 1)
    return jnp.where(end, rh, rm), jnp.where(end, rm, rh)


def wrapped(x, count):
    return jnp.where(x >= count, x - count, jnp.where(x < 0, x + count, x))


def around(M, H, x, count):
    xn, xl = wrapped(x + 1, count), wrapped(x - 1, count)
    m, h = M[x], H[x]
    zn, zl = z_next(m, h), z_last(m, h)
    sm = M[xn] + M[xl] + y_next(m) + y_last(m) + zn[0] + zl[0]
    sh = H[xn] + H[xl] + y_next(h) + y_last(h) + zn[1] + zl[1]
    return m, h, sm, sh


def gather_rows(table, index, out):
    rows_n = table.shape[0]

    def tile(i):
        top = pl.multiple_of(i * 8, 8)
        for j in range(index.shape[1] // LANES):
            spot = (pl.ds(top, 8), slice(j * LANES, (j + 1) * LANES))
            where = index[spot[0], spot[1]]
            cols, rows = where & (LANES - 1), where >> 7
            total = jnp.zeros((8, LANES), jnp.float32)
            for r in range(rows_n):
                line = jnp.broadcast_to(table[r : r + 1, :], (8, LANES))
                got = jnp.take_along_axis(line, cols, axis=1, mode="promise_in_bounds")
                total = jnp.where(rows == r, got, total)
            out[spot[0], 0, spot[1]] = total

    loop(0, index.shape[0] // 8 - 1, tile, 2)


def scatter_rows(value_of, index, rows_n, total, batch):
    cap = index.shape[1]
    total[...] = jnp.zeros_like(total)
    half = jnp.bfloat16

    def rows_iota(count):
        return lax.broadcasted_iota(jnp.int32, (count, cap), 0).astype(jnp.float32).astype(half)

    row_ids, col_ids = rows_iota(rows_n), rows_iota(LANES)
    ones = jnp.ones((1, cap), half)

    def hot(ids, key, weight):
        key = jnp.broadcast_to(key.astype(jnp.float32).astype(half), ids.shape)
        return jnp.where(ids == key, jnp.broadcast_to(weight, ids.shape), jnp.zeros((), half))

    def one(s):
        where = index[pl.ds(s, 1), :]
        rows, cols = where >> 7, where & (LANES - 1)
        if value_of is None:
            left = hot(row_ids, rows, ones)
        else:
            value = value_of(s)
            high = value.astype(half)
            low = (value - high.astype(jnp.float32)).astype(half)
            left = jnp.concatenate([hot(row_ids, rows, high), hot(row_ids, rows, low)], 0)
        return left, hot(col_ids, cols, ones)

    def step(i, carry):
        part = None
        for b in range(batch):
            sides = [one(i * (8 * batch) + 8 * b + k) for k in range(8)]
            product = lax.dot_general(
                jnp.concatenate([side[0] for side in sides], 1),
                jnp.concatenate([side[1] for side in sides], 1),
                (((1,), (1,)), ((), ())),
                preferred_element_type=jnp.float32,
            )
            part = product if part is None else part + product
        total[...] += part
        return carry

    lax.fori_loop(0, index.shape[0] // (8 * batch), step, 0)


def conductivity(table, scale, labels):
    picked = jnp.zeros(labels.shape, jnp.float32)
    for number in range(LABELS):
        picked = jnp.where(labels[...] == number, table[number], picked)
    return scale[...] * picked


def start_body(table, m, p, phi, scale, labels, zlo, zhi):
    X, Y, _ = m.shape
    TX, TY, _ = phi.shape
    cols, more = pl.ds(0, X * Y), pl.ds(X * Y, TX * TY)
    z_faces(
        [m[...].reshape(X * Y, LANES), p[...].reshape(X * Y, LANES)], zlo.at[:, cols], zhi.at[:, cols]
    )
    value = conductivity(table, scale, labels)
    z_faces(
        [phi[...].reshape(TX * TY, LANES), value.reshape(TX * TY, LANES)], zlo.at[:, more], zhi.at[:, more]
    )


def weight_body(index, weight, total):
    scatter_rows(None, index, total.shape[0], total, 4)
    weight[...] = (penalty * total[...]).reshape(weight.shape)


def heart_tiles(place, Y):
    j, g = place[0], place[1]
    row = lax.broadcasted_iota(jnp.int32, (Y + 2 * W, LANES), 0)
    lane = lane_iota(Y + 2 * W)
    yg = j * Y + jnp.where(row >= Y + W, row - Y - 2 * W, row)
    tiles = []
    for zl in (lane, jnp.where(lane >= LANES // 2, lane - LANES, lane + LANES)):
        zg = g * LANES + zl
        ny, nz = place[2], place[3]
        one = lambda cond: cond.astype(jnp.float32)
        inside = one((yg >= 0) & (yg < ny) & (zg >= 0) & (zg < nz))
        diag = 2.0 + one(yg + 1 < ny) + one(yg - 1 >= 0) + one(zg + 1 < nz) + one(zg - 1 >= 0)
        tiles.append((diag, inside / diag, inside))
    return tiles


def heart_surface_body(place, E, rxl, index, sent, table, mM, mH, uM, uH, wM, wH, vM, vH, fM, fH):
    S, Y = E.shape[1] // 4, E.shape[2] - 2 * W
    for number, (M, H) in enumerate(((mM, mH), (uM, uH))):
        base = (W + 1) * number
        M[0:W] = rxl[base : base + W]
        for x in range(W):
            H[x] = lane_unpack(rxl[base + W], x)
        M[W:] = E[2 * number, 0 : 2 * W]
        H[W:] = E[2 * number + 1, 0 : 2 * W]
    count = 3 * W
    (_, qm, im), (_, qh, ih) = heart_tiles(place, Y)
    ratio = intra_cond / (intra_cond + extra_cond)
    old, new = (uM, uH), (wM, wH)
    for number, (carry_coef, resid_coef) in enumerate(cheb_coeffs(SWEEPS_H)):
        reach = SWEEPS_H - 1 - number
        for x in range(W - reach, W + S + reach):
            a, b, sa, sb = around(old[0], old[1], x, count)
            if number == 0:
                c, d, sc, sd = around(mM, mH, x, count)
                fa, fb = -ratio * (c * im - sc * qm), -ratio * (d * ih - sd * qh)
                fM[x], fH[x] = fa, fb
            else:
                fa, fb = fM[x], fH[x]
            va = resid_coef * (fa + sa * qm - a)
            vb = resid_coef * (fb + sb * qh - b)
            if number > 0:
                va, vb = carry_coef * vM[x] + va, carry_coef * vH[x] + vb
            if number < SWEEPS_H - 1:
                vM[x], vH[x] = va, vb
                new[0][x], new[1][x] = a + va, b + vb
            else:
                table[(x - W) * Y : (x - W + 1) * Y, :] = (a + va)[0:Y]
        old, new = new, old

    gather_rows(table, index, sent)


def heart_body(
    place, current, E, rxl, rxr, phi_out, new_out, mM, mH, uM, uH, wM, wH, vM, vH, fM, fH
):
    X, Y, _ = phi_out.shape
    count = X + 2 * W
    near = pl.ds(0, Y + 2 * W)
    assemble(mM, mH, 0, E, rxl, rxr.at[:, near])
    assemble(uM, uH, 1, E, rxl, rxr.at[:, near])
    (dm, qm, im), (_, qh, ih) = heart_tiles(place, Y)
    ratio = intra_cond / (intra_cond + extra_cond)
    old, new = (uM, uH), (wM, wH)
    for number, (carry_coef, resid_coef) in enumerate(cheb_coeffs(SWEEPS_H)):

        def sweep(x, old=old, new=new, cc=carry_coef, rc=resid_coef, number=number):
            x = wrapped(x, count)
            a, b, sa, sb = around(old[0], old[1], x, count)
            if number == 0:
                c, d, sc, sd = around(mM, mH, x, count)
                fa, fb = -ratio * (c * im - sc * qm), -ratio * (d * ih - sd * qh)
                fM[x], fH[x] = fa, fb
            else:
                fa, fb = fM[x], fH[x]
            va = rc * (fa + sa * qm - a)
            vb = rc * (fb + sb * qh - b)
            if number > 0:
                va, vb = cc * vM[x] + va, cc * vH[x] + vb
            vM[x], vH[x] = va, vb
            new[0][x], new[1][x] = a + va, b + vb

        reach = SWEEPS_H - number
        loop(-reach, X - 1 + reach, sweep)
        old, new = new, old
    phi_out[...] = old[0][0:X, 0:Y]

    def finish(x):
        a, _, sa, _ = around(mM, mH, x, count)
        c, _, sc, _ = around(old[0], old[1], x, count)
        lap = dm * (a + c) - (sa + sc)
        new_out[x] = (a - time_step * intra_cond * lap)[0:Y] - time_step * current[x]

    loop(0, X - 1, finish)


def right_body(arrived, index, weight, right, zlo, zhi, total):
    rows = index_rows = weight.shape[0] * weight.shape[1]
    scatter_rows(lambda s: arrived[pl.ds(s, 1), 0, :], index, rows, total, 8)
    value = penalty * (total[0:rows] + total[rows : 2 * rows])
    right[...] = value.reshape(right.shape)
    z_faces([value, weight[...].reshape(index_rows, LANES)], zlo, zhi)


def faces_body(E, rxl, rxr, F, G, middle, cM, cH, aM, aH, bM, bH, vM, vH, iM, iH):
    uM, uH, fxM, fxH, fyM, fyH, fzM, fzH, dM, dH = (F.at[k] for k in range(10))
    X, rows = E.shape[1], E.shape[2]
    count = X + 2 * W
    far = pl.ds(rxr.shape[1] - rows, rows)
    assemble(uM, uH, 0, E, rxl, rxr.at[:, far])
    assemble(cM, cH, 1, E, rxl, rxr.at[:, far])

    def harmonic(a, b):
        total = a + b
        return jnp.where(total > 0.0, 2.0 * a * b / jnp.where(total > 0.0, total, 1.0), 0.0)

    def prepare(x):
        xn = wrapped(x + 1, count)
        a, b = cM[x], cH[x]
        za, zb = z_next(a, b)
        fxM[x], fxH[x] = harmonic(a, cM[xn]), harmonic(b, cH[xn])
        fyM[x], fyH[x] = harmonic(a, y_next(a)), harmonic(b, y_next(b))
        fzM[x], fzH[x] = harmonic(a, za), harmonic(b, zb)

    loop(0, count - 1, prepare, 4)

    def total(x):
        xl = wrapped(x - 1, count)
        za, zb = z_last(fzM[x], fzH[x])
        dM[x] = fxM[x] + fxM[xl] + fyM[x] + y_last(fyM[x]) + fzM[x] + za
        dH[x] = fxH[x] + fxH[xl] + fyH[x] + y_last(fyH[x]) + fzH[x] + zb

    loop(0, count - 1, total, 4)

    first = 2 * W - 1
    last = first + middle.shape[0] - 1
    old, new = (uM, uH), (aM, aH)
    for number, (carry_coef, resid_coef) in enumerate(cheb_coeffs(SWEEPS_T)):

        def sweep(x, old=old, new=new, cc=carry_coef, rc=resid_coef, number=number):
            xn, xl = x + 1, x - 1
            m, h = old[0][x], old[1][x]
            if number == 0:
                iM[x], iH[x] = reciprocal(dM[x]), reciprocal(dH[x])
            sm, sh = flow(
                m, h, old[0][xn], old[1][xn], old[0][xl], old[1][xl],
                fxM[x], fxH[x], fxM[xl], fxH[xl], fyM[x], fyH[x], fzM[x], fzH[x],
            )
            va, vb = rc * (sm * iM[x] - m), rc * (sh * iH[x] - h)
            if number > 0:
                va, vb = cc * vM[x] + va, cc * vH[x] + vb
            vM[x], vH[x] = va, vb
            new[0][x], new[1][x] = m + va, h + vb

        reach = SWEEPS_T - 1 - number
        loop(first - reach, last + reach, sweep)
        old, new = new, ((bM, bH) if number == 0 else old)
    middle[...] = old[0][first : last + 1, 0 : middle.shape[1]]
    G[...] = F[:, last + 1 - W : last + 1 - W + G.shape[1]]


def reciprocal(value):
    return jnp.where(value > 0.0, 1.0 / jnp.where(value > 0.0, value, 1.0), 0.0)


def flow(m, h, nM, nH, lM, lH, fxM, fxH, gxM, gxH, fy, gy, fz, gz):
    zn = z_next(m, h)
    zl = z_last(fz * m, gz * h)
    sm = fxM * nM + gxM * lM + fy * y_next(m) + y_last(fy * m)
    sh = fxH * nH + gxH * lH + gy * y_next(h) + y_last(gy * h)
    return sm + fz * zn[0] + zl[0], sh + gz * zn[1] + zl[1]


def torso_surface_body(
    R, index, F, surface, returned, aM, aH, bM, bH, vM, vH, iM, iH
):
    uM, uH, fxM, fxH, fyM, fyH, fzM, fzH, dM, dH = (F.at[k] for k in range(10))
    S, Y = R.shape[1], surface.shape[1]
    N = surface.shape[0]
    count = F.shape[1]
    old, new = None, (aM, aH)
    for number, (carry_coef, resid_coef) in enumerate(cheb_coeffs(SWEEPS_T)):
        reach = SWEEPS_T - 1 - number

        def value(x, tile, old=old):
            return (uM, uH)[tile][x % count] if old is None else old[tile][x + W]

        for x in range(-reach, N + reach):
            at, last = x % count, (x - 1) % count
            m, h = value(x, 0), value(x, 1)
            sm, sh = flow(
                m, h, value(x + 1, 0), value(x + 1, 1), value(x - 1, 0), value(x - 1, 1),
                fxM[at], fxH[at], fxM[last], fxH[last], fyM[at], fyH[at], fzM[at], fzH[at],
            )
            inside = 0 <= x < S
            if number == 0:
                wm, wh = dM[at], dH[at]
                if inside:
                    wm, wh = wm + R[2, x], wh + R[3, x]
                wm, wh = reciprocal(wm), reciprocal(wh)
                iM[x + W], iH[x + W] = wm, wh
            else:
                wm, wh = iM[x + W], iH[x + W]
            if inside:
                sm, sh = sm + R[0, x], sh + R[1, x]
            va, vb = resid_coef * (sm * wm - m), resid_coef * (sh * wh - h)
            if number > 0:
                va, vb = carry_coef * vM[x + W] + va, carry_coef * vH[x + W] + vb
            if number < SWEEPS_T - 1:
                vM[x + W], vH[x + W] = va, vb
                new[0][x + W], new[1][x + W] = m + va, h + vb
            else:
                surface[x] = (m + va)[0:Y]
        old, new = new, ((bM, bH) if number == 0 else old)
    table = surface[0:S].reshape(S * Y, LANES)

    gather_rows(table, index, returned)


def torso_body(
    surface, middle, rxr, G, torso_out, aM, aH, bM, bH, vM, vH, iM, iH
):
    N, M = surface.shape[0], middle.shape[0]
    X, Y, _ = torso_out.shape
    first = N + M - W
    torso_out[0:N] = surface[...]
    torso_out[N : N + M] = middle[...]
    uM, uH, fxM, fxH, fyM, fyH, fzM, fzH, dM, dH = (G.at[k] for k in range(10))
    old, new = (uM, uH), (aM, aH)
    for number, (carry_coef, resid_coef) in enumerate(cheb_coeffs(SWEEPS_T)):
        reach = SWEEPS_T - 1 - number
        for x in range(N + M - reach, X + reach):
            at = x - first
            m, h = old[0][at], old[1][at]
            sm, sh = flow(
                m, h, old[0][at + 1], old[1][at + 1], old[0][at - 1], old[1][at - 1],
                fxM[at], fxH[at], fxM[at - 1], fxH[at - 1], fyM[at], fyH[at], fzM[at], fzH[at],
            )
            beyond = x - X
            if number == 0:
                wm, wh = dM[at], dH[at]
                if beyond >= 0:
                    wm = wm + rxr[W + 1 + beyond]
                    wh = wh + lane_unpack(rxr[2 * W + 1], beyond)
                wm, wh = reciprocal(wm), reciprocal(wh)
                iM[at], iH[at] = wm, wh
            else:
                wm, wh = iM[at], iH[at]
            if beyond >= 0:
                sm = sm + rxr[beyond]
                sh = sh + lane_unpack(rxr[W], beyond)
            va, vb = resid_coef * (sm * wm - m), resid_coef * (sh * wh - h)
            if number > 0:
                va, vb = carry_coef * vM[at] + va, carry_coef * vH[at] + vb
            if number < SWEEPS_T - 1:
                vM[at], vH[at] = va, vb
                new[0][at], new[1][at] = m + va, h + vb
            else:
                torso_out[x] = (m + va)[0:Y]
        old, new = new, ((bM, bH) if number == 0 else old)


def final_body(place, sent, back, index, phi, out, total):
    X, Y, _ = phi.shape
    rows = X // 4 * Y
    scatter_rows(
        lambda s: penalty * (sent[pl.ds(s, 1), 0, :] - back[pl.ds(s, 1), 0, :]), index, rows, total, 4
    )
    flux = (total[0:rows] + total[rows : 2 * rows]).reshape(X // 4, Y, LANES)
    (dm, _, _), _ = heart_tiles(place, Y)
    out[X // 4 :] = phi[X // 4 :]
    scale = (1.0 / ((intra_cond + extra_cond) * dm))[0:Y]
    for x in range(X // 4):
        out[x] = phi[x] - flux[x] * scale


def ionic_current(states, membrane, ion_params):
    params_col = ion_params[:, :, None, None, None]
    gate_vals = states.astype(jnp.float32)
    voltage = membrane[None]
    steady = jax.nn.sigmoid((voltage - params_col[0]) / params_col[1])
    gate_vals = steady + (gate_vals - steady) * jnp.exp(-time_step * params_col[2])
    return jnp.sum(params_col[3] * gate_vals * (voltage - params_col[4]), axis=0)


def per_device(
    states, membrane, phi_heart, ion_params, torso_phi, tissue_scale, labels, cond_table,
    send_node, send_count, recv_voxel, recv_count,
):
    X, Y, _ = membrane.shape
    TX, TY, _ = torso_phi.shape
    peers = lax.axis_size("gx") * lax.axis_size("gy")
    cap = send_node.shape[-1]
    place = jnp.stack([
        lax.axis_index("gy"), lax.axis_index("grp"),
        jnp.int32(Y * lax.axis_size("gy")), jnp.int32(LANES * lax.axis_size("grp")), jnp.int32(Y),
    ])
    slots = jnp.arange(cap, dtype=jnp.int32)[None, :]
    send_index = jnp.where(slots < send_count.reshape(peers, 1), send_node.reshape(peers, cap), -1)
    recv_index = jnp.where(slots < recv_count.reshape(peers, 1), recv_voxel.reshape(peers, cap), -1)

    S = TX // 4
    wide = f32(2 * W, X * Y + TX * TY)
    zlo, zhi = call(start_body, (wide, wide), 6, smem=(0,), whole=True)(
        cond_table, membrane, phi_heart, torso_phi, tissue_scale, labels
    )
    weight = call(
        weight_body, f32(S, TY, LANES), 1, scratch=[pltpu.VMEM((S * TY, LANES), jnp.float32)]
    )(recv_index)
    current = ionic_current(states, membrane, ion_params)

    hbox, tbox, tall = f32(X, Y, LANES), f32(TX, TY, LANES), f32(X + TX + 2, 2 * W, LANES)
    *halos, cond, ylo, yhi = call(
        static_y_body, (hbox, hbox, tbox, tbox, tbox, tall, tall), 9, smem=(0, 1),
    )(
        place, cond_table, membrane, phi_heart, torso_phi, tissue_scale, labels,
        *both_ways(zlo, zhi, "grp"),
    )
    heart, torso = (membrane, phi_heart), (torso_phi, cond)
    ryl, ryr = both_ways(ylo, yhi, "gy")
    heart_wide, high = call(
        heart_x_body, (wide_of(X, Y), face_of(Y)), 7, smem=(0,)
    )(place, *heart, *halos[:2], ryl, ryr)
    hxl = from_last(high, "gx")
    torso_wide, high, low = call(
        torso_x_body, (wide_of(TX, TY), face_of(TY), face_of(Y + 2 * W + TY)), 8,
        smem=(0,),
    )(place, heart_wide, *torso, *halos[2:], ryl, ryr)
    txl, xr = from_last(high, "gx"), from_next(low, "gx")

    thin = pltpu.VMEM((3 * W, Y + 2 * W, LANES), jnp.float32)
    sent = call(
        heart_surface_body, f32(peers, 1, cap), 4,
        scratch=[pltpu.VMEM((X // 4 * Y, LANES), jnp.float32)] + [thin] * 10, smem=(0,),
    )(place, heart_wide, hxl, send_index)
    arrived = swap(sent)

    ext = pltpu.VMEM((X + 2 * W, Y + 2 * W, LANES), jnp.float32)
    phi_new, new_membrane = call(
        heart_body, (f32(X, Y, LANES), f32(X, Y, LANES)), 5,
        scratch=[ext] * 10, smem=(0,),
    )(place, current, heart_wide, hxl, xr)
    right, rzlo, rzhi = call(
        right_body,
        (f32(S, TY, LANES), f32(2 * W, S * TY), f32(2 * W, S * TY)),
        3, scratch=[pltpu.VMEM((2 * S * TY, LANES), jnp.float32)],
    )(arrived, recv_index, weight)
    text = (TX + 2 * W, TY + 2 * W, LANES)
    big = pltpu.VMEM(text, jnp.float32)
    N = S + SWEEPS_T - 1
    middle_n = TX - S - 2 * (SWEEPS_T - 1)
    last_n = TX - N - middle_n + 2 * W
    faces, last_faces, middle = call(
        faces_body,
        (f32(10, *text), f32(10, last_n, *text[1:]), f32(middle_n, TY, LANES)),
        3, scratch=[big] * 10,
    )(torso_wide, txl, xr)
    tall = f32(S + 1, 2 * W, LANES)
    *halos, ylo, yhi = call(
        right_y_body, (f32(S, TY, LANES),) * 2 + (tall, tall), 5, smem=(0,),
    )(place, right, weight, *both_ways(rzlo, rzhi, "grp"))
    ryl, ryr = both_ways(ylo, yhi, "gy")
    right_wide, low = call(
        right_x_body, (wide_of(S, TY), face_of(TY)), 7, smem=(0,)
    )(place, right, weight, *halos, ryl, ryr)
    rxr = from_next(low, "gx")
    flat = pltpu.VMEM((N + 2 * W, TY + 2 * W, LANES), jnp.float32)
    surface, returned = call(
        torso_surface_body, (f32(N, TY, LANES), f32(peers, 1, cap)), 3,
        scratch=[flat] * 8,
    )(right_wide, recv_index, faces)
    back = swap(returned)
    thin = pltpu.VMEM((last_n, TY + 2 * W, LANES), jnp.float32)
    torso_out = call(
        torso_body, f32(TX, TY, LANES), 4,
        scratch=[thin] * 8,
    )(surface, middle, rxr, last_faces)
    heart_phi = call(
        final_body, f32(X, Y, LANES), 5,
        scratch=[pltpu.VMEM((2 * X // 4 * Y, LANES), jnp.float32)], smem=(0,),
    )(place, sent, back, send_index, phi_new)
    return (new_membrane, heart_phi, torso_out)


def solution(mesh):
    placed = (
        P(None, "gx", "gy", "grp"),
        P("gx", "gy", "grp"),
        P("gx", "gy", "grp"),
        P(),
        P("gx", "gy", "grp"),
        P("gx", "gy", "grp"),
        P("gx", "gy", "grp"),
        P(),
        P("grp", "gx", "gy", None, None),
        P("grp", "gx", "gy", None),
        P("grp", "gx", "gy", None, None),
        P("grp", "gx", "gy", None),
    )
    return jax.shard_map(
        per_device,
        mesh=mesh,
        in_specs=placed,
        out_specs=(P("gx", "gy", "grp"), P("gx", "gy", "grp"), P("gx", "gy", "grp")),
        check_vma=False,
    )
```
